128 devices in a mesh: outer: 4 (over x), inner: 32 (over z, y, core).
Axes of the slice: x: 4, y: 4, z: 4, core: 2. Of those that a mesh axis runs over, the one named last changes fastest.
Arguments:
- events: bfloat16 [16, 1048576], P(None, ('outer', 'inner')), may hold values from -6 to 6
- coeffs: bfloat16 [64, 1048576], P(None, ('outer', 'inner')), may hold values from -6 to 6
- tree_perm: int32 [128, 8192], P(('outer', 'inner')), may hold values from 0 to 8191, each once within a row
- near_list: int32 [2048, 32], P(('outer', 'inner')), may hold values from 0 to 2047, as said below
- near_count: int32 [2048], P(('outer', 'inner')), may hold values from 1 to 32, as said below
- far_list: int32 [2048, 16], P(('outer', 'inner')), may hold values from 0 to 31, as said below
- skel_low: int32 [128, 128], P(('outer', 'inner')), may hold values from 0 to 8191, as said below
- skel_high: int32 [4, 128], P('outer'), may hold values from 0 to 4095, as said below
Outputs:
- product: bfloat16 [64, 1048576], P(None, ('outer', 'inner'))
The draws below stay inside these ranges and needn't reach their ends.
Inputs may be any that keep to these rules, and one draw needn't show every extreme that they name: `near_list`: slot 0 of leaf i is i; the first near_count[i] slots are distinct leaves within 8 leaves of the leaf's own lower node (i // 16) on either side; the other slots repeat i. `near_count`: some leaf has all 32 slots live. `far_list`: distinct within a leaf, never the leaf's own lower node nor the ones next to it. `skel_low`: distinct within a row. `skel_high`: distinct within a row.
All inputs are finite; a program needn't handle non-finite values.
Results may differ from the reference program's by a relative error of at most 0.006.
Values may be sent and summed in bfloat16 or wider, within the bound.
No kernel may reach another device: no remote copies, remote signals or barrier semaphores. Data moves between devices by JAX's collectives and lax.ppermute only.
A program may use at most 64 MiB of HBM per device.

```python
import jax
import jax.numpy as jnp
from jax import lax

FEAT = 16
COLS = 64
LEAF = 512
RANK = 128
NEAR = 32
LEAF_DEV = 16
REACH = 8
GROUPS = 4
GROUP_DEVS = 32
NODES = 128
FAR = 16
EV_DEV = 8192
LEAVES = 2048
EVENTS = 1048576


def near_plan(key):
    leaf = jnp.arange(LEAVES, dtype=jnp.int32)
    node = leaf // LEAF_DEV
    base = jax.random.randint(jax.random.fold_in(key, 101), (LEAVES,), 2, 7)
    heavy = jax.random.randint(jax.random.fold_in(key, 102), (LEAVES,), 0, 16) == 0
    heavy_val = jax.random.randint(jax.random.fold_in(key, 103), (LEAVES,), 3 * NEAR // 4, NEAR + 1)
    count = jnp.where(heavy, heavy_val, base)
    pick_node = jax.random.randint(jax.random.fold_in(key, 104), (), 1, NODES - 1)
    pick_leaf = jax.random.randint(jax.random.fold_in(key, 105), (), 0, LEAF_DEV)
    count = jnp.where(leaf == pick_node * LEAF_DEV + pick_leaf, NEAR, count)
    width = 2 * LEAF_DEV
    offs = jnp.arange(width, dtype=jnp.int32)
    cand = node[:, None] * LEAF_DEV - REACH + offs[None, :]
    valid = (cand >= 0) & (cand < LEAVES)
    scores = jax.random.randint(jax.random.fold_in(key, 106), (LEAVES, width), 0, 2 ** 20) * width + offs[None, :]
    scores = jnp.where(cand == leaf[:, None], 2 ** 30, scores)
    scores = jnp.where(valid, scores, -1 - offs[None, :])
    order = jnp.argsort(-scores, axis=1)[:, :NEAR]
    picked = jnp.take_along_axis(cand, order, axis=1)
    count = jnp.minimum(jnp.minimum(count, jnp.sum(valid, axis=1)), NEAR)
    slots = jnp.arange(NEAR, dtype=jnp.int32)
    lists = jnp.where(slots[None, :] < count[:, None], picked, leaf[:, None])
    return (lists.astype(jnp.int32), count.astype(jnp.int32))


def draw_near_list(key, part):
    return near_plan(key)[0]


def draw_near_count(key, part):
    return near_plan(key)[1]


def draw_far_list(key, part):
    leaf = jnp.arange(LEAVES, dtype=jnp.int32)
    own = leaf // LEAF_DEV % GROUP_DEVS
    cand = jnp.arange(GROUP_DEVS, dtype=jnp.int32)
    allowed = jnp.abs(cand[None, :] - own[:, None]) >= 2
    scores = jax.random.randint(jax.random.fold_in(key, 201), (LEAVES, GROUP_DEVS), 0, 2 ** 20) * GROUP_DEVS + cand[None, :]
    scores = jnp.where(allowed, scores, -1 - cand[None, :])
    order = jnp.argsort(-scores, axis=1)[:, :FAR]
    return order.astype(jnp.int32)


def distinct_rows(key, rows, total, count):
    keys = jax.random.split(key, rows)
    perms = jax.vmap(lambda k: jax.random.permutation(k, total))(keys).astype(jnp.int32)
    top_pos = jnp.argmax(perms[0] == total - 1).astype(jnp.int32)
    low_pos = jnp.argmax(perms[1] == 0).astype(jnp.int32)
    first = jnp.roll(perms[0], -top_pos)
    second = jnp.roll(perms[1], -low_pos)
    perms = perms.at[0].set(first).at[1].set(second)
    return perms[:, :count]


def draw_skel_low(key, part):
    return distinct_rows(jax.random.fold_in(key, 301), NODES, EV_DEV, RANK)


def draw_skel_high(key, part):
    return distinct_rows(jax.random.fold_in(key, 302), GROUPS, GROUP_DEVS * RANK, RANK)


def steps_of(stream_key, dims, pieces, smallest, largest):
    factor_of, own = 1.0, jax.random.fold_in(stream_key, 6)
    for axis_at, blocks in pieces:
        draws = jnp.exp(jax.random.uniform(jax.random.fold_in(own, axis_at), (blocks,), jnp.float32, smallest / len(pieces), largest / len(pieces)))
        factor_of = factor_of * jnp.repeat(draws, dims[axis_at] // blocks).reshape([-1 if axis == axis_at else 1 for axis in range(len(dims))])
    return factor_of


def gaussian(stream_key, shape, scale, bound, cuts=(), held_as=jnp.bfloat16):
    entries = jax.random.normal(stream_key, shape, jnp.float32) * scale
    if len(cuts) > 0:
        entries = steps_of(stream_key, shape, cuts, -0.22, 0.18) * entries
    return jnp.clip(entries, min=-bound, max=bound).astype(held_as)


def setup_inputs(seed: int = 0) -> dict:
    streams_of = jax.random.split(jax.random.key(seed), 9)
    events = gaussian(streams_of[0], (FEAT, EVENTS), 1.0, 6.0, ((1, 128),))
    coeffs = gaussian(streams_of[1], (COLS, EVENTS), 1.0, 6.0, ((1, 128),))
    tree_perm = jax.vmap(lambda own: jax.random.permutation(own, EV_DEV))(jax.random.split(streams_of[2], NODES)).reshape((NODES, EV_DEV)).astype(jnp.int32)
    near_list = draw_near_list(jax.random.fold_in(streams_of[8], 71), 0)
    near_count = draw_near_count(jax.random.fold_in(streams_of[8], 71), 0)
    far_list = draw_far_list(jax.random.fold_in(streams_of[8], 71), 0)
    skel_low = draw_skel_low(jax.random.fold_in(streams_of[8], 71), 0)
    skel_high = draw_skel_high(jax.random.fold_in(streams_of[8], 71), 0)
    return dict(events=events, coeffs=coeffs, tree_perm=tree_perm, near_list=near_list, near_count=near_count, far_list=far_list, skel_low=skel_low, skel_high=skel_high)


def kernel_tile(left, right):
    left = left.astype(jnp.float32)
    right = right.astype(jnp.float32)
    left_sq = jnp.sum(left * left, axis=0)
    right_sq = jnp.sum(right * right, axis=0)
    cross = jnp.dot(left.T, right, precision=lax.Precision.HIGHEST, preferred_element_type=jnp.float32)
    dist = left_sq[:, None] + right_sq[None, :] - 2.0 * cross
    return jnp.exp(dist * (-2.0 / left.shape[0])).astype(jnp.bfloat16)


def near_sum(padded_x, padded_w, x_leaf, row, count, shift):
    leaf_len = x_leaf.shape[1]
    groups = (count + 3) // 4

    def step(turn, total):
        ids = lax.dynamic_slice_in_dim(row, 4 * turn, 4)
        starts = (ids * leaf_len - shift).astype(jnp.int32)
        block_x = jnp.concatenate([lax.dynamic_slice_in_dim(padded_x, starts[j], leaf_len, 1) for j in range(4)], axis=1)
        block_w = jnp.concatenate([lax.dynamic_slice_in_dim(padded_w, starts[j], leaf_len, 1) for j in range(4)], axis=1)
        live = jnp.repeat(4 * turn + jnp.arange(4, dtype=jnp.int32) < count, leaf_len)
        block_w = jnp.where(live[None, :], block_w, jnp.zeros_like(block_w))
        return total + jnp.dot(block_w, kernel_tile(block_x, x_leaf), preferred_element_type=jnp.float32)

    start = jnp.zeros((padded_w.shape[0], leaf_len), jnp.float32)
    return lax.fori_loop(jnp.int32(0), groups.astype(jnp.int32), step, start)


def far_sum(skel_x, skel_w, x_leaf):
    return jnp.dot(skel_w, kernel_tile(skel_x, x_leaf), preferred_element_type=jnp.float32)


def flat_skel(stack):
    return jnp.transpose(stack, (1, 0, 2)).reshape(stack.shape[1], -1)


def reference(events, coeffs, tree_perm, near_list, near_count, far_list, skel_low, skel_high):
    gidx = (jnp.arange(NODES, dtype=jnp.int32)[:, None] * EV_DEV + tree_perm).reshape(-1)
    xt = events[:, gidx]
    wt = coeffs[:, gidx]
    near_scale = 16.0 / (LEAF * NEAR) ** 0.5
    low_scale = 128.0 / (FAR * RANK) ** 0.5
    high_scale = 128.0 / (GROUPS * RANK) ** 0.5

    def lower(node):
        xd = lax.dynamic_slice_in_dim(xt, node * EV_DEV, EV_DEV, 1)
        wd = lax.dynamic_slice_in_dim(wt, node * EV_DEV, EV_DEV, 1)
        xs = xd[:, skel_low[node]]
        term = jnp.dot(wd, kernel_tile(xd, xs), preferred_element_type=jnp.float32) / EV_DEV ** 0.5
        return xs, term.astype(jnp.bfloat16)

    low_x, low_u = lax.map(lower, jnp.arange(NODES, dtype=jnp.int32))
    pools = low_x.reshape(GROUPS, GROUP_DEVS, FEAT, RANK)
    high_x = jnp.stack([flat_skel(pools[o])[:, skel_high[o]] for o in range(GROUPS)])

    def upper(node):
        xd = lax.dynamic_slice_in_dim(xt, node * EV_DEV, EV_DEV, 1)
        wd = lax.dynamic_slice_in_dim(wt, node * EV_DEV, EV_DEV, 1)
        xso = high_x[node // GROUP_DEVS]
        return jnp.dot(wd, kernel_tile(xd, xso), preferred_element_type=jnp.float32) / (EV_DEV * GROUP_DEVS) ** 0.5

    terms = lax.map(upper, jnp.arange(NODES, dtype=jnp.int32))
    high_u = jnp.sum(terms.reshape(GROUPS, GROUP_DEVS, COLS, RANK), axis=1).astype(jnp.bfloat16)
    high_xf = flat_skel(high_x)

    def leaf_out(leaf):
        x_leaf = lax.dynamic_slice_in_dim(xt, leaf * LEAF, LEAF, 1)
        near = near_sum(xt, wt, x_leaf, near_list[leaf], near_count[leaf], jnp.int32(0))
        group = leaf // LEAF_DEV // GROUP_DEVS
        ids = group * GROUP_DEVS + far_list[leaf]
        low = far_sum(flat_skel(low_x[ids]), flat_skel(low_u[ids]), x_leaf)
        keep = jnp.arange(GROUPS, dtype=jnp.int32) != group
        masked = jnp.where(keep[:, None, None], high_u, jnp.zeros_like(high_u))
        high = far_sum(high_xf, flat_skel(masked), x_leaf)
        return (near * near_scale + low * low_scale + high * high_scale).astype(jnp.bfloat16)

    blocks = lax.map(leaf_out, jnp.arange(LEAVES, dtype=jnp.int32))
    return jnp.transpose(blocks, (1, 0, 2)).reshape(COLS, EVENTS)
```

```python
import jax
import jax.numpy as jnp
from jax import lax
from jax.experimental import pallas as pl
from jax.experimental.pallas import tpu as pltpu
from jax.sharding import PartitionSpec as P

LEAF = 512
RANK = 128
NEAR = 32
LEAF_DEV = 16
COLS = 64
FEAT = 16
LANES = 128
REACH = 8
UNROLL = 4
NT = (((1,), (1,)), ((), ()))
NN = (((1,), (0,)), ((), ()))
VMEM_LIMIT = 48 << 20

X0 = COLS
N0 = X0 + FEAT
O0 = N0 + 3


def dot(a, b, dims=NN):
    return lax.dot_general(a, b, dims, preferred_element_type=jnp.float32)


def target_map():
    k = lax.broadcasted_iota(jnp.int32, (LANES, LANES), 0)
    m = lax.broadcasted_iota(jnp.int32, (LANES, LANES), 1)
    quarter = (k == m) & (k >= X0) & (k < N0)
    ones = (k == m + 3) & (m >= N0) & (m < O0)
    pieces = (k + 3 == m) & (k >= N0) & (k < O0)
    return jnp.where(quarter, 0.25, jnp.where(ones | pieces, 1.0, 0.0)).astype(jnp.bfloat16)


def targets(rows):
    return dot(rows, target_map()).astype(jnp.bfloat16)


def cost(pairs):
    return pl.CostEstimate(
        flops=pairs * 2 * LEAF * LEAF * 384, bytes_accessed=4 << 20, transcendentals=pairs * LEAF * LEAF
    )


def tree_kernel(perm, skel, events, coeffs, rows_out, w_out, t_out, own_out, table, picked, spick):
    chunks = events.shape[1] // LEAF

    def build(c, _):
        at = pl.ds(pl.multiple_of(c * LEAF, LEAF), LEAF)
        x = events[:, at].astype(jnp.float32)
        w = coeffs[:, at].astype(jnp.float32)
        n = jnp.sum(x * x, axis=0, keepdims=True) * -0.125
        n1 = n.astype(jnp.bfloat16).astype(jnp.float32)
        n2 = (n - n1).astype(jnp.bfloat16).astype(jnp.float32)
        n3 = (n - n1 - n2).astype(jnp.bfloat16).astype(jnp.float32)
        r = lax.broadcasted_iota(jnp.int32, (FEAT, LEAF), 0)
        one = jnp.where(r < 6, 1.0, 0.0)
        ext = jnp.where(r == 0, n1, jnp.where(r == 1, n2, jnp.where(r == 2, n3, one)))
        pad = jnp.zeros((LANES - COLS - 2 * FEAT, LEAF), jnp.float32)
        table[at, :] = jnp.concatenate([w, x, ext, pad], axis=0).T
        return 0

    lax.fori_loop(0, chunks, build, 0)

    for j in range(RANK):
        spick[pl.ds(j, 1), :] = table[pl.ds(perm[0, skel[0, j]], 1), :]

    def gather(c, _):
        base = c * LEAF

        def some(b, _):
            for u in range(16):
                e = b * 16 + u
                picked[pl.ds(e, 1), :] = table[pl.ds(perm[0, base + e], 1), :]
            return 0

        lax.fori_loop(0, LEAF // 16, some, 0)
        at = pl.ds(pl.multiple_of(base, LEAF), LEAF)
        r = picked[...]
        rb = r.astype(jnp.bfloat16)
        rows_out[at, :] = rb
        w_out[:, at] = r.T[:COLS].astype(jnp.bfloat16)
        t_out[at, :] = targets(rb)
        return 0

    lax.fori_loop(0, chunks, gather, 0)

    s = spick[...]
    ts = targets(s.astype(jnp.bfloat16))
    k = jnp.exp(dot(rows_out[...], ts, NT)).astype(jnp.bfloat16)
    su = dot(w_out[...], k) / events.shape[1] ** 0.5
    flipped = jnp.concatenate([su, jnp.zeros_like(su)], axis=0).T
    lane = lax.broadcasted_iota(jnp.int32, (RANK, LANES), 1)
    own_out[...] = jnp.where(lane < COLS, flipped, s).astype(jnp.bfloat16)


def tree_call(perm, skel, events, coeffs):
    n = events.shape[1]
    smem = pl.BlockSpec(memory_space=pltpu.SMEM)
    vmem = pl.BlockSpec(memory_space=pltpu.VMEM)
    return pl.pallas_call(
        tree_kernel,
        out_shape=(
            jax.ShapeDtypeStruct((n, LANES), jnp.bfloat16),
            jax.ShapeDtypeStruct((COLS, n), jnp.bfloat16),
            jax.ShapeDtypeStruct((n, LANES), jnp.bfloat16),
            jax.ShapeDtypeStruct((RANK, LANES), jnp.bfloat16),
        ),
        in_specs=[smem, smem, vmem, vmem],
        out_specs=(vmem, vmem, vmem, vmem),
        scratch_shapes=[
            pltpu.VMEM((n, LANES), jnp.float32),
            pltpu.VMEM((LEAF, LANES), jnp.float32),
            pltpu.VMEM((RANK, LANES), jnp.float32),
        ],
        compiler_params=pltpu.CompilerParams(vmem_limit_bytes=VMEM_LIMIT),
        name="tree_rows",
    )(perm, skel, events, coeffs)


def term_kernel(picks, low, rows, w, term_out, hx_out):
    total = low.shape[0]
    hit = lax.broadcasted_iota(jnp.int32, (RANK, total), 1) == picks[...]
    hx = dot(jnp.where(hit, 1.0, 0.0).astype(jnp.bfloat16), low[...]).astype(jnp.bfloat16)
    hx_out[...] = hx
    k = jnp.exp(dot(rows[...], targets(hx), NT)).astype(jnp.bfloat16)
    term_out[...] = dot(w[...], k)


def term_call(picks, low, rows, w):
    vmem = pl.BlockSpec(memory_space=pltpu.VMEM)
    return pl.pallas_call(
        term_kernel,
        out_shape=(
            jax.ShapeDtypeStruct((COLS, RANK), jnp.float32),
            jax.ShapeDtypeStruct((RANK, LANES), jnp.bfloat16),
        ),
        in_specs=[vmem] * 4,
        out_specs=(vmem, vmem),
        compiler_params=pltpu.CompilerParams(vmem_limit_bytes=VMEM_LIMIT),
        cost_estimate=cost(4),
        name="high_term",
    )(picks, low, rows, w)


def near_loop(lo, hi, near, count, src, t, acc, pairs, rows_of, w_of):
    def leaf_slots(leaf, n):
        def slot(s, n):
            at = near[leaf, s] - src
            pairs[n] = leaf * 64 + (at - lo)
            return n + jnp.where((at >= lo) & (at < hi), 1, 0)

        return lax.fori_loop(0, count[leaf], slot, n)

    n = lax.fori_loop(0, LEAF_DEV, leaf_slots, jnp.int32(0))
    for u in range(UNROLL):
        pairs[n + u] = LEAF_DEV * 64

    def step(s, _):
        parts = []
        for u in range(UNROLL):
            e = pairs[s * UNROLL + u]
            leaf, at = e // 64, e % 64
            tl = t[pl.ds(pl.multiple_of(jnp.minimum(leaf, LEAF_DEV - 1) * LEAF, LEAF), LEAF), :]
            k = jnp.exp(dot(rows_of(at), tl, NT)).astype(jnp.bfloat16)
            parts.append((leaf, dot(w_of(at), k)))
        for leaf, part in parts:
            acc[leaf] = acc[leaf] + part
        return 0

    lax.fori_loop(0, (n + UNROLL - 1) // UNROLL, step, 0)


def own_kernel(near, count, first, rows, w, t, acc, pairs):
    acc[...] = jnp.zeros_like(acc)
    near_loop(
        0, LEAF_DEV, near, count, first[0], t, acc, pairs,
        lambda at: rows[pl.ds(pl.multiple_of(at * LEAF, LEAF), LEAF), :],
        lambda at: w[:, pl.ds(pl.multiple_of(at * LEAF, LEAF), LEAF)],
    )


def own_call(near, count, first, rows, w, t):
    smem = pl.BlockSpec(memory_space=pltpu.SMEM)
    vmem = pl.BlockSpec(memory_space=pltpu.VMEM)
    return pl.pallas_call(
        own_kernel,
        out_shape=jax.ShapeDtypeStruct((LEAF_DEV + 1, COLS, LEAF), jnp.float32),
        in_specs=[smem, smem, smem, vmem, vmem, vmem],
        out_specs=vmem,
        scratch_shapes=[pltpu.SMEM((LEAF_DEV * NEAR + 8,), jnp.int32)],
        compiler_params=pltpu.CompilerParams(vmem_limit_bytes=VMEM_LIMIT),
        cost_estimate=cost(60),
        name="near_own",
    )(near, count, first, rows, w, t)


def flip_weights(rows, w, blocks, size):
    def one(b, _):
        at = pl.ds(pl.multiple_of(b * size, size), size)
        w[:, at] = rows[at, :].T[:COLS]
        return 0

    lax.fori_loop(0, blocks, one, 0)


def side_kernel(near, count, first, left, right, t, acc_in, acc, rows, w, pairs):
    half = REACH * LEAF
    rows[:half, :] = left[...]
    rows[half:, :] = right[...]
    flip_weights(rows, w, 2 * REACH, LEAF)
    acc[...] = acc_in[...]
    rows_of = lambda at: rows[pl.ds(pl.multiple_of(at * LEAF, LEAF), LEAF), :]
    w_of = lambda at: w[:, pl.ds(pl.multiple_of(at * LEAF, LEAF), LEAF)]

    def leaf_slots(leaf, n):
        def slot(s, n):
            at = near[leaf, s] - first[0]
            inside = (at >= 0) & (at < LEAF_DEV)
            pairs[n] = leaf * 64 + jnp.where(at < 0, at + REACH, at - REACH)
            return n + jnp.where(inside, 0, 1)

        return lax.fori_loop(0, count[leaf], slot, n)

    n = lax.fori_loop(0, LEAF_DEV, leaf_slots, jnp.int32(0))
    for u in range(UNROLL):
        pairs[n + u] = LEAF_DEV * 64

    def step(s, _):
        parts = []
        for u in range(UNROLL):
            e = pairs[s * UNROLL + u]
            leaf, at = e // 64, e % 64
            tl = t[pl.ds(pl.multiple_of(jnp.minimum(leaf, LEAF_DEV - 1) * LEAF, LEAF), LEAF), :]
            k = jnp.exp(dot(rows_of(at), tl, NT)).astype(jnp.bfloat16)
            parts.append((leaf, dot(w_of(at), k)))
        for leaf, part in parts:
            acc[leaf] = acc[leaf] + part
        return 0

    lax.fori_loop(0, (n + UNROLL - 1) // UNROLL, step, 0)


def side_call(near, count, first, left, right, t, acc):
    smem = pl.BlockSpec(memory_space=pltpu.SMEM)
    vmem = pl.BlockSpec(memory_space=pltpu.VMEM)
    n = 2 * REACH * LEAF
    return pl.pallas_call(
        side_kernel,
        out_shape=jax.ShapeDtypeStruct(acc.shape, jnp.float32),
        in_specs=[smem, smem, smem, vmem, vmem, vmem, vmem],
        out_specs=vmem,
        scratch_shapes=[
            pltpu.VMEM((n, LANES), jnp.bfloat16),
            pltpu.VMEM((COLS, n), jnp.bfloat16),
            pltpu.SMEM((LEAF_DEV * NEAR + 8,), jnp.int32),
        ],
        compiler_params=pltpu.CompilerParams(vmem_limit_bytes=VMEM_LIMIT),
        cost_estimate=cost(30),
        name="near_sides",
    )(near, count, first, left, right, t, acc)


def far_kernel(scales, far, me, low, high_x, high_w, t, acc, out, low_w):
    near_scale, low_scale = scales
    nodes = low.shape[0] // RANK
    flip_weights(low, low_w, nodes * RANK // LEAF, LEAF)
    groups = far.shape[1] // 4

    def leaf_out(leaf, _):
        at = pl.ds(pl.multiple_of(leaf * LEAF, LEAF), LEAF)
        tl = t[at, :]
        total = None
        for g in range(groups):
            spots = [
                pl.ds(pl.multiple_of((far[leaf, 4 * g + j] ^ me[0]) * RANK, RANK), RANK)
                for j in range(4)
            ]
            r = jnp.concatenate([low[s, :] for s in spots], axis=0)
            w = jnp.concatenate([low_w[:, s] for s in spots], axis=1)
            k = jnp.exp(dot(r, tl, NT)).astype(jnp.bfloat16)
            part = dot(w, k)
            total = part if total is None else total + part
        k = jnp.exp(dot(high_x[...], tl, NT)).astype(jnp.bfloat16)
        total = total + dot(high_w[...], k)
        out[:, at] = (acc[leaf] * near_scale + total * low_scale).astype(jnp.bfloat16)
        return 0

    lax.fori_loop(0, LEAF_DEV, leaf_out, 0)


def far_call(scales, far, me, low, high_x, high_w, t, acc):
    smem = pl.BlockSpec(memory_space=pltpu.SMEM)
    vmem = pl.BlockSpec(memory_space=pltpu.VMEM)
    return pl.pallas_call(
        lambda *refs: far_kernel(scales, *refs),
        out_shape=jax.ShapeDtypeStruct((COLS, LEAF_DEV * LEAF), jnp.bfloat16),
        in_specs=[smem, smem, vmem, vmem, vmem, vmem, vmem],
        out_specs=vmem,
        scratch_shapes=[pltpu.VMEM((COLS, low.shape[0]), jnp.bfloat16)],
        compiler_params=pltpu.CompilerParams(vmem_limit_bytes=VMEM_LIMIT),
        cost_estimate=cost(80),
        name="far_out",
    )(far, me, low, high_x, high_w, t, acc)


def swap(x, axis, mask):
    count = lax.axis_size(axis)
    return lax.ppermute(x, axis, [(i, i ^ mask) for i in range(count)])


def per_device(events, coeffs, tree_perm, near_list, near_count, far_list, skel_low, skel_high):
    group_devs = lax.axis_size("inner")
    group_count = lax.axis_size("outer")
    far_count = far_list.shape[1]
    ev_dev = events.shape[1]
    inner = lax.axis_index("inner").astype(jnp.int32)
    device = lax.axis_index("outer").astype(jnp.int32) * group_devs + inner
    devices = group_devs * group_count
    first = (device * LEAF_DEV).reshape(1)
    me = inner.reshape(1)

    rows, w, t, own = tree_call(tree_perm, skel_low, events, coeffs)

    half = REACH * LEAF
    both = ("outer", "inner")
    left = lax.ppermute(rows[ev_dev - half :], both, [(i, i + 1) for i in range(devices - 1)])
    right = lax.ppermute(rows[:half], both, [(i + 1, i) for i in range(devices - 1)])

    low = own
    for masks in ((1,), (2, 4, 6), (8, 16, 24)):
        low = jnp.concatenate([low] + [swap(low, "inner", m) for m in masks], axis=0)

    pick = skel_high.reshape(RANK, 1)
    pick = ((pick // RANK) ^ inner) * RANK + pick % RANK
    term, hx = term_call(pick, low, rows, w)
    for masks in ((1,), (2, 4, 6), (8, 16, 24)):
        term = sum([swap(term, "inner", m) for m in masks], term)
    hu = (term * (1.0 / (ev_dev * group_devs) ** 0.5)).astype(jnp.bfloat16)
    upper = jnp.concatenate([hu, hx], axis=0)
    others = [swap(upper, "outer", m) for m in range(1, group_count)]
    high_w = jnp.concatenate([o[:COLS] for o in others], axis=1) * jnp.bfloat16(2.0)
    high_x = jnp.concatenate([o[COLS:] for o in others], axis=0)

    acc = own_call(near_list, near_count, first, rows, w, t)
    acc = side_call(near_list, near_count, first, left, right, t, acc)
    near_scale = 16.0 / (LEAF * NEAR) ** 0.5
    low_scale = 128.0 / (far_count * RANK) ** 0.5
    return far_call((near_scale, low_scale), far_list, me, low, high_x, high_w, t, acc)


def solution(mesh):
    return jax.shard_map(
        per_device,
        mesh=mesh,
        in_specs=(
            P(None, ("outer", "inner")),
            P(None, ("outer", "inner")),
            P(("outer", "inner"), None),
            P(("outer", "inner"), None),
            P(("outer", "inner")),
            P(("outer", "inner"), None),
            P(("outer", "inner"), None),
            P("outer", None),
        ),
        out_specs=P(None, ("outer", "inner")),
        check_vma=False,
    )
```

```python
import jax
import jax.numpy as jnp
from jax import lax
from jax.experimental import pallas as pl
from jax.experimental.pallas import tpu as pltpu
from jax.sharding import PartitionSpec as P

LEAF = 512
RANK = 128
NEAR = 32
LEAF_DEV = 16
COLS = 64
FEAT = 16
LANES = 128
REACH = 8
NT = (((1,), (1,)), ((), ()))
NN = (((1,), (0,)), ((), ()))
VMEM_LIMIT = 32 << 20

X0 = COLS
N0 = X0 + FEAT
O0 = N0 + 3


def dot(a, b, dims=NN):
    return lax.dot_general(a, b, dims, preferred_element_type=jnp.float32)


def target_map():
    k = lax.broadcasted_iota(jnp.int32, (LANES, LANES), 0)
    m = lax.broadcasted_iota(jnp.int32, (LANES, LANES), 1)
    quarter = (k == m) & (k >= X0) & (k < N0)
    ones = (k == m + 3) & (m >= N0) & (m < O0)
    pieces = (k + 3 == m) & (k >= N0) & (k < O0)
    return jnp.where(quarter, 0.25, jnp.where(ones | pieces, 1.0, 0.0)).astype(jnp.bfloat16)


def targets(rows):
    return dot(rows, target_map()).astype(jnp.bfloat16)


def weight_map():
    k = lax.broadcasted_iota(jnp.int32, (COLS, LANES), 0)
    m = lax.broadcasted_iota(jnp.int32, (COLS, LANES), 1)
    return jnp.where(k == m, 1.0, 0.0).astype(jnp.bfloat16)


def weights(rows):
    return dot(weight_map(), rows, NT).astype(jnp.bfloat16)


def block(i, size):
    return pl.ds(pl.multiple_of(i * size, size), size)


def cost(pairs):
    return pl.CostEstimate(
        flops=pairs * 2 * LEAF * LEAF * 384, bytes_accessed=4 << 20, transcendentals=pairs * LEAF * LEAF
    )


def tree_kernel(
    perm_hbm, skel_hbm, events_hbm, coeffs_hbm, rows_out, w_out, t_out, own_out,
    table, picked, spick, perm, skel, events, coeffs, sems,
):
    moves = [
        pltpu.make_async_copy(src, dst, sems.at[i])
        for i, (src, dst) in enumerate(
            [(events_hbm, events), (coeffs_hbm, coeffs), (perm_hbm, perm), (skel_hbm, skel)]
        )
    ]
    for m in moves:
        m.start()
    for m in moves:
        m.wait()
    chunks = events.shape[1] // LEAF

    def build(c, _):
        at = block(c, LEAF)
        xb = events[:, at]
        x = xb.astype(jnp.float32)
        n = jnp.sum(x * x, axis=0, keepdims=True) * -0.125
        n1 = n.astype(jnp.bfloat16).astype(jnp.float32)
        n2 = (n - n1).astype(jnp.bfloat16).astype(jnp.float32)
        n3 = (n - n1 - n2).astype(jnp.bfloat16).astype(jnp.float32)
        r = lax.broadcasted_iota(jnp.int32, (FEAT, LEAF), 0)
        one = jnp.where(r < 6, 1.0, 0.0)
        ext = jnp.where(r == 0, n1, jnp.where(r == 1, n2, jnp.where(r == 2, n3, one)))
        pad = jnp.zeros((LANES - COLS - 2 * FEAT, LEAF), jnp.bfloat16)
        full = jnp.concatenate([coeffs[:, at], xb, ext.astype(jnp.bfloat16), pad], axis=0)
        table[at, :] = full.T.astype(jnp.float32)
        return 0

    lax.fori_loop(0, chunks, build, 0)

    def fetch(ids):
        return jnp.concatenate([table[pl.ds(i, 1), :] for i in ids], axis=0)

    for j in range(0, RANK, 8):
        spick[j : j + 8, :] = fetch([perm[0, skel[0, j + u]] for u in range(8)])

    step = 64

    def gather(c, _):
        def some(b, _):
            for v in range(0, step, 8):
                e = c * LEAF + b * step + v
                picked[block(b * (step // 8) + v // 8, 8), :] = fetch(
                    [perm[0, e + u] for u in range(8)]
                )
            return 0

        lax.fori_loop(0, LEAF // step, some, 0)
        at = block(c, LEAF)
        r = picked[...]
        rb = r.astype(jnp.bfloat16)
        rows_out[at, :] = rb
        w_out[:, at] = r.T[:COLS].astype(jnp.bfloat16)
        t_out[at, :] = targets(rb)
        return 0

    lax.fori_loop(0, chunks, gather, 0)

    s = spick[...]
    ts = targets(s.astype(jnp.bfloat16))
    k = jnp.exp(dot(rows_out[...], ts, NT)).astype(jnp.bfloat16)
    su = dot(w_out[...], k) / events.shape[1] ** 0.5
    flipped = jnp.concatenate([su, jnp.zeros_like(su)], axis=0).T
    lane = lax.broadcasted_iota(jnp.int32, (RANK, LANES), 1)
    own_out[...] = jnp.where(lane < COLS, flipped, s).astype(jnp.bfloat16)


SMEM = pl.BlockSpec(memory_space=pltpu.SMEM)
VMEM = pl.BlockSpec(memory_space=pltpu.VMEM)
ANY = pl.BlockSpec(memory_space=pl.ANY)
HBM = pl.BlockSpec(memory_space=pltpu.HBM)


def params(limit=VMEM_LIMIT):
    return pltpu.CompilerParams(vmem_limit_bytes=limit)


def tree_call(perm, skel, events, coeffs):
    n = events.shape[1]
    return pl.pallas_call(
        tree_kernel,
        out_shape=(
            jax.ShapeDtypeStruct((n, LANES), jnp.bfloat16),
            jax.ShapeDtypeStruct((COLS, n), jnp.bfloat16),
            jax.ShapeDtypeStruct((n, LANES), jnp.bfloat16),
            jax.ShapeDtypeStruct((RANK, LANES), jnp.bfloat16),
        ),
        in_specs=[HBM] * 4,
        out_specs=(VMEM,) * 4,
        scratch_shapes=[
            pltpu.VMEM((n, LANES), jnp.float32),
            pltpu.VMEM((LEAF, LANES), jnp.float32),
            pltpu.VMEM((RANK, LANES), jnp.float32),
            pltpu.SMEM(perm.shape, jnp.int32),
            pltpu.SMEM(skel.shape, jnp.int32),
            pltpu.VMEM(events.shape, jnp.bfloat16),
            pltpu.VMEM(coeffs.shape, jnp.bfloat16),
            pltpu.SemaphoreType.DMA((4,)),
        ],
        compiler_params=params(),
        name="tree_rows",
    )(perm, skel, events, coeffs)


def self_kernel(leaves, rows, w, t, part):
    for leaf in range(leaves):
        at = slice(leaf * LEAF, (leaf + 1) * LEAF)
        k = jnp.exp(dot(rows[at, :], t[at, :], NT)).astype(jnp.bfloat16)
        part[leaf] = dot(w[:, at], k)


def self_call(rows, w, t, first, leaves):
    spot = first // leaves
    size = leaves * LEAF
    return pl.pallas_call(
        lambda *refs: self_kernel(leaves, *refs),
        out_shape=jax.ShapeDtypeStruct((leaves, COLS, LEAF), jnp.float32),
        grid=(1,),
        in_specs=[
            pl.BlockSpec((size, LANES), lambda i: (spot, 0)),
            pl.BlockSpec((COLS, size), lambda i: (0, spot)),
            pl.BlockSpec((size, LANES), lambda i: (spot, 0)),
        ],
        out_specs=pl.BlockSpec((leaves, COLS, LEAF), lambda i: (0, 0, 0)),
        compiler_params=params(),
        cost_estimate=cost(leaves),
        name="near_self",
    )(rows, w, t)


def term_kernel(parts, picks, *refs):
    pieces, (rows, w, term_out, hx_out, low_out, low_w) = refs[:parts], refs[parts:]
    size = pieces[0].shape[0]
    total = parts * size
    for i, piece in enumerate(pieces):
        low_out[i * size : (i + 1) * size, :] = piece[...]
    hit = lax.broadcasted_iota(jnp.int32, (RANK, total), 1) == picks[...]
    hx = dot(jnp.where(hit, 1.0, 0.0).astype(jnp.bfloat16), low_out[...]).astype(jnp.bfloat16)
    hx_out[...] = hx
    k = jnp.exp(dot(rows[...], targets(hx), NT)).astype(jnp.bfloat16)
    term_out[...] = dot(w[...], k)
    low_w[...] = weights(low_out[...])


def term_call(picks, pieces, rows, w):
    total = len(pieces) * pieces[0].shape[0]
    return pl.pallas_call(
        lambda *refs: term_kernel(len(pieces), *refs),
        out_shape=(
            jax.ShapeDtypeStruct((COLS, RANK), jnp.float32),
            jax.ShapeDtypeStruct((RANK, LANES), jnp.bfloat16),
            jax.ShapeDtypeStruct((total, LANES), jnp.bfloat16),
            jax.ShapeDtypeStruct((COLS, total), jnp.bfloat16),
        ),
        in_specs=[VMEM] * (3 + len(pieces)),
        out_specs=(VMEM,) * 4,
        compiler_params=params(),
        cost_estimate=cost(4),
        name="high_term",
    )(picks, *pieces, rows, w)


def low_kernel(first, leaves, far, me, low, low_w, t, part):
    groups = far.shape[1] // 4
    both = 2

    def some(b, _):
        ks = []
        for j in range(both):
            leaf = b * both + j
            tl = t[block(leaf, LEAF), :]
            for g in range(groups):
                spots = [block(far[first + leaf, 4 * g + i] ^ me[0], RANK) for i in range(4)]
                r = jnp.concatenate([low[s, :] for s in spots], axis=0)
                ks.append((spots, jnp.exp(dot(r, tl, NT)).astype(jnp.bfloat16)))
        for j in range(both):
            total = None
            for spots, k in ks[j * groups : (j + 1) * groups]:
                p = dot(jnp.concatenate([low_w[:, s] for s in spots], axis=1), k)
                total = p if total is None else total + p
            part[b * both + j] = total
        return 0

    lax.fori_loop(0, leaves // both, some, 0)


def low_call(far, me, low, low_w, t, first, leaves):
    spot = first // leaves
    return pl.pallas_call(
        lambda *refs: low_kernel(first, leaves, *refs),
        out_shape=jax.ShapeDtypeStruct((leaves, COLS, LEAF), jnp.float32),
        grid=(1,),
        in_specs=[
            SMEM,
            SMEM,
            VMEM,
            VMEM,
            pl.BlockSpec((leaves * LEAF, LANES), lambda i: (spot, 0)),
        ],
        out_specs=pl.BlockSpec((leaves, COLS, LEAF), lambda i: (0, 0, 0)),
        compiler_params=params(),
        cost_estimate=cost(4 * leaves),
        name="far_low",
    )(far, me, low, low_w, t)


def last_kernel(counts, scales, near, count, first, *refs):
    n_self, n_low, n_up = counts
    near_scale, low_scale = scales
    rows_own, left, right, w_own, t = refs[:5]
    refs = refs[5:]
    selfs, refs = refs[:n_self], refs[n_self:]
    lows, refs = refs[:n_low], refs[n_low:]
    ups, refs = refs[:n_up], refs[n_up:]
    out, rows, w, acc, pairs, sems = refs
    side = REACH * LEAF
    own = LEAF_DEV * LEAF
    moves = [
        pltpu.make_async_copy(left, rows.at[pl.ds(0, side), :], sems.at[0]),
        pltpu.make_async_copy(right, rows.at[pl.ds(side + own, side), :], sems.at[1]),
        pltpu.make_async_copy(rows_own, rows.at[pl.ds(side, own), :], sems.at[2]),
        pltpu.make_async_copy(w_own, w.at[:, pl.ds(side, own)], sems.at[3]),
    ]
    for m in moves:
        m.start()

    def leaf_slots(leaf, n):
        def slot(s, n):
            pairs[n] = leaf * 64 + (near[leaf, s] - first[0] + REACH)
            return n + 1

        return lax.fori_loop(1, count[leaf], slot, n)

    n = lax.fori_loop(0, LEAF_DEV, leaf_slots, jnp.int32(0))
    for u in range(8):
        pairs[n + u] = LEAF_DEV * 64

    leaf = 0
    for part in selfs:
        acc[leaf : leaf + part.shape[0]] = part[...]
        leaf += part.shape[0]
    acc[LEAF_DEV] = jnp.zeros((COLS, LEAF), jnp.float32)
    moves[0].wait()
    moves[1].wait()

    def flip(b, _):
        at = block(b, LEAF)
        there = block(b + REACH + LEAF_DEV, LEAF)
        w[:, at] = weights(rows[at, :])
        w[:, there] = weights(rows[there, :])
        return 0

    lax.fori_loop(0, REACH, flip, 0)
    moves[2].wait()
    moves[3].wait()

    def step(begin, many):
        ks = []
        for u in range(many):
            e = pairs[begin + u]
            leaf, at = e // 64, e % 64
            tl = t[block(jnp.minimum(leaf, LEAF_DEV - 1), LEAF), :]
            k = jnp.exp(dot(rows[block(at, LEAF), :], tl, NT)).astype(jnp.bfloat16)
            ks.append((leaf, at, k))
        for leaf, at, k in ks:
            acc[leaf] = acc[leaf] + dot(w[:, block(at, LEAF)], k)

    def eight(s, _):
        step(s * 8, 8)
        return 0

    lax.fori_loop(0, n // 8, eight, 0)

    def four(s, _):
        step(n // 8 * 8 + s * 4, 4)
        return 0

    lax.fori_loop(0, (n % 8 + 3) // 4, four, 0)

    high_w = jnp.concatenate([u[:COLS, :] for u in ups], axis=1)
    high_x = jnp.concatenate([u[COLS:, :] for u in ups], axis=0)
    leaf = 0
    for part in lows:
        size = part.shape[0]
        ks = []
        for j in range(size):
            at = slice((leaf + j) * LEAF, (leaf + j + 1) * LEAF)
            ks.append(jnp.exp(dot(high_x, t[at, :], NT)).astype(jnp.bfloat16))
        for j in range(size):
            at = slice((leaf + j) * LEAF, (leaf + j + 1) * LEAF)
            far = part[j] + dot(high_w, ks[j])
            out[:, at] = (acc[leaf + j] * near_scale + far * low_scale).astype(jnp.bfloat16)
        leaf += size


def last_call(scales, near, count, first, rows, left, right, w, t, selfs, lows, ups):
    n = (LEAF_DEV + 2 * REACH) * LEAF
    return pl.pallas_call(
        lambda *refs: last_kernel((len(selfs), len(lows), len(ups)), scales, *refs),
        out_shape=jax.ShapeDtypeStruct((COLS, LEAF_DEV * LEAF), jnp.bfloat16),
        in_specs=[SMEM] * 3 + [ANY] * 4 + [VMEM] * (1 + len(selfs) + len(lows) + len(ups)),
        out_specs=VMEM,
        scratch_shapes=[
            pltpu.VMEM((n, LANES), jnp.bfloat16),
            pltpu.VMEM((COLS, n), jnp.bfloat16),
            pltpu.VMEM((LEAF_DEV + 1, COLS, LEAF), jnp.float32),
            pltpu.SMEM((LEAF_DEV * NEAR + 8,), jnp.int32),
            pltpu.SemaphoreType.DMA((4,)),
        ],
        compiler_params=params(40 << 20),
        cost_estimate=cost(150),
        name="near_out",
    )(near, count, first, rows, left, right, w, t, *selfs, *lows, *ups)


def swap(x, axis, mask):
    count = lax.axis_size(axis)
    return lax.ppermute(x, axis, [(i, i ^ mask) for i in range(count)])


def after(x, *others):
    return lax.optimization_barrier((x, *others))[0]


def per_device(events, coeffs, tree_perm, near_list, near_count, far_list, skel_low, skel_high):
    group_devs = lax.axis_size("inner")
    group_count = lax.axis_size("outer")
    far_count = far_list.shape[1]
    ev_dev = events.shape[1]
    inner = lax.axis_index("inner").astype(jnp.int32)
    device = lax.axis_index("outer").astype(jnp.int32) * group_devs + inner
    devices = group_devs * group_count
    first = (device * LEAF_DEV).reshape(1)
    me = inner.reshape(1)
    pick = skel_high.reshape(RANK, 1)
    pick = ((pick // RANK) ^ inner) * RANK + pick % RANK

    rows, w, t, own = tree_call(tree_perm, skel_low, events, coeffs)

    half = REACH * LEAF
    both = ("outer", "inner")
    left = lax.ppermute(rows[ev_dev - half :], both, [(i, i + 1) for i in range(devices - 1)])
    right = lax.ppermute(rows[:half], both, [(i + 1, i) for i in range(devices - 1)])

    rounds = ((1,), (2, 4, 6), (8, 16, 24))
    spans = ((0, 4), (4, 4), (8, 8))
    low = own
    selfs = []
    pieces = None
    for masks, span in zip(rounds, spans):
        if pieces is not None:
            low = after(jnp.concatenate(pieces, axis=0), selfs[-1])
        pieces = [low] + [swap(low, "inner", m) for m in masks]
        selfs.append(self_call(after(rows, low), w, t, *span))
    pieces = [after(p, selfs[-1]) for p in pieces]

    term, hx, low, low_w = term_call(pick, pieces, rows, w)
    lows = []
    for i, masks in enumerate(rounds):
        terms = [swap(term, "inner", m) for m in masks]
        lows.append(low_call(far_list, me, after(low, term), low_w, t, 4 * i, 4))
        term = after(sum(terms, term), lows[-1])
    hu = (term * (1.0 / (ev_dev * group_devs) ** 0.5)).astype(jnp.bfloat16)
    ratio = (far_count / group_count) ** 0.5
    upper = jnp.concatenate([hu * jnp.bfloat16(ratio), hx], axis=0)
    ups = [swap(upper, "outer", m) for m in range(1, group_count)]
    lows.append(low_call(far_list, me, after(low, upper), low_w, t, 12, 4))
    ups = [after(u, lows[-1]) for u in ups]

    near_scale = 16.0 / (LEAF * NEAR) ** 0.5
    low_scale = 128.0 / (far_count * RANK) ** 0.5
    return last_call(
        (near_scale, low_scale), near_list, near_count, first, rows, left, right, w, t, selfs, lows, ups
    )


def solution(mesh):
    return jax.shard_map(
        per_device,
        mesh=mesh,
        in_specs=(
            P(None, ("outer", "inner")),
            P(None, ("outer", "inner")),
            P(("outer", "inner"), None),
            P(("outer", "inner"), None),
            P(("outer", "inner")),
            P(("outer", "inner"), None),
            P(("outer", "inner"), None),
            P("outer", None),
        ),
        out_specs=P(None, ("outer", "inner")),
        check_vma=False,
    )
```

```python
import functools

import jax
import jax.numpy as jnp
from jax import lax
from jax.experimental import pallas as pl
from jax.experimental.pallas import tpu as pltpu
from jax.sharding import PartitionSpec as P

LEAF = 512
RANK = 128
NEAR = 32
LEAF_DEV = 16
COLS = 64
FEAT = 16
LANES = 128
REACH = 8
LOW_ROUNDS = ((1,), (2,), (4,), (8, 16, 24))
SELF_SPANS = ((0, 2), (2, 2), (4, 4), (8, 8))
SUM_ROUNDS = (1, 2, 4, 8, 16)
NT = (((1,), (1,)), ((), ()))
NN = (((1,), (0,)), ((), ()))
VMEM_LIMIT = 24 << 20
LAST_LIMIT = 32 << 20

X0 = COLS
N0 = X0 + FEAT
O0 = N0 + 3


def dot(a, b, dims=NN):
    return lax.dot_general(a, b, dims, preferred_element_type=jnp.float32)


def target_map():
    k = lax.broadcasted_iota(jnp.int32, (LANES, LANES), 0)
    m = lax.broadcasted_iota(jnp.int32, (LANES, LANES), 1)
    quarter = (k == m) & (k >= X0) & (k < N0)
    ones = (k == m + 3) & (m >= N0) & (m < O0)
    pieces = (k + 3 == m) & (k >= N0) & (k < O0)
    return jnp.where(quarter, 0.25, jnp.where(ones | pieces, 1.0, 0.0)).astype(jnp.bfloat16)


def targets(rows):
    return dot(rows, target_map()).astype(jnp.bfloat16)


def weight_map():
    k = lax.broadcasted_iota(jnp.int32, (COLS, LANES), 0)
    m = lax.broadcasted_iota(jnp.int32, (COLS, LANES), 1)
    return jnp.where(k == m, 1.0, 0.0).astype(jnp.bfloat16)


def weights(rows):
    return dot(weight_map(), rows, NT).astype(jnp.bfloat16)


def block(i, size):
    return pl.ds(pl.multiple_of(i * size, size), size)


def cost(pairs):
    return pl.CostEstimate(
        flops=pairs * 2 * LEAF * LEAF * 384, bytes_accessed=4 << 20, transcendentals=pairs * LEAF * LEAF
    )


def features(xb):
    x = xb.astype(jnp.float32)
    n = jnp.sum(x * x, axis=0, keepdims=True) * -0.125
    n1 = n.astype(jnp.bfloat16).astype(jnp.float32)
    n2 = (n - n1).astype(jnp.bfloat16).astype(jnp.float32)
    n3 = (n - n1 - n2).astype(jnp.bfloat16).astype(jnp.float32)
    r = lax.broadcasted_iota(jnp.int32, xb.shape, 0)
    one = jnp.where(r < 6, 1.0, 0.0)
    ext = jnp.where(r == 0, n1, jnp.where(r == 1, n2, jnp.where(r == 2, n3, one)))
    pad = jnp.zeros((LANES - COLS - 2 * FEAT, xb.shape[1]), jnp.bfloat16)
    return [xb, ext.astype(jnp.bfloat16), pad]


def tree_kernel(
    perm_hbm, skel_hbm, events_hbm, coeffs_hbm, lo_out, hi_out, w_out, t_out, own_out,
    table, picked, spick, perm, skel, events, coeffs, sems,
):
    moves = [
        pltpu.make_async_copy(src, dst, sems.at[i])
        for i, (src, dst) in enumerate(
            [(events_hbm, events), (coeffs_hbm, coeffs), (perm_hbm, perm), (skel_hbm, skel)]
        )
    ]
    for m in moves:
        m.start()
    for m in moves:
        m.wait()
    chunks = events.shape[1] // LEAF

    def build(c, _):
        at = block(c, LEAF)
        full = jnp.concatenate([coeffs[:, at]] + features(events[:, at]), axis=0)
        table[at, :] = full.T.astype(jnp.float32)
        return 0

    lax.fori_loop(0, chunks, build, 0)

    def fetch(ids):
        return jnp.concatenate([table[pl.ds(i, 1), :] for i in ids], axis=0)

    for j in range(0, RANK, 8):
        spick[j : j + 8, :] = fetch([perm[0, skel[0, j + u]] for u in range(8)])

    step = 64

    def gather(rows_out, base, c, _):
        def some(b, _):
            for v in range(0, step, 8):
                e = (base + c) * LEAF + b * step + v
                picked[block(b * (step // 8) + v // 8, 8), :] = fetch(
                    [perm[0, e + u] for u in range(8)]
                )
            return 0

        lax.fori_loop(0, LEAF // step, some, 0)
        at = block(base + c, LEAF)
        r = picked[...]
        rb = r.astype(jnp.bfloat16)
        rows_out[block(c, LEAF), :] = rb
        w_out[:, at] = r.T[:COLS].astype(jnp.bfloat16)
        t_out[at, :] = targets(rb)
        return 0

    half = chunks // 2
    lax.fori_loop(0, half, functools.partial(gather, lo_out, 0), 0)
    lax.fori_loop(0, half, functools.partial(gather, hi_out, half), 0)

    s = spick[...]
    ts = targets(s.astype(jnp.bfloat16))
    su = halves_dot(lo_out, hi_out, w_out, ts) / events.shape[1] ** 0.5
    own_out[:COLS, :] = su.astype(jnp.bfloat16)
    own_out[COLS:, :] = s.T[X0:N0].astype(jnp.bfloat16)


def halves_dot(lo, hi, w, ts):
    half = lo.shape[0]
    ka = jnp.exp(dot(lo[...], ts, NT)).astype(jnp.bfloat16)
    kb = jnp.exp(dot(hi[...], ts, NT)).astype(jnp.bfloat16)
    return dot(w[:, :half], ka) + dot(w[:, half:], kb)


SMEM = pl.BlockSpec(memory_space=pltpu.SMEM)
VMEM = pl.BlockSpec(memory_space=pltpu.VMEM)
ANY = pl.BlockSpec(memory_space=pl.ANY)
HBM = pl.BlockSpec(memory_space=pltpu.HBM)


def params(limit=VMEM_LIMIT):
    return pltpu.CompilerParams(vmem_limit_bytes=limit)


def tree_call(perm, skel, events, coeffs):
    n = events.shape[1]
    return pl.pallas_call(
        tree_kernel,
        out_shape=(
            jax.ShapeDtypeStruct((n // 2, LANES), jnp.bfloat16),
            jax.ShapeDtypeStruct((n // 2, LANES), jnp.bfloat16),
            jax.ShapeDtypeStruct((COLS, n), jnp.bfloat16),
            jax.ShapeDtypeStruct((n, LANES), jnp.bfloat16),
            jax.ShapeDtypeStruct((COLS + FEAT, RANK), jnp.bfloat16),
        ),
        in_specs=[HBM] * 4,
        out_specs=(VMEM,) * 5,
        scratch_shapes=[
            pltpu.VMEM((n, LANES), jnp.float32),
            pltpu.VMEM((LEAF, LANES), jnp.float32),
            pltpu.VMEM((RANK, LANES), jnp.float32),
            pltpu.SMEM(perm.shape, jnp.int32),
            pltpu.SMEM(skel.shape, jnp.int32),
            pltpu.VMEM(events.shape, jnp.bfloat16),
            pltpu.VMEM(coeffs.shape, jnp.bfloat16),
            pltpu.SemaphoreType.DMA((4,)),
        ],
        compiler_params=params(),
        name="tree_rows",
    )(perm, skel, events, coeffs)


def self_kernel(leaves, rows, w, t, part):
    for leaf in range(leaves):
        at = slice(leaf * LEAF, (leaf + 1) * LEAF)
        k = jnp.exp(dot(rows[at, :], t[at, :], NT)).astype(jnp.bfloat16)
        part[leaf] = dot(w[:, at], k)


def self_call(lo, hi, w, t, first, leaves):
    spot = first // leaves
    halves = LEAF_DEV // 2 // leaves
    rows, row_spot = (lo, spot) if spot < halves else (hi, spot - halves)
    size = leaves * LEAF
    return pl.pallas_call(
        lambda *refs: self_kernel(leaves, *refs),
        out_shape=jax.ShapeDtypeStruct((leaves, COLS, LEAF), jnp.float32),
        grid=(1,),
        in_specs=[
            pl.BlockSpec((size, LANES), lambda i: (row_spot, 0)),
            pl.BlockSpec((COLS, size), lambda i: (0, spot)),
            pl.BlockSpec((size, LANES), lambda i: (spot, 0)),
        ],
        out_specs=pl.BlockSpec((leaves, COLS, LEAF), lambda i: (0, 0, 0)),
        compiler_params=params(),
        cost_estimate=cost(leaves),
        name="near_self",
    )(rows, w, t)


def term_kernel(parts, picks, *refs):
    pieces, (lo, hi, w, term_out, hx_out, low_out, low_w) = refs[:parts], refs[parts:]
    each = COLS + FEAT
    blocks = pieces[0].shape[0] // each
    size = blocks * RANK
    for i, piece in enumerate(pieces):
        xs = []
        for b in range(blocks):
            j = i * blocks + b
            low_w[:, j * RANK : (j + 1) * RANK] = piece[b * each : b * each + COLS, :]
            xs.append(piece[b * each + COLS : (b + 1) * each, :])
        none = jnp.zeros((COLS, size), jnp.bfloat16)
        full = jnp.concatenate([none] + features(jnp.concatenate(xs, axis=1)), axis=0)
        low_out[i * size : (i + 1) * size, :] = full.T
    hit = lax.broadcasted_iota(jnp.int32, (RANK, parts * size), 1) == picks[...]
    hx = dot(jnp.where(hit, 1.0, 0.0).astype(jnp.bfloat16), low_out[...]).astype(jnp.bfloat16)
    hx_out[...] = hx
    term_out[...] = halves_dot(lo, hi, w, targets(hx))


def term_call(picks, pieces, lo, hi, w):
    total = len(pieces) * pieces[0].shape[0] // (COLS + FEAT) * RANK
    return pl.pallas_call(
        lambda *refs: term_kernel(len(pieces), *refs),
        out_shape=(
            jax.ShapeDtypeStruct((COLS, RANK), jnp.float32),
            jax.ShapeDtypeStruct((RANK, LANES), jnp.bfloat16),
            jax.ShapeDtypeStruct((total, LANES), jnp.bfloat16),
            jax.ShapeDtypeStruct((COLS, total), jnp.bfloat16),
        ),
        in_specs=[VMEM] * (4 + len(pieces)),
        out_specs=(VMEM,) * 4,
        compiler_params=params(),
        cost_estimate=cost(4),
        name="high_term",
    )(picks, *pieces, lo, hi, w)


def low_kernel(first, leaves, far, me, low, low_w, t, part):
    groups = far.shape[1] // 4
    both = 2

    def some(b, _):
        ks = []
        for j in range(both):
            leaf = b * both + j
            tl = t[block(leaf, LEAF), :]
            for g in range(groups):
                spots = [block(far[first + leaf, 4 * g + i] ^ me[0], RANK) for i in range(4)]
                r = jnp.concatenate([low[s, :] for s in spots], axis=0)
                ks.append((spots, jnp.exp(dot(r, tl, NT)).astype(jnp.bfloat16)))
        for j in range(both):
            total = None
            for spots, k in ks[j * groups : (j + 1) * groups]:
                p = dot(jnp.concatenate([low_w[:, s] for s in spots], axis=1), k)
                total = p if total is None else total + p
            part[b * both + j] = total
        return 0

    lax.fori_loop(0, leaves // both, some, 0)


def low_call(far, me, low, low_w, t, first, leaves):
    spot = first // leaves
    return pl.pallas_call(
        lambda *refs: low_kernel(first, leaves, *refs),
        out_shape=jax.ShapeDtypeStruct((leaves, COLS, LEAF), jnp.float32),
        grid=(1,),
        in_specs=[
            SMEM,
            SMEM,
            VMEM,
            VMEM,
            pl.BlockSpec((leaves * LEAF, LANES), lambda i: (spot, 0)),
        ],
        out_specs=pl.BlockSpec((leaves, COLS, LEAF), lambda i: (0, 0, 0)),
        compiler_params=params(),
        cost_estimate=cost(4 * leaves),
        name="far_low",
    )(far, me, low, low_w, t)


def last_kernel(counts, scales, near, count, first, *refs):
    n_self, n_low, n_up = counts
    near_scale, low_scale = scales
    lo, hi, left, right, w_own, t = refs[:6]
    refs = refs[6:]
    selfs, refs = refs[:n_self], refs[n_self:]
    lows, refs = refs[:n_low], refs[n_low:]
    ups, refs = refs[:n_up], refs[n_up:]
    out, rows, w, acc, pairs, sems = refs
    side = REACH * LEAF
    own = LEAF_DEV * LEAF
    moves = [
        pltpu.make_async_copy(left, rows.at[pl.ds(0, side), :], sems.at[0]),
        pltpu.make_async_copy(right, rows.at[pl.ds(side + own, side), :], sems.at[1]),
        pltpu.make_async_copy(lo, rows.at[pl.ds(side, own // 2), :], sems.at[2]),
        pltpu.make_async_copy(hi, rows.at[pl.ds(side + own // 2, own // 2), :], sems.at[3]),
        pltpu.make_async_copy(w_own, w.at[:, pl.ds(side, own)], sems.at[4]),
    ]
    for m in moves:
        m.start()

    def leaf_slots(leaf, n):
        def slot(s, n):
            pairs[n] = leaf * 64 + (near[leaf, s] - first[0] + REACH)
            return n + 1

        return lax.fori_loop(1, count[leaf], slot, n)

    n = lax.fori_loop(0, LEAF_DEV, leaf_slots, jnp.int32(0))
    for u in range(8):
        pairs[n + u] = LEAF_DEV * 64

    leaf = 0
    for part in selfs:
        acc[leaf : leaf + part.shape[0]] = part[...]
        leaf += part.shape[0]
    acc[LEAF_DEV] = jnp.zeros((COLS, LEAF), jnp.float32)
    moves[0].wait()
    moves[1].wait()

    def flip(b, _):
        at = block(b, LEAF)
        there = block(b + REACH + LEAF_DEV, LEAF)
        w[:, at] = weights(rows[at, :])
        w[:, there] = weights(rows[there, :])
        return 0

    lax.fori_loop(0, REACH, flip, 0)
    for m in moves[2:]:
        m.wait()

    def step(begin, many):
        ks = []
        for u in range(many):
            e = pairs[begin + u]
            leaf, at = e // 64, e % 64
            tl = t[block(jnp.minimum(leaf, LEAF_DEV - 1), LEAF), :]
            k = jnp.exp(dot(rows[block(at, LEAF), :], tl, NT)).astype(jnp.bfloat16)
            ks.append((leaf, at, k))
        for leaf, at, k in ks:
            acc[leaf] = acc[leaf] + dot(w[:, block(at, LEAF)], k)

    def eight(s, _):
        step(s * 8, 8)
        return 0

    lax.fori_loop(0, n // 8, eight, 0)

    def four(s, _):
        step(n // 8 * 8 + s * 4, 4)
        return 0

    lax.fori_loop(0, (n % 8 + 3) // 4, four, 0)

    each = COLS + RANK
    starts = [(u, i) for u in ups for i in range(0, u.shape[0], each)]
    high_w = jnp.concatenate([u[i : i + COLS, :] for u, i in starts], axis=1)
    high_x = jnp.concatenate([u[i + COLS : i + each, :] for u, i in starts], axis=0)
    leaf = 0
    for part in lows:
        size = part.shape[0]
        ks = []
        for j in range(size):
            at = slice((leaf + j) * LEAF, (leaf + j + 1) * LEAF)
            ks.append(jnp.exp(dot(high_x, t[at, :], NT)).astype(jnp.bfloat16))
        for j in range(size):
            at = slice((leaf + j) * LEAF, (leaf + j + 1) * LEAF)
            far = part[j] + dot(high_w, ks[j])
            out[:, at] = (acc[leaf + j] * near_scale + far * low_scale).astype(jnp.bfloat16)
        leaf += size


def last_call(scales, near, count, first, lo, hi, left, right, w, t, selfs, lows, ups):
    n = (LEAF_DEV + 2 * REACH) * LEAF
    return pl.pallas_call(
        lambda *refs: last_kernel((len(selfs), len(lows), len(ups)), scales, *refs),
        out_shape=jax.ShapeDtypeStruct((COLS, LEAF_DEV * LEAF), jnp.bfloat16),
        in_specs=[SMEM] * 3 + [ANY] * 5 + [VMEM] * (1 + len(selfs) + len(lows) + len(ups)),
        out_specs=VMEM,
        scratch_shapes=[
            pltpu.VMEM((n, LANES), jnp.bfloat16),
            pltpu.VMEM((COLS, n), jnp.bfloat16),
            pltpu.VMEM((LEAF_DEV + 1, COLS, LEAF), jnp.float32),
            pltpu.SMEM((LEAF_DEV * NEAR + 8,), jnp.int32),
            pltpu.SemaphoreType.DMA((5,)),
        ],
        compiler_params=params(LAST_LIMIT),
        cost_estimate=cost(150),
        name="near_out",
    )(near, count, first, lo, hi, left, right, w, t, *selfs, *lows, *ups)


def swap(x, axis, mask):
    count = lax.axis_size(axis)
    return lax.ppermute(x, axis, [(i, i ^ mask) for i in range(count)])


def after(x, *others):
    return lax.optimization_barrier((x, *others))[0]


def per_device(events, coeffs, tree_perm, near_list, near_count, far_list, skel_low, skel_high):
    group_devs = lax.axis_size("inner")
    group_count = lax.axis_size("outer")
    far_count = far_list.shape[1]
    ev_dev = events.shape[1]
    inner = lax.axis_index("inner").astype(jnp.int32)
    device = lax.axis_index("outer").astype(jnp.int32) * group_devs + inner
    devices = group_devs * group_count
    first = (device * LEAF_DEV).reshape(1)
    me = inner.reshape(1)
    pick = skel_high.reshape(RANK, 1)
    pick = ((pick // RANK) ^ inner) * RANK + pick % RANK

    lo, hi, w, t, own = tree_call(tree_perm, skel_low, events, coeffs)

    low = own
    selfs = []
    pieces = None
    for masks, span in zip(LOW_ROUNDS, SELF_SPANS):
        if pieces is not None:
            low = after(jnp.concatenate(pieces, axis=0), selfs[-1])
        pieces = [low] + [swap(low, "inner", m) for m in masks]
        selfs.append(self_call(after(lo, low), after(hi, low), w, t, *span))
    pieces = [after(p, selfs[-1]) for p in pieces]

    both = ("outer", "inner")
    left = lax.ppermute(after(hi, *pieces), both, [(i, i + 1) for i in range(devices - 1)])
    right = lax.ppermute(after(lo, *pieces), both, [(i + 1, i) for i in range(devices - 1)])

    term, hx, low, low_w = term_call(pick, pieces, lo, hi, w)
    lows = []
    for i, mask in enumerate(SUM_ROUNDS):
        moved = swap(term, "inner", mask)
        lows.append(low_call(far_list, me, after(low, term), low_w, t, 2 * i, 2))
        term = after(term + moved, lows[-1])
    hu = (term * (1.0 / (ev_dev * group_devs) ** 0.5)).astype(jnp.bfloat16)
    ratio = (far_count / group_count) ** 0.5
    upper = jnp.concatenate([hu * jnp.bfloat16(ratio), hx], axis=0)
    up = swap(upper, "outer", 1)
    lows.append(low_call(far_list, me, after(low, upper), low_w, t, 10, 2))
    up = after(up, lows[-1])
    upper = jnp.concatenate([upper, up], axis=0)
    ups = [up, swap(upper, "outer", 2)]
    lows.append(low_call(far_list, me, after(low, upper), low_w, t, 12, 4))
    ups = [after(u, lows[-1]) for u in ups]

    near_scale = 16.0 / (LEAF * NEAR) ** 0.5
    low_scale = 128.0 / (far_count * RANK) ** 0.5
    return last_call(
        (near_scale, low_scale), near_list, near_count, first, lo, hi, left, right, w, t, selfs, lows, ups
    )


def solution(mesh):
    return jax.shard_map(
        per_device,
        mesh=mesh,
        in_specs=(
            P(None, ("outer", "inner")),
            P(None, ("outer", "inner")),
            P(("outer", "inner"), None),
            P(("outer", "inner"), None),
            P(("outer", "inner")),
            P(("outer", "inner"), None),
            P(("outer", "inner"), None),
            P("outer", None),
        ),
        out_specs=P(None, ("outer", "inner")),
        check_vma=False,
    )
```

```python
import functools

import jax
import jax.numpy as jnp
from jax import lax
from jax.experimental import pallas as pl
from jax.experimental.pallas import tpu as pltpu
from jax.sharding import PartitionSpec as P

LEAF = 512
RANK = 128
NEAR = 32
LEAF_DEV = 16
COLS = 64
FEAT = 16
LANES = 128
REACH = 8
LOW_ROUNDS = ((1,), (2,), (4,), (8, 16, 24))
NT = (((1,), (1,)), ((), ()))
NN = (((1,), (0,)), ((), ()))
VMEM_LIMIT = 24 << 20
LAST_LIMIT = 32 << 20

X0 = COLS
N0 = X0 + FEAT
O0 = N0 + 3


def dot(a, b, dims=NN):
    return lax.dot_general(a, b, dims, preferred_element_type=jnp.float32)


def target_map():
    k = lax.broadcasted_iota(jnp.int32, (LANES, LANES), 0)
    m = lax.broadcasted_iota(jnp.int32, (LANES, LANES), 1)
    quarter = (k == m) & (k >= X0) & (k < N0)
    ones = (k == m + 3) & (m >= N0) & (m < O0)
    pieces = (k + 3 == m) & (k >= N0) & (k < O0)
    return jnp.where(quarter, 0.25, jnp.where(ones | pieces, 1.0, 0.0)).astype(jnp.bfloat16)


def targets(rows):
    return dot(rows, target_map()).astype(jnp.bfloat16)


def weight_map():
    k = lax.broadcasted_iota(jnp.int32, (COLS, LANES), 0)
    m = lax.broadcasted_iota(jnp.int32, (COLS, LANES), 1)
    return jnp.where(k == m, 1.0, 0.0).astype(jnp.bfloat16)


def weights(rows):
    return dot(weight_map(), rows, NT).astype(jnp.bfloat16)


def block(i, size):
    return pl.ds(pl.multiple_of(i * size, size), size)


def cost(pairs):
    return pl.CostEstimate(
        flops=pairs * 2 * LEAF * LEAF * 384, bytes_accessed=4 << 20, transcendentals=pairs * LEAF * LEAF
    )


def features(xb):
    x = xb.astype(jnp.float32)
    n = jnp.sum(x * x, axis=0, keepdims=True) * -0.125
    n1 = n.astype(jnp.bfloat16).astype(jnp.float32)
    n2 = (n - n1).astype(jnp.bfloat16).astype(jnp.float32)
    n3 = (n - n1 - n2).astype(jnp.bfloat16).astype(jnp.float32)
    r = lax.broadcasted_iota(jnp.int32, xb.shape, 0)
    one = jnp.where(r < 6, 1.0, 0.0)
    ext = jnp.where(r == 0, n1, jnp.where(r == 1, n2, jnp.where(r == 2, n3, one)))
    pad = jnp.zeros((LANES - COLS - 2 * FEAT, xb.shape[1]), jnp.bfloat16)
    return [xb, ext.astype(jnp.bfloat16), pad]


def tree_kernel(
    perm_hbm, skel_hbm, events_hbm, coeffs_hbm, lo_out, hi_out, w_out, t_out, own_out,
    table, picked, spick, perm, skel, events, coeffs, sems,
):
    moves = [
        pltpu.make_async_copy(src, dst, sems.at[i])
        for i, (src, dst) in enumerate(
            [(events_hbm, events), (coeffs_hbm, coeffs), (perm_hbm, perm), (skel_hbm, skel)]
        )
    ]
    for m in moves:
        m.start()
    for m in moves:
        m.wait()
    chunks = events.shape[1] // LEAF

    def build(c, _):
        at = block(c, LEAF)
        full = jnp.concatenate([coeffs[:, at]] + features(events[:, at]), axis=0)
        table[at, :] = full.T.astype(jnp.float32)
        return 0

    lax.fori_loop(0, chunks, build, 0)

    def fetch(ids):
        return jnp.concatenate([table[pl.ds(i, 1), :] for i in ids], axis=0)

    for j in range(0, RANK, 8):
        spick[j : j + 8, :] = fetch([perm[0, skel[0, j + u]] for u in range(8)])

    step = 64

    def gather(rows_out, base, c, _):
        def some(b, _):
            for v in range(0, step, 8):
                e = (base + c) * LEAF + b * step + v
                picked[block(b * (step // 8) + v // 8, 8), :] = fetch(
                    [perm[0, e + u] for u in range(8)]
                )
            return 0

        lax.fori_loop(0, LEAF // step, some, 0)
        at = block(base + c, LEAF)
        r = picked[...]
        rb = r.astype(jnp.bfloat16)
        rows_out[block(c, LEAF), :] = rb
        w_out[:, at] = r.T[:COLS].astype(jnp.bfloat16)
        t_out[at, :] = targets(rb)
        return 0

    half = chunks // 2
    lax.fori_loop(0, half, functools.partial(gather, lo_out, 0), 0)
    lax.fori_loop(0, half, functools.partial(gather, hi_out, half), 0)

    s = spick[...]
    ts = targets(s.astype(jnp.bfloat16))
    su = halves_dot(lo_out, hi_out, w_out, ts) / events.shape[1] ** 0.5
    own_out[:COLS, :] = su.astype(jnp.bfloat16)
    own_out[COLS:, :] = s.T[X0:N0].astype(jnp.bfloat16)


def halves_dot(lo, hi, w, ts):
    half = lo.shape[0]
    ka = jnp.exp(dot(lo[...], ts, NT)).astype(jnp.bfloat16)
    kb = jnp.exp(dot(hi[...], ts, NT)).astype(jnp.bfloat16)
    return dot(w[:, :half], ka) + dot(w[:, half:], kb)


SMEM = pl.BlockSpec(memory_space=pltpu.SMEM)
VMEM = pl.BlockSpec(memory_space=pltpu.VMEM)
ANY = pl.BlockSpec(memory_space=pl.ANY)
HBM = pl.BlockSpec(memory_space=pltpu.HBM)


def params(limit=VMEM_LIMIT):
    return pltpu.CompilerParams(vmem_limit_bytes=limit)


def tree_call(perm, skel, events, coeffs):
    n = events.shape[1]
    return pl.pallas_call(
        tree_kernel,
        out_shape=(
            jax.ShapeDtypeStruct((n // 2, LANES), jnp.bfloat16),
            jax.ShapeDtypeStruct((n // 2, LANES), jnp.bfloat16),
            jax.ShapeDtypeStruct((COLS, n), jnp.bfloat16),
            jax.ShapeDtypeStruct((n, LANES), jnp.bfloat16),
            jax.ShapeDtypeStruct((COLS + FEAT, RANK), jnp.bfloat16),
        ),
        in_specs=[HBM] * 4,
        out_specs=(VMEM,) * 5,
        scratch_shapes=[
            pltpu.VMEM((n, LANES), jnp.float32),
            pltpu.VMEM((LEAF, LANES), jnp.float32),
            pltpu.VMEM((RANK, LANES), jnp.float32),
            pltpu.SMEM(perm.shape, jnp.int32),
            pltpu.SMEM(skel.shape, jnp.int32),
            pltpu.VMEM(events.shape, jnp.bfloat16),
            pltpu.VMEM(coeffs.shape, jnp.bfloat16),
            pltpu.SemaphoreType.DMA((4,)),
        ],
        compiler_params=params(),
        name="tree_rows",
    )(perm, skel, events, coeffs)


def event_rows(xb):
    none = jnp.zeros((COLS, xb.shape[1]), jnp.bfloat16)
    return jnp.concatenate([none] + features(xb), axis=0).T


def term_kernel(scale, parts, me, picks, *refs):
    pieces, (lo, hi, w, term_out, low_out, low_w, low_x) = refs[:parts], refs[parts:]
    each = COLS + FEAT
    blocks = pieces[0].shape[0] // each
    size = blocks * RANK
    for i, piece in enumerate(pieces):
        for b in range(blocks):
            at = slice((i * blocks + b) * RANK, (i * blocks + b + 1) * RANK)
            low_w[:, at] = piece[b * each : b * each + COLS, :]
            low_x[:, at] = piece[b * each + COLS : (b + 1) * each, :]
        at = slice(i * size, (i + 1) * size)
        low_out[at, :] = event_rows(low_x[:, at])
    p = picks[...]
    p = ((p // RANK) ^ me[0]) * RANK + p % RANK
    hit = lax.broadcasted_iota(jnp.int32, (parts * size, RANK), 0) == p
    hx = dot(low_x[...], jnp.where(hit, 1.0, 0.0).astype(jnp.bfloat16)).astype(jnp.bfloat16)
    term_out[COLS:, :] = hx
    term = halves_dot(lo, hi, w, targets(event_rows(hx))) * scale
    term_out[:COLS, :] = term.astype(jnp.bfloat16)


def term_call(scale, me, picks, pieces, lo, hi, w):
    total = len(pieces) * pieces[0].shape[0] // (COLS + FEAT) * RANK
    return pl.pallas_call(
        lambda *refs: term_kernel(scale, len(pieces), *refs),
        out_shape=(
            jax.ShapeDtypeStruct((COLS + FEAT, RANK), jnp.bfloat16),
            jax.ShapeDtypeStruct((total, LANES), jnp.bfloat16),
            jax.ShapeDtypeStruct((COLS, total), jnp.bfloat16),
        ),
        in_specs=[SMEM] + [VMEM] * (4 + len(pieces)),
        out_specs=(VMEM,) * 3,
        scratch_shapes=[pltpu.VMEM((FEAT, total), jnp.bfloat16)],
        compiler_params=params(),
        cost_estimate=cost(4),
        name="high_term",
    )(me, picks, *pieces, lo, hi, w)


def low_kernel(far, me, low, low_w, t, part):
    groups = far.shape[1] // 4
    both = 2

    def some(b, _):
        ks = []
        for j in range(both):
            leaf = b * both + j
            tl = t[block(leaf, LEAF), :]
            for g in range(groups):
                spots = [block(far[leaf, 4 * g + i] ^ me[0], RANK) for i in range(4)]
                r = jnp.concatenate([low[s, :] for s in spots], axis=0)
                ks.append((spots, jnp.exp(dot(r, tl, NT)).astype(jnp.bfloat16)))
        for j in range(both):
            total = None
            for spots, k in ks[j * groups : (j + 1) * groups]:
                p = dot(jnp.concatenate([low_w[:, s] for s in spots], axis=1), k)
                total = p if total is None else total + p
            part[b * both + j] = total
        return 0

    lax.fori_loop(0, LEAF_DEV // both, some, 0)


def low_call(far, me, low, low_w, t):
    return pl.pallas_call(
        low_kernel,
        out_shape=jax.ShapeDtypeStruct((LEAF_DEV, COLS, LEAF), jnp.float32),
        in_specs=[SMEM, SMEM, VMEM, VMEM, VMEM],
        out_specs=VMEM,
        compiler_params=params(),
        cost_estimate=cost(64),
        name="far_low",
    )(far, me, low, low_w, t)


def near_kernel(scales, near, count, first, lo, hi, left, right, w_own, t, low, out, rows, w, acc, pairs, sems):
    near_scale, low_scale = scales
    side = REACH * LEAF
    own = LEAF_DEV * LEAF
    moves = [
        pltpu.make_async_copy(left, rows.at[pl.ds(0, side), :], sems.at[0]),
        pltpu.make_async_copy(right, rows.at[pl.ds(side + own, side), :], sems.at[1]),
        pltpu.make_async_copy(lo, rows.at[pl.ds(side, own // 2), :], sems.at[2]),
        pltpu.make_async_copy(hi, rows.at[pl.ds(side + own // 2, own // 2), :], sems.at[3]),
        pltpu.make_async_copy(w_own, w.at[:, pl.ds(side, own)], sems.at[4]),
    ]
    for m in moves:
        m.start()

    def leaf_slots(leaf, n):
        def slot(s, n):
            pairs[n] = leaf * 64 + (near[leaf, s] - first[0] + REACH)
            return n + 1

        return lax.fori_loop(0, count[leaf], slot, n)

    n = lax.fori_loop(0, LEAF_DEV, leaf_slots, jnp.int32(0))
    for u in range(8):
        pairs[n + u] = LEAF_DEV * 64

    acc[...] = jnp.zeros_like(acc)
    moves[0].wait()
    moves[1].wait()

    def flip(b, _):
        at = block(b, LEAF)
        there = block(b + REACH + LEAF_DEV, LEAF)
        w[:, at] = weights(rows[at, :])
        w[:, there] = weights(rows[there, :])
        return 0

    lax.fori_loop(0, REACH, flip, 0)
    for m in moves[2:]:
        m.wait()

    def step(begin, many):
        ks = []
        for u in range(many):
            e = pairs[begin + u]
            leaf, at = e // 64, e % 64
            tl = t[block(jnp.minimum(leaf, LEAF_DEV - 1), LEAF), :]
            k = jnp.exp(dot(rows[block(at, LEAF), :], tl, NT)).astype(jnp.bfloat16)
            ks.append((leaf, at, k))
        for leaf, at, k in ks:
            acc[leaf] = acc[leaf] + dot(w[:, block(at, LEAF)], k)

    def eight(s, _):
        step(s * 8, 8)
        return 0

    lax.fori_loop(0, n // 8, eight, 0)

    def four(s, _):
        step(n // 8 * 8 + s * 4, 4)
        return 0

    lax.fori_loop(0, (n % 8 + 3) // 4, four, 0)

    for leaf in range(LEAF_DEV):
        at = slice(leaf * LEAF, (leaf + 1) * LEAF)
        out[:, at] = acc[leaf] * near_scale + low[leaf] * low_scale


def near_call(scales, near, count, first, lo, hi, left, right, w, t, low):
    n = (LEAF_DEV + 2 * REACH) * LEAF
    return pl.pallas_call(
        lambda *refs: near_kernel(scales, *refs),
        out_shape=jax.ShapeDtypeStruct((COLS, LEAF_DEV * LEAF), jnp.float32),
        in_specs=[SMEM] * 3 + [ANY] * 5 + [VMEM] * 2,
        out_specs=VMEM,
        scratch_shapes=[
            pltpu.VMEM((n, LANES), jnp.bfloat16),
            pltpu.VMEM((COLS, n), jnp.bfloat16),
            pltpu.VMEM((LEAF_DEV + 1, COLS, LEAF), jnp.float32),
            pltpu.SMEM((LEAF_DEV * NEAR + 8,), jnp.int32),
            pltpu.SemaphoreType.DMA((5,)),
        ],
        compiler_params=params(LAST_LIMIT),
        cost_estimate=cost(150),
        name="near_sum",
    )(near, count, first, lo, hi, left, right, w, t, low)


def high_kernel(scale, ratio, group_count, own_group, terms, t, part, out):
    each = COLS + FEAT
    members = terms.shape[0] // each // group_count
    ws, xs = [], []
    for k in range(1, group_count):
        group = (own_group[0] + k) % group_count
        base = group * (members * each)
        total = jnp.zeros((COLS, RANK), jnp.float32)
        for m in range(members):
            at = pl.ds(pl.multiple_of(base + m * each, 16), COLS)
            total = total + terms[at, :].astype(jnp.float32)
        ws.append(total.astype(jnp.bfloat16) * jnp.bfloat16(ratio))
        xs.append(terms[pl.ds(pl.multiple_of(base + COLS, 16), FEAT), :])
    high_w = jnp.concatenate(ws, axis=1)
    high_x = event_rows(jnp.concatenate(xs, axis=1))
    many = 8

    def some(b, _):
        ats = [block(b * many + j, LEAF) for j in range(many)]
        ks = [jnp.exp(dot(high_x, t[at, :], NT)).astype(jnp.bfloat16) for at in ats]
        for at, k in zip(ats, ks):
            out[:, at] = (part[:, at] + dot(high_w, k) * scale).astype(jnp.bfloat16)
        return 0

    lax.fori_loop(0, LEAF_DEV // many, some, 0)


def high_call(scale, ratio, group_count, own_group, terms, t, part):
    return pl.pallas_call(
        lambda *refs: high_kernel(scale, ratio, group_count, *refs),
        out_shape=jax.ShapeDtypeStruct(part.shape, jnp.bfloat16),
        in_specs=[SMEM] + [VMEM] * 3,
        out_specs=VMEM,
        compiler_params=params(),
        cost_estimate=cost(12),
        name="high_out",
    )(own_group, terms, t, part)


def swap(x, axis, mask):
    count = lax.axis_size(axis)
    return lax.ppermute(x, axis, [(i, i ^ mask) for i in range(count)])


def after(x, *others):
    return lax.optimization_barrier((x, *others))[0]


def per_device(events, coeffs, tree_perm, near_list, near_count, far_list, skel_low, skel_high):
    group_devs = lax.axis_size("inner")
    group_count = lax.axis_size("outer")
    far_count = far_list.shape[1]
    ev_dev = events.shape[1]
    inner = lax.axis_index("inner").astype(jnp.int32)
    device = lax.axis_index("outer").astype(jnp.int32) * group_devs + inner
    devices = group_devs * group_count
    first = (device * LEAF_DEV).reshape(1)
    me = inner.reshape(1)
    lo, hi, w, t, own = tree_call(tree_perm, skel_low, events, coeffs)

    low = own
    for masks in LOW_ROUNDS:
        pieces = [low] + [swap(low, "inner", m) for m in masks]
        low = jnp.concatenate(pieces, axis=0) if masks is not LOW_ROUNDS[-1] else low

    both = ("outer", "inner")
    left = lax.ppermute(after(hi, low), both, [(i, i + 1) for i in range(devices - 1)])
    right = lax.ppermute(after(lo, low), both, [(i + 1, i) for i in range(devices - 1)])

    scale = 1.0 / (ev_dev * group_devs) ** 0.5
    term, low, low_w = term_call(scale, me, skel_high, pieces, lo, hi, w)
    terms = lax.all_gather(term, both, axis=0, tiled=True)
    far = low_call(far_list, me, low, low_w, t)
    near_scale = 16.0 / (LEAF * NEAR) ** 0.5
    low_scale = 128.0 / (far_count * RANK) ** 0.5
    ratio = (far_count / group_count) ** 0.5
    part = near_call(
        (near_scale, low_scale), near_list, near_count, first, lo, hi, left, right, w, t, far
    )
    group = lax.axis_index("outer").astype(jnp.int32).reshape(1)
    return high_call(low_scale, ratio, group_count, group, after(terms, part), t, part)


def solution(mesh):
    return jax.shard_map(
        per_device,
        mesh=mesh,
        in_specs=(
            P(None, ("outer", "inner")),
            P(None, ("outer", "inner")),
            P(("outer", "inner"), None),
            P(("outer", "inner"), None),
            P(("outer", "inner")),
            P(("outer", "inner"), None),
            P(("outer", "inner"), None),
            P("outer", None),
        ),
        out_specs=P(None, ("outer", "inner")),
        check_vma=False,
    )
```

```python
import functools

import jax
import jax.numpy as jnp
from jax import lax
from jax.experimental import pallas as pl
from jax.experimental.pallas import tpu as pltpu
from jax.sharding import PartitionSpec as P

LEAF = 512
RANK = 128
NEAR = 32
LEAF_DEV = 16
COLS = 64
FEAT = 16
LANES = 128
REACH = 8
LOW_ROUNDS = ((1,), (2,), (4,), (8, 16, 24))
SELF_SPANS = ((0, 2), (2, 2), (4, 4), (8, 8))
NT = (((1,), (1,)), ((), ()))
NN = (((1,), (0,)), ((), ()))
VMEM_LIMIT = 60 << 20

X0 = COLS
N0 = X0 + FEAT
O0 = N0 + 3


def dot(a, b, dims=NN):
    return lax.dot_general(a, b, dims, preferred_element_type=jnp.float32)


def target_map():
    k = lax.broadcasted_iota(jnp.int32, (LANES, LANES), 0)
    m = lax.broadcasted_iota(jnp.int32, (LANES, LANES), 1)
    quarter = (k == m) & (k >= X0) & (k < N0)
    ones = (k == m + 3) & (m >= N0) & (m < O0)
    pieces = (k + 3 == m) & (k >= N0) & (k < O0)
    return jnp.where(quarter, 0.25, jnp.where(ones | pieces, 1.0, 0.0)).astype(jnp.bfloat16)


def targets(rows):
    return dot(rows, target_map()).astype(jnp.bfloat16)


def weight_map():
    k = lax.broadcasted_iota(jnp.int32, (COLS, LANES), 0)
    m = lax.broadcasted_iota(jnp.int32, (COLS, LANES), 1)
    return jnp.where(k == m, 1.0, 0.0).astype(jnp.bfloat16)


def weights(rows):
    return dot(weight_map(), rows, NT).astype(jnp.bfloat16)


def block(i, size):
    return pl.ds(pl.multiple_of(i * size, size), size)


def cost(pairs):
    return pl.CostEstimate(
        flops=pairs * 2 * LEAF * LEAF * 384, bytes_accessed=4 << 20, transcendentals=pairs * LEAF * LEAF
    )


def features(xb):
    x = xb.astype(jnp.float32)
    n = jnp.sum(x * x, axis=0, keepdims=True) * -0.125
    n1 = n.astype(jnp.bfloat16).astype(jnp.float32)
    n2 = (n - n1).astype(jnp.bfloat16).astype(jnp.float32)
    n3 = (n - n1 - n2).astype(jnp.bfloat16).astype(jnp.float32)
    r = lax.broadcasted_iota(jnp.int32, xb.shape, 0)
    one = jnp.where(r < 6, 1.0, 0.0)
    ext = jnp.where(r == 0, n1, jnp.where(r == 1, n2, jnp.where(r == 2, n3, one)))
    pad = jnp.zeros((LANES - COLS - 2 * FEAT, xb.shape[1]), jnp.bfloat16)
    return [xb, ext.astype(jnp.bfloat16), pad]


def tree_kernel(
    perm_hbm, skel_hbm, events_hbm, coeffs_hbm, lo_hbm, hi_hbm, w_hbm, t_hbm, own_out,
    lo_out, hi_out, w_out, t_out, table, picked, spick, perm, skel, events, coeffs, sems,
):
    moves = [
        pltpu.make_async_copy(src, dst, sems.at[i])
        for i, (src, dst) in enumerate(
            [(events_hbm, events), (coeffs_hbm, coeffs), (perm_hbm, perm), (skel_hbm, skel)]
        )
    ]
    for m in moves:
        m.start()
    moves[0].wait()
    moves[1].wait()
    chunks = events.shape[1] // LEAF

    def build(c, _):
        at = block(c, LEAF)
        full = jnp.concatenate([coeffs[:, at]] + features(events[:, at]), axis=0)
        table[at, :] = full.T.astype(jnp.float32)
        return 0

    lax.fori_loop(0, chunks, build, 0)
    moves[2].wait()
    moves[3].wait()

    def fetch(ids):
        return jnp.concatenate([table[pl.ds(i, 1), :] for i in ids], axis=0)

    for j in range(0, RANK, 8):
        spick[j : j + 8, :] = fetch([perm[0, skel[0, j + u]] for u in range(8)])

    step = 64

    def gather(rows_out, base, c, _):
        def some(b, _):
            for v in range(0, step, 8):
                e = (base + c) * LEAF + b * step + v
                picked[block(b * (step // 8) + v // 8, 8), :] = fetch(
                    [perm[0, e + u] for u in range(8)]
                )
            return 0

        lax.fori_loop(0, LEAF // step, some, 0)
        at = block(base + c, LEAF)
        r = picked[...]
        rb = r.astype(jnp.bfloat16)
        rows_out[block(c, LEAF), :] = rb
        w_out[:, at] = r.T[:COLS].astype(jnp.bfloat16)
        t_out[at, :] = targets(rb)
        return 0

    half = chunks // 2
    lax.fori_loop(0, half, functools.partial(gather, lo_out, 0), 0)
    outs = [
        pltpu.make_async_copy(src, dst, sems.at[4 + i])
        for i, (src, dst) in enumerate(
            [(lo_out, lo_hbm), (hi_out, hi_hbm), (w_out, w_hbm), (t_out, t_hbm)]
        )
    ]
    outs[0].start()
    lax.fori_loop(0, half, functools.partial(gather, hi_out, half), 0)
    for m in outs[1:]:
        m.start()

    s = spick[...]
    ts = targets(s.astype(jnp.bfloat16))
    su = halves_dot(lo_out, hi_out, w_out, ts) / events.shape[1] ** 0.5
    own_out[:COLS, :] = su.astype(jnp.bfloat16)
    own_out[COLS:, :] = s.T[X0:N0].astype(jnp.bfloat16)
    for m in outs:
        m.wait()


def halves_dot(lo, hi, w, ts):
    half = lo.shape[0]
    ka = jnp.exp(dot(lo[...], ts, NT)).astype(jnp.bfloat16)
    kb = jnp.exp(dot(hi[...], ts, NT)).astype(jnp.bfloat16)
    return dot(w[:, :half], ka) + dot(w[:, half:], kb)


SMEM = pl.BlockSpec(memory_space=pltpu.SMEM)
VMEM = pl.BlockSpec(memory_space=pltpu.VMEM)
ANY = pl.BlockSpec(memory_space=pl.ANY)


def params(limit=VMEM_LIMIT):
    return pltpu.CompilerParams(vmem_limit_bytes=limit)


def tree_call(perm, skel, events, coeffs):
    n = events.shape[1]
    return pl.pallas_call(
        tree_kernel,
        out_shape=(
            jax.ShapeDtypeStruct((n // 2, LANES), jnp.bfloat16),
            jax.ShapeDtypeStruct((n // 2, LANES), jnp.bfloat16),
            jax.ShapeDtypeStruct((COLS, n), jnp.bfloat16),
            jax.ShapeDtypeStruct((n, LANES), jnp.bfloat16),
            jax.ShapeDtypeStruct((COLS + FEAT, RANK), jnp.bfloat16),
        ),
        in_specs=[ANY] * 4,
        out_specs=(ANY,) * 4 + (VMEM,),
        scratch_shapes=[
            pltpu.VMEM((n // 2, LANES), jnp.bfloat16),
            pltpu.VMEM((n // 2, LANES), jnp.bfloat16),
            pltpu.VMEM((COLS, n), jnp.bfloat16),
            pltpu.VMEM((n, LANES), jnp.bfloat16),
            pltpu.VMEM((n, LANES), jnp.float32),
            pltpu.VMEM((LEAF, LANES), jnp.float32),
            pltpu.VMEM((RANK, LANES), jnp.float32),
            pltpu.SMEM(perm.shape, jnp.int32),
            pltpu.SMEM(skel.shape, jnp.int32),
            pltpu.VMEM(events.shape, jnp.bfloat16),
            pltpu.VMEM(coeffs.shape, jnp.bfloat16),
            pltpu.SemaphoreType.DMA((8,)),
        ],
        compiler_params=params(),
        name="tree_rows",
    )(perm, skel, events, coeffs)


def self_kernel(leaves, rows, w, t, part):
    for leaf in range(leaves):
        at = slice(leaf * LEAF, (leaf + 1) * LEAF)
        k = jnp.exp(dot(rows[at, :], t[at, :], NT)).astype(jnp.bfloat16)
        part[leaf] = dot(w[:, at], k)


def self_call(lo, hi, w, t, first, leaves):
    spot = first // leaves
    halves = LEAF_DEV // 2 // leaves
    rows, row_spot = (lo, spot) if spot < halves else (hi, spot - halves)
    size = leaves * LEAF
    return pl.pallas_call(
        lambda *refs: self_kernel(leaves, *refs),
        out_shape=jax.ShapeDtypeStruct((leaves, COLS, LEAF), jnp.float32),
        grid=(1,),
        in_specs=[
            pl.BlockSpec((size, LANES), lambda i: (row_spot, 0)),
            pl.BlockSpec((COLS, size), lambda i: (0, spot)),
            pl.BlockSpec((size, LANES), lambda i: (spot, 0)),
        ],
        out_specs=pl.BlockSpec((leaves, COLS, LEAF), lambda i: (0, 0, 0)),
        compiler_params=params(),
        cost_estimate=cost(leaves),
        name="near_self",
    )(rows, w, t)


def event_rows(xb):
    none = jnp.zeros((COLS, xb.shape[1]), jnp.bfloat16)
    return jnp.concatenate([none] + features(xb), axis=0).T


def term_kernel(scale, parts, me, picks, *refs):
    pieces, refs = refs[:parts], refs[parts:]
    sources, (term_out, low_out, low_w, low_x, lo, hi, w, sems) = refs[:3], refs[3:]
    moves = [
        pltpu.make_async_copy(src, dst, sems.at[i])
        for i, (src, dst) in enumerate(zip(sources, (lo, hi, w)))
    ]
    for m in moves:
        m.start()
    each = COLS + FEAT
    blocks = pieces[0].shape[0] // each
    size = blocks * RANK
    for i, piece in enumerate(pieces):
        for b in range(blocks):
            at = slice((i * blocks + b) * RANK, (i * blocks + b + 1) * RANK)
            low_w[:, at] = piece[b * each : b * each + COLS, :]
            low_x[:, at] = piece[b * each + COLS : (b + 1) * each, :]
        at = slice(i * size, (i + 1) * size)
        low_out[at, :] = event_rows(low_x[:, at])
    p = picks[...]
    p = ((p // RANK) ^ me[0]) * RANK + p % RANK
    hit = lax.broadcasted_iota(jnp.int32, (parts * size, RANK), 0) == p
    hx = dot(low_x[...], jnp.where(hit, 1.0, 0.0).astype(jnp.bfloat16)).astype(jnp.bfloat16)
    term_out[COLS:, :] = hx
    for m in moves:
        m.wait()
    term = halves_dot(lo, hi, w, targets(event_rows(hx))) * scale
    term_out[:COLS, :] = term.astype(jnp.bfloat16)


def term_call(scale, me, picks, pieces, lo, hi, w):
    total = len(pieces) * pieces[0].shape[0] // (COLS + FEAT) * RANK
    return pl.pallas_call(
        lambda *refs: term_kernel(scale, len(pieces), *refs),
        out_shape=(
            jax.ShapeDtypeStruct((COLS + FEAT, RANK), jnp.bfloat16),
            jax.ShapeDtypeStruct((total, LANES), jnp.bfloat16),
            jax.ShapeDtypeStruct((COLS, total), jnp.bfloat16),
        ),
        in_specs=[SMEM] + [VMEM] * (1 + len(pieces)) + [ANY] * 3,
        out_specs=(VMEM,) * 3,
        scratch_shapes=[
            pltpu.VMEM((FEAT, total), jnp.bfloat16),
            pltpu.VMEM(lo.shape, jnp.bfloat16),
            pltpu.VMEM(hi.shape, jnp.bfloat16),
            pltpu.VMEM(w.shape, jnp.bfloat16),
            pltpu.SemaphoreType.DMA((3,)),
        ],
        compiler_params=params(),
        cost_estimate=cost(4),
        name="high_term",
    )(me, picks, *pieces, lo, hi, w)


def low_kernel(far, me, low, low_w, t, part):
    groups = far.shape[1] // 4
    leaves = part.shape[0]
    ks = []
    for j in range(leaves):
        leaf = pl.program_id(0) * leaves + j
        tl = t[j * LEAF : (j + 1) * LEAF, :]
        for g in range(groups):
            spots = [block(far[leaf, 4 * g + i] ^ me[0], RANK) for i in range(4)]
            r = jnp.concatenate([low[s, :] for s in spots], axis=0)
            ks.append((spots, jnp.exp(dot(r, tl, NT)).astype(jnp.bfloat16)))
    for j in range(leaves):
        total = None
        for spots, k in ks[j * groups : (j + 1) * groups]:
            p = dot(jnp.concatenate([low_w[:, s] for s in spots], axis=1), k)
            total = p if total is None else total + p
        part[j] = total


def low_call(far, me, low, low_w, t):
    leaves = 2
    return pl.pallas_call(
        low_kernel,
        out_shape=jax.ShapeDtypeStruct((LEAF_DEV, COLS, LEAF), jnp.float32),
        grid=(LEAF_DEV // leaves,),
        in_specs=[
            SMEM,
            SMEM,
            pl.BlockSpec(low.shape, lambda i: (0, 0)),
            pl.BlockSpec(low_w.shape, lambda i: (0, 0)),
            pl.BlockSpec((leaves * LEAF, LANES), lambda i: (i, 0)),
        ],
        out_specs=pl.BlockSpec((leaves, COLS, LEAF), lambda i: (i, 0, 0)),
        compiler_params=params(),
        cost_estimate=cost(64),
        name="far_low",
    )(far, me, low, low_w, t)


def near_kernel(scales, near, count, first, lo, hi, left, right, w_own, t_hbm, low_hbm, *refs):
    near_scale, low_scale = scales
    selfs, (out, rows, w, t, low, acc, pairs, sems) = refs[:-8], refs[-8:]
    side = REACH * LEAF
    own = LEAF_DEV * LEAF
    moves = [
        pltpu.make_async_copy(left, rows.at[pl.ds(0, side), :], sems.at[0]),
        pltpu.make_async_copy(right, rows.at[pl.ds(side + own, side), :], sems.at[1]),
        pltpu.make_async_copy(lo, rows.at[pl.ds(side, own // 2), :], sems.at[2]),
        pltpu.make_async_copy(hi, rows.at[pl.ds(side + own // 2, own // 2), :], sems.at[3]),
        pltpu.make_async_copy(w_own, w.at[:, pl.ds(side, own)], sems.at[4]),
        pltpu.make_async_copy(t_hbm, t, sems.at[5]),
    ]
    leaf = 0
    for part in selfs:
        there = acc.at[pl.ds(leaf, part.shape[0])]
        moves.append(pltpu.make_async_copy(part, there, sems.at[len(moves)]))
        leaf += part.shape[0]
    low_move = pltpu.make_async_copy(low_hbm, low, sems.at[len(moves)])
    for m in moves:
        m.start()
    low_move.start()

    def leaf_slots(leaf, n):
        def slot(s, n):
            pairs[n] = leaf * 64 + (near[leaf, s] - first[0] + REACH)
            return n + 1

        return lax.fori_loop(1, count[leaf], slot, n)

    n = lax.fori_loop(0, LEAF_DEV, leaf_slots, jnp.int32(0))
    for u in range(8):
        pairs[n + u] = LEAF_DEV * 64

    acc[LEAF_DEV] = jnp.zeros((COLS, LEAF), jnp.float32)
    moves[0].wait()
    moves[1].wait()

    def flip(b, _):
        at = block(b, LEAF)
        there = block(b + REACH + LEAF_DEV, LEAF)
        w[:, at] = weights(rows[at, :])
        w[:, there] = weights(rows[there, :])
        return 0

    lax.fori_loop(0, REACH, flip, 0)
    for m in moves[2:]:
        m.wait()

    def step(begin, many):
        ks = []
        for u in range(many):
            e = pairs[begin + u]
            leaf, at = e // 64, e % 64
            tl = t[block(jnp.minimum(leaf, LEAF_DEV - 1), LEAF), :]
            k = jnp.exp(dot(rows[block(at, LEAF), :], tl, NT)).astype(jnp.bfloat16)
            ks.append((leaf, at, k))
        for leaf, at, k in ks:
            acc[leaf] = acc[leaf] + dot(w[:, block(at, LEAF)], k)

    def eight(s, _):
        step(s * 8, 8)
        return 0

    lax.fori_loop(0, n // 8, eight, 0)

    def four(s, _):
        step(n // 8 * 8 + s * 4, 4)
        return 0

    lax.fori_loop(0, (n % 8 + 3) // 4, four, 0)

    low_move.wait()
    for leaf in range(LEAF_DEV):
        at = slice(leaf * LEAF, (leaf + 1) * LEAF)
        out[:, at] = acc[leaf] * near_scale + low[leaf] * low_scale


def near_call(scales, near, count, first, lo, hi, left, right, w, t, low, selfs):
    n = (LEAF_DEV + 2 * REACH) * LEAF
    return pl.pallas_call(
        lambda *refs: near_kernel(scales, *refs),
        out_shape=jax.ShapeDtypeStruct((COLS, LEAF_DEV * LEAF), jnp.float32),
        in_specs=[SMEM] * 3 + [ANY] * (7 + len(selfs)),
        out_specs=VMEM,
        scratch_shapes=[
            pltpu.VMEM((n, LANES), jnp.bfloat16),
            pltpu.VMEM((COLS, n), jnp.bfloat16),
            pltpu.VMEM(t.shape, jnp.bfloat16),
            pltpu.VMEM(low.shape, jnp.float32),
            pltpu.VMEM((LEAF_DEV + 1, COLS, LEAF), jnp.float32),
            pltpu.SMEM((LEAF_DEV * NEAR + 8,), jnp.int32),
            pltpu.SemaphoreType.DMA((7 + len(selfs),)),
        ],
        compiler_params=params(),
        cost_estimate=cost(150),
        name="near_sum",
    )(near, count, first, lo, hi, left, right, w, t, low, *selfs)


def high_kernel(scale, ratio, group_count, own_group, terms, t, part, out, high_w, high_x):
    @pl.when(pl.program_id(0) == 0)
    def _():
        each = COLS + FEAT
        members = terms.shape[0] // each // group_count
        xs = []
        for k in range(1, group_count):
            group = (own_group[0] + k) % group_count
            base = group * (members * each)
            total = jnp.zeros((COLS, RANK), jnp.float32)
            for m in range(members):
                at = pl.ds(pl.multiple_of(base + m * each, 16), COLS)
                total = total + terms[at, :].astype(jnp.float32)
            spot = slice((k - 1) * RANK, k * RANK)
            high_w[:, spot] = total.astype(jnp.bfloat16) * jnp.bfloat16(ratio)
            xs.append(terms[pl.ds(pl.multiple_of(base + COLS, 16), FEAT), :])
        high_x[...] = event_rows(jnp.concatenate(xs, axis=1))

    many = out.shape[1] // LEAF
    ats = [slice(j * LEAF, (j + 1) * LEAF) for j in range(many)]
    ks = [jnp.exp(dot(high_x[...], t[at, :], NT)).astype(jnp.bfloat16) for at in ats]
    for at, k in zip(ats, ks):
        out[:, at] = (part[:, at] + dot(high_w[...], k) * scale).astype(jnp.bfloat16)


def high_call(scale, ratio, group_count, own_group, terms, t, part):
    many = 4
    total = (group_count - 1) * RANK
    return pl.pallas_call(
        lambda *refs: high_kernel(scale, ratio, group_count, *refs),
        out_shape=jax.ShapeDtypeStruct(part.shape, jnp.bfloat16),
        grid=(LEAF_DEV // many,),
        in_specs=[
            SMEM,
            pl.BlockSpec(terms.shape, lambda i: (0, 0)),
            pl.BlockSpec((many * LEAF, LANES), lambda i: (i, 0)),
            pl.BlockSpec((COLS, many * LEAF), lambda i: (0, i)),
        ],
        out_specs=pl.BlockSpec((COLS, many * LEAF), lambda i: (0, i)),
        scratch_shapes=[
            pltpu.VMEM((COLS, total), jnp.bfloat16),
            pltpu.VMEM((total, LANES), jnp.bfloat16),
        ],
        compiler_params=params(),
        cost_estimate=cost(12),
        name="high_out",
    )(own_group, terms, t, part)


def swap(x, axis, mask):
    count = lax.axis_size(axis)
    return lax.ppermute(x, axis, [(i, i ^ mask) for i in range(count)])


def after(x, *others):
    return lax.optimization_barrier((x, *others))[0]


def per_device(events, coeffs, tree_perm, near_list, near_count, far_list, skel_low, skel_high):
    group_devs = lax.axis_size("inner")
    group_count = lax.axis_size("outer")
    far_count = far_list.shape[1]
    ev_dev = events.shape[1]
    inner = lax.axis_index("inner").astype(jnp.int32)
    device = lax.axis_index("outer").astype(jnp.int32) * group_devs + inner
    devices = group_devs * group_count
    first = (device * LEAF_DEV).reshape(1)
    me = inner.reshape(1)
    lo, hi, w, t, own = tree_call(tree_perm, skel_low, events, coeffs)

    low = own
    selfs = []
    pieces = None
    for masks, span in zip(LOW_ROUNDS, SELF_SPANS):
        if pieces is not None:
            low = after(jnp.concatenate(pieces, axis=0), selfs[-1])
        pieces = [low] + [swap(low, "inner", m) for m in masks]
        selfs.append(self_call(after(lo, low), after(hi, low), w, t, *span))
    pieces = [after(p, selfs[-1]) for p in pieces]

    both = ("outer", "inner")
    left = lax.ppermute(after(hi, low), both, [(i, i + 1) for i in range(devices - 1)])
    right = lax.ppermute(after(lo, low), both, [(i + 1, i) for i in range(devices - 1)])

    scale = 1.0 / (ev_dev * group_devs) ** 0.5
    term, low, low_w = term_call(scale, me, skel_high, pieces, lo, hi, w)
    terms = lax.all_gather(term, both, axis=0, tiled=True)
    far = low_call(far_list, me, low, low_w, t)
    near_scale = 16.0 / (LEAF * NEAR) ** 0.5
    low_scale = 128.0 / (far_count * RANK) ** 0.5
    ratio = (far_count / group_count) ** 0.5
    part = near_call(
        (near_scale, low_scale), near_list, near_count, first, lo, hi, left, right, w, t, far, selfs
    )
    group = lax.axis_index("outer").astype(jnp.int32).reshape(1)
    return high_call(low_scale, ratio, group_count, group, after(terms, part), t, part)


def solution(mesh):
    return jax.shard_map(
        per_device,
        mesh=mesh,
        in_specs=(
            P(None, ("outer", "inner")),
            P(None, ("outer", "inner")),
            P(("outer", "inner"), None),
            P(("outer", "inner"), None),
            P(("outer", "inner")),
            P(("outer", "inner"), None),
            P(("outer", "inner"), None),
            P("outer", None),
        ),
        out_specs=P(None, ("outer", "inner")),
        check_vma=False,
    )
```

```python
import functools

import jax
import jax.numpy as jnp
from jax import lax
from jax.experimental import pallas as pl
from jax.experimental.pallas import tpu as pltpu
from jax.sharding import PartitionSpec as P

LEAF = 512
RANK = 128
NEAR = 32
LEAF_DEV = 16
COLS = 64
FEAT = 16
LANES = 128
REACH = 8
LOW_ROUNDS = ((1,), (2,), (4,), (8, 16, 24))
SELF_SPANS = (None, (0, 4), (4, 4), (8, 8))
SUM_ROUNDS = ((1, None), (2, (0, 2)), (4, (2, 2)), (8, (4, 2)), (16, (6, 2)))
UP_SPANS = ((8, 4), (12, 4))
NT = (((1,), (1,)), ((), ()))
NN = (((1,), (0,)), ((), ()))
VMEM_LIMIT = 60 << 20
SMALL_LIMIT = 24 << 20

X0 = COLS
N0 = X0 + FEAT
O0 = N0 + 3


def dot(a, b, dims=NN):
    return lax.dot_general(a, b, dims, preferred_element_type=jnp.float32)


def target_map():
    k = lax.broadcasted_iota(jnp.int32, (LANES, LANES), 0)
    m = lax.broadcasted_iota(jnp.int32, (LANES, LANES), 1)
    quarter = (k == m) & (k >= X0) & (k < N0)
    ones = (k == m + 3) & (m >= N0) & (m < O0)
    pieces = (k + 3 == m) & (k >= N0) & (k < O0)
    return jnp.where(quarter, 0.25, jnp.where(ones | pieces, 1.0, 0.0)).astype(jnp.bfloat16)


def targets(rows):
    return dot(rows, target_map()).astype(jnp.bfloat16)


def weight_map():
    k = lax.broadcasted_iota(jnp.int32, (COLS, LANES), 0)
    m = lax.broadcasted_iota(jnp.int32, (COLS, LANES), 1)
    return jnp.where(k == m, 1.0, 0.0).astype(jnp.bfloat16)


def weights(rows):
    return dot(weight_map(), rows, NT).astype(jnp.bfloat16)


def block(i, size):
    return pl.ds(pl.multiple_of(i * size, size), size)


def cost(pairs):
    return pl.CostEstimate(
        flops=pairs * 2 * LEAF * LEAF * 384, bytes_accessed=4 << 20, transcendentals=pairs * LEAF * LEAF
    )


def features(xb):
    x = xb.astype(jnp.float32)
    n = jnp.sum(x * x, axis=0, keepdims=True) * -0.125
    n1 = n.astype(jnp.bfloat16).astype(jnp.float32)
    n2 = (n - n1).astype(jnp.bfloat16).astype(jnp.float32)
    n3 = (n - n1 - n2).astype(jnp.bfloat16).astype(jnp.float32)
    r = lax.broadcasted_iota(jnp.int32, xb.shape, 0)
    one = jnp.where(r < 6, 1.0, 0.0)
    ext = jnp.where(r == 0, n1, jnp.where(r == 1, n2, jnp.where(r == 2, n3, one)))
    pad = jnp.zeros((LANES - COLS - 2 * FEAT, xb.shape[1]), jnp.bfloat16)
    return [xb, ext.astype(jnp.bfloat16), pad]


def tree_kernel(
    perm_hbm, skel_hbm, events_hbm, coeffs_hbm, lo_hbm, hi_hbm, w_hbm, t_hbm, own_out,
    lo_out, hi_out, w_out, t_out, table, picked, spick, perm, skel, events, coeffs, sems,
):
    moves = [
        pltpu.make_async_copy(src, dst, sems.at[i])
        for i, (src, dst) in enumerate(
            [(events_hbm, events), (coeffs_hbm, coeffs), (perm_hbm, perm), (skel_hbm, skel)]
        )
    ]
    for m in moves:
        m.start()
    moves[0].wait()
    moves[1].wait()
    chunks = events.shape[1] // LEAF

    def build(c, _):
        at = block(c, LEAF)
        full = jnp.concatenate([coeffs[:, at]] + features(events[:, at]), axis=0)
        table[at, :] = full.T.astype(jnp.float32)
        return 0

    lax.fori_loop(0, chunks, build, 0)
    moves[2].wait()
    moves[3].wait()

    def fetch(ids):
        return jnp.concatenate([table[pl.ds(i, 1), :] for i in ids], axis=0)

    for j in range(0, RANK, 8):
        spick[j : j + 8, :] = fetch([perm[0, skel[0, j + u]] for u in range(8)])

    step = 64

    def gather(rows_out, base, c, _):
        def some(b, _):
            for v in range(0, step, 8):
                e = (base + c) * LEAF + b * step + v
                picked[block(b * (step // 8) + v // 8, 8), :] = fetch(
                    [perm[0, e + u] for u in range(8)]
                )
            return 0

        lax.fori_loop(0, LEAF // step, some, 0)
        at = block(base + c, LEAF)
        r = picked[...]
        rb = r.astype(jnp.bfloat16)
        rows_out[block(c, LEAF), :] = rb
        w_out[:, at] = r.T[:COLS].astype(jnp.bfloat16)
        t_out[at, :] = targets(rb)
        return 0

    half = chunks // 2
    lax.fori_loop(0, half, functools.partial(gather, lo_out, 0), 0)
    outs = [
        pltpu.make_async_copy(src, dst, sems.at[4 + i])
        for i, (src, dst) in enumerate(
            [(lo_out, lo_hbm), (hi_out, hi_hbm), (w_out, w_hbm), (t_out, t_hbm)]
        )
    ]
    outs[0].start()
    lax.fori_loop(0, half, functools.partial(gather, hi_out, half), 0)
    for m in outs[1:]:
        m.start()

    s = spick[...]
    ts = targets(s.astype(jnp.bfloat16))
    su = halves_dot(lo_out, hi_out, w_out, ts) / events.shape[1] ** 0.5
    own_out[:COLS, :] = su.astype(jnp.bfloat16)
    own_out[COLS:, :] = s.T[X0:N0].astype(jnp.bfloat16)
    for m in outs:
        m.wait()


def halves_dot(lo, hi, w, ts):
    half = lo.shape[0]
    ka = jnp.exp(dot(lo[...], ts, NT)).astype(jnp.bfloat16)
    kb = jnp.exp(dot(hi[...], ts, NT)).astype(jnp.bfloat16)
    return dot(w[:, :half], ka) + dot(w[:, half:], kb)


SMEM = pl.BlockSpec(memory_space=pltpu.SMEM)
VMEM = pl.BlockSpec(memory_space=pltpu.VMEM)
ANY = pl.BlockSpec(memory_space=pl.ANY)


def params(limit=VMEM_LIMIT):
    return pltpu.CompilerParams(vmem_limit_bytes=limit)


def tree_call(perm, skel, events, coeffs):
    n = events.shape[1]
    return pl.pallas_call(
        tree_kernel,
        out_shape=(
            jax.ShapeDtypeStruct((n // 2, LANES), jnp.bfloat16),
            jax.ShapeDtypeStruct((n // 2, LANES), jnp.bfloat16),
            jax.ShapeDtypeStruct((COLS, n), jnp.bfloat16),
            jax.ShapeDtypeStruct((n, LANES), jnp.bfloat16),
            jax.ShapeDtypeStruct((COLS + FEAT, RANK), jnp.bfloat16),
        ),
        in_specs=[ANY] * 4,
        out_specs=(ANY,) * 4 + (VMEM,),
        scratch_shapes=[
            pltpu.VMEM((n // 2, LANES), jnp.bfloat16),
            pltpu.VMEM((n // 2, LANES), jnp.bfloat16),
            pltpu.VMEM((COLS, n), jnp.bfloat16),
            pltpu.VMEM((n, LANES), jnp.bfloat16),
            pltpu.VMEM((n, LANES), jnp.float32),
            pltpu.VMEM((LEAF, LANES), jnp.float32),
            pltpu.VMEM((RANK, LANES), jnp.float32),
            pltpu.SMEM(perm.shape, jnp.int32),
            pltpu.SMEM(skel.shape, jnp.int32),
            pltpu.VMEM(events.shape, jnp.bfloat16),
            pltpu.VMEM(coeffs.shape, jnp.bfloat16),
            pltpu.SemaphoreType.DMA((8,)),
        ],
        compiler_params=params(),
        name="tree_rows",
    )(perm, skel, events, coeffs)


def self_kernel(rows, w, t, part):
    ks = []
    for leaf in range(part.shape[0]):
        at = slice(leaf * LEAF, (leaf + 1) * LEAF)
        ks.append((at, jnp.exp(dot(rows[at, :], t[at, :], NT)).astype(jnp.bfloat16)))
    for leaf, (at, k) in enumerate(ks):
        part[leaf] = dot(w[:, at], k)


def self_call(lo, hi, w, t, first, leaves):
    each = 2
    size = each * LEAF
    spot = first // each
    half = LEAF_DEV // 2
    rows, row_spot = (lo, spot) if first < half else (hi, (first - half) // each)
    return pl.pallas_call(
        self_kernel,
        out_shape=jax.ShapeDtypeStruct((leaves, COLS, LEAF), jnp.float32),
        grid=(leaves // each,),
        in_specs=[
            pl.BlockSpec((size, LANES), lambda i: (row_spot + i, 0)),
            pl.BlockSpec((COLS, size), lambda i: (0, spot + i)),
            pl.BlockSpec((size, LANES), lambda i: (spot + i, 0)),
        ],
        out_specs=pl.BlockSpec((each, COLS, LEAF), lambda i: (i, 0, 0)),
        compiler_params=params(),
        cost_estimate=cost(leaves),
        name="near_self",
    )(rows, w, t)


def event_rows(xb):
    none = jnp.zeros((COLS, xb.shape[1]), jnp.bfloat16)
    return jnp.concatenate([none] + features(xb), axis=0).T


def term_kernel(parts, me, picks, *refs):
    pieces, refs = refs[:parts], refs[parts:]
    sources, (term_out, hx_out, low_out, low_w, low_x, lo, hi, w, sems) = refs[:3], refs[3:]
    moves = [
        pltpu.make_async_copy(src, dst, sems.at[i])
        for i, (src, dst) in enumerate(zip(sources, (lo, hi, w)))
    ]
    for m in moves:
        m.start()
    each = COLS + FEAT
    blocks = pieces[0].shape[0] // each
    size = blocks * RANK
    for i, piece in enumerate(pieces):
        for b in range(blocks):
            at = slice((i * blocks + b) * RANK, (i * blocks + b + 1) * RANK)
            low_w[:, at] = piece[b * each : b * each + COLS, :]
            low_x[:, at] = piece[b * each + COLS : (b + 1) * each, :]
        at = slice(i * size, (i + 1) * size)
        low_out[at, :] = event_rows(low_x[:, at])
    p = picks[...]
    p = ((p // RANK) ^ me[0]) * RANK + p % RANK
    hit = lax.broadcasted_iota(jnp.int32, (parts * size, RANK), 0) == p
    hx = dot(low_x[...], jnp.where(hit, 1.0, 0.0).astype(jnp.bfloat16)).astype(jnp.bfloat16)
    hx_out[...] = hx
    for m in moves:
        m.wait()
    term_out[...] = halves_dot(lo, hi, w, targets(event_rows(hx)))


def term_call(me, picks, pieces, lo, hi, w):
    total = len(pieces) * pieces[0].shape[0] // (COLS + FEAT) * RANK
    return pl.pallas_call(
        lambda *refs: term_kernel(len(pieces), *refs),
        out_shape=(
            jax.ShapeDtypeStruct((COLS, RANK), jnp.float32),
            jax.ShapeDtypeStruct((FEAT, RANK), jnp.bfloat16),
            jax.ShapeDtypeStruct((total, LANES), jnp.bfloat16),
            jax.ShapeDtypeStruct((COLS, total), jnp.bfloat16),
        ),
        in_specs=[SMEM] + [VMEM] * (1 + len(pieces)) + [ANY] * 3,
        out_specs=(VMEM,) * 4,
        scratch_shapes=[
            pltpu.VMEM((FEAT, total), jnp.bfloat16),
            pltpu.VMEM(lo.shape, jnp.bfloat16),
            pltpu.VMEM(hi.shape, jnp.bfloat16),
            pltpu.VMEM(w.shape, jnp.bfloat16),
            pltpu.SemaphoreType.DMA((3,)),
        ],
        compiler_params=params(),
        cost_estimate=cost(4),
        name="high_term",
    )(me, picks, *pieces, lo, hi, w)


def low_kernel(first, far, me, low, low_w, t, part):
    groups = far.shape[1] // 4
    leaves = part.shape[0]
    ks = []
    for j in range(leaves):
        leaf = first + pl.program_id(0) * leaves + j
        tl = t[j * LEAF : (j + 1) * LEAF, :]
        for g in range(groups):
            spots = [block(far[leaf, 4 * g + i] ^ me[0], RANK) for i in range(4)]
            r = jnp.concatenate([low[s, :] for s in spots], axis=0)
            ks.append((spots, jnp.exp(dot(r, tl, NT)).astype(jnp.bfloat16)))
    for j in range(leaves):
        total = None
        for spots, k in ks[j * groups : (j + 1) * groups]:
            p = dot(jnp.concatenate([low_w[:, s] for s in spots], axis=1), k)
            total = p if total is None else total + p
        part[j] = total


def low_call(far, me, low, low_w, t, first, leaves):
    each = 2
    spot = first // each
    return pl.pallas_call(
        lambda *refs: low_kernel(first, *refs),
        out_shape=jax.ShapeDtypeStruct((leaves, COLS, LEAF), jnp.float32),
        grid=(leaves // each,),
        in_specs=[
            SMEM,
            SMEM,
            pl.BlockSpec(low.shape, lambda i: (0, 0)),
            pl.BlockSpec(low_w.shape, lambda i: (0, 0)),
            pl.BlockSpec((each * LEAF, LANES), lambda i: (spot + i, 0)),
        ],
        out_specs=pl.BlockSpec((each, COLS, LEAF), lambda i: (i, 0, 0)),
        compiler_params=params(SMALL_LIMIT),
        cost_estimate=cost(4 * leaves),
        name="far_low",
    )(far, me, low, low_w, t)


def near_kernel(scales, n_self, n_up, near, count, first, lo, hi, left, right, w_own, t_hbm, *refs):
    near_scale, low_scale = scales
    ups, refs = refs[:n_up], refs[n_up:]
    parts, (out, rows, w, t, low, acc, pairs, sems) = refs[:-8], refs[-8:]
    selfs, lows = parts[:n_self], parts[n_self:]
    side = REACH * LEAF
    own = LEAF_DEV * LEAF
    moves = [
        pltpu.make_async_copy(left, rows.at[pl.ds(0, side), :], sems.at[0]),
        pltpu.make_async_copy(right, rows.at[pl.ds(side + own, side), :], sems.at[1]),
        pltpu.make_async_copy(lo, rows.at[pl.ds(side, own // 2), :], sems.at[2]),
        pltpu.make_async_copy(hi, rows.at[pl.ds(side + own // 2, own // 2), :], sems.at[3]),
        pltpu.make_async_copy(w_own, w.at[:, pl.ds(side, own)], sems.at[4]),
        pltpu.make_async_copy(t_hbm, t, sems.at[5]),
    ]
    leaf = 0
    for part in selfs:
        there = acc.at[pl.ds(leaf, part.shape[0])]
        moves.append(pltpu.make_async_copy(part, there, sems.at[len(moves)]))
        leaf += part.shape[0]
    low_moves = []
    leaf = 0
    for part in lows:
        there = low.at[pl.ds(leaf, part.shape[0])]
        sem = sems.at[len(moves) + len(low_moves)]
        low_moves.append(pltpu.make_async_copy(part, there, sem))
        leaf += part.shape[0]
    for m in moves + low_moves:
        m.start()

    def leaf_slots(leaf, n):
        def slot(s, n):
            pairs[n] = leaf * 64 + (near[leaf, s] - first[0] + REACH)
            return n + 1

        return lax.fori_loop(1, count[leaf], slot, n)

    n = lax.fori_loop(0, LEAF_DEV, leaf_slots, jnp.int32(0))
    for u in range(8):
        pairs[n + u] = LEAF_DEV * 64

    acc[LEAF_DEV] = jnp.zeros((COLS, LEAF), jnp.float32)
    moves[0].wait()
    moves[1].wait()

    def flip(b, _):
        at = block(b, LEAF)
        there = block(b + REACH + LEAF_DEV, LEAF)
        w[:, at] = weights(rows[at, :])
        w[:, there] = weights(rows[there, :])
        return 0

    lax.fori_loop(0, REACH, flip, 0)
    for m in moves[2:]:
        m.wait()

    def step(begin, many):
        ks = []
        for u in range(many):
            e = pairs[begin + u]
            leaf, at = e // 64, e % 64
            tl = t[block(jnp.minimum(leaf, LEAF_DEV - 1), LEAF), :]
            k = jnp.exp(dot(rows[block(at, LEAF), :], tl, NT)).astype(jnp.bfloat16)
            ks.append((leaf, at, k))
        for leaf, at, k in ks:
            acc[leaf] = acc[leaf] + dot(w[:, block(at, LEAF)], k)

    def eight(s, _):
        step(s * 8, 8)
        return 0

    lax.fori_loop(0, n // 8, eight, 0)

    def four(s, _):
        step(n // 8 * 8 + s * 4, 4)
        return 0

    lax.fori_loop(0, (n % 8 + 3) // 4, four, 0)

    for m in low_moves:
        m.wait()
    each = COLS + FEAT
    starts = [(u, i) for u in ups for i in range(0, u.shape[0], each)]
    high_w = jnp.concatenate([u[i : i + COLS, :] for u, i in starts], axis=1)
    xs = [u[i + COLS : i + each, :] for u, i in starts]
    high_x = event_rows(jnp.concatenate(xs, axis=1))
    many = 8
    for begin in range(0, LEAF_DEV, many):
        leaves = [(leaf, slice(leaf * LEAF, (leaf + 1) * LEAF)) for leaf in range(begin, begin + many)]
        ks = [jnp.exp(dot(high_x, t[at, :], NT)).astype(jnp.bfloat16) for _, at in leaves]
        for (leaf, at), k in zip(leaves, ks):
            far = low[leaf] + dot(high_w, k)
            out[:, at] = (acc[leaf] * near_scale + far * low_scale).astype(jnp.bfloat16)


def near_call(scales, near, count, first, lo, hi, left, right, w, t, ups, selfs, lows):
    n = (LEAF_DEV + 2 * REACH) * LEAF
    copies = 6 + len(selfs) + len(lows)
    return pl.pallas_call(
        lambda *refs: near_kernel(scales, len(selfs), len(ups), *refs),
        out_shape=jax.ShapeDtypeStruct((COLS, LEAF_DEV * LEAF), jnp.bfloat16),
        in_specs=[SMEM] * 3 + [ANY] * 6 + [VMEM] * len(ups) + [ANY] * (len(selfs) + len(lows)),
        out_specs=VMEM,
        scratch_shapes=[
            pltpu.VMEM((n, LANES), jnp.bfloat16),
            pltpu.VMEM((COLS, n), jnp.bfloat16),
            pltpu.VMEM(t.shape, jnp.bfloat16),
            pltpu.VMEM((LEAF_DEV, COLS, LEAF), jnp.float32),
            pltpu.VMEM((LEAF_DEV + 1, COLS, LEAF), jnp.float32),
            pltpu.SMEM((LEAF_DEV * NEAR + 8,), jnp.int32),
            pltpu.SemaphoreType.DMA((copies,)),
        ],
        compiler_params=params(),
        cost_estimate=cost(150),
        name="near_out",
    )(near, count, first, lo, hi, left, right, w, t, *ups, *selfs, *lows)


def swap(x, axis, mask):
    count = lax.axis_size(axis)
    return lax.ppermute(x, axis, [(i, i ^ mask) for i in range(count)])


def after(x, *others):
    return lax.optimization_barrier((x, *others))[0]


def per_device(events, coeffs, tree_perm, near_list, near_count, far_list, skel_low, skel_high):
    group_devs = lax.axis_size("inner")
    group_count = lax.axis_size("outer")
    far_count = far_list.shape[1]
    ev_dev = events.shape[1]
    inner = lax.axis_index("inner").astype(jnp.int32)
    device = lax.axis_index("outer").astype(jnp.int32) * group_devs + inner
    devices = group_devs * group_count
    first = (device * LEAF_DEV).reshape(1)
    me = inner.reshape(1)
    lo, hi, w, t, own = tree_call(tree_perm, skel_low, events, coeffs)

    low = own
    selfs = []
    pieces = None
    for masks, span in zip(LOW_ROUNDS, SELF_SPANS):
        if pieces is not None:
            low = after(jnp.concatenate(pieces, axis=0), *selfs[-1:])
        pieces = [low] + [swap(low, "inner", m) for m in masks]
        if span is not None:
            selfs.append(self_call(after(lo, low), after(hi, low), w, t, *span))
    pieces = [after(p, selfs[-1]) for p in pieces]

    term, hx, low, low_w = term_call(me, skel_high, pieces, lo, hi, w)
    lows = []
    for mask, span in SUM_ROUNDS:
        moved = swap(term, "inner", mask)
        if span is not None:
            lows.append(low_call(far_list, me, after(low, term), low_w, t, *span))
        term = after(term + moved, *lows[-1:])
    hu = (term * (1.0 / (ev_dev * group_devs) ** 0.5)).astype(jnp.bfloat16)
    ratio = (far_count / group_count) ** 0.5
    upper = jnp.concatenate([hu * jnp.bfloat16(ratio), hx], axis=0)
    up = swap(upper, "outer", 1)
    both = ("outer", "inner")
    left = lax.ppermute(after(hi, upper), both, [(i, i + 1) for i in range(devices - 1)])
    right = lax.ppermute(after(lo, upper), both, [(i + 1, i) for i in range(devices - 1)])
    lows.append(low_call(far_list, me, after(low, upper), low_w, t, *UP_SPANS[0]))
    up = after(up, lows[-1])
    upper = jnp.concatenate([upper, up], axis=0)
    ups = [up, swap(upper, "outer", 2)]
    lows.append(low_call(far_list, me, after(low, upper), low_w, t, *UP_SPANS[1]))
    ups = [after(u, lows[-1]) for u in ups]

    near_scale = 16.0 / (LEAF * NEAR) ** 0.5
    low_scale = 128.0 / (far_count * RANK) ** 0.5
    scales = (near_scale, low_scale)
    return near_call(
        scales, near_list, near_count, first, lo, hi, left, right, w, t, ups, selfs, lows
    )


def solution(mesh):
    return jax.shard_map(
        per_device,
        mesh=mesh,
        in_specs=(
            P(None, ("outer", "inner")),
            P(None, ("outer", "inner")),
            P(("outer", "inner"), None),
            P(("outer", "inner"), None),
            P(("outer", "inner")),
            P(("outer", "inner"), None),
            P(("outer", "inner"), None),
            P("outer", None),
        ),
        out_specs=P(None, ("outer", "inner")),
        check_vma=False,
    )
```

```python
import functools

import jax
import jax.numpy as jnp
from jax import lax
from jax.experimental import pallas as pl
from jax.experimental.pallas import tpu as pltpu
from jax.sharding import PartitionSpec as P

LEAF = 512
RANK = 128
NEAR = 32
LEAF_DEV = 16
COLS = 64
FEAT = 16
LANES = 128
REACH = 8
NT = (((1,), (1,)), ((), ()))
NN = (((1,), (0,)), ((), ()))
VMEM_LIMIT = 60 << 20

X0 = COLS
N0 = X0 + FEAT
O0 = N0 + 3


def dot(a, b, dims=NN):
    return lax.dot_general(a, b, dims, preferred_element_type=jnp.float32)


def target_map():
    k = lax.broadcasted_iota(jnp.int32, (LANES, LANES), 0)
    m = lax.broadcasted_iota(jnp.int32, (LANES, LANES), 1)
    quarter = (k == m) & (k >= X0) & (k < N0)
    ones = (k == m + 3) & (m >= N0) & (m < O0)
    pieces = (k + 3 == m) & (k >= N0) & (k < O0)
    return jnp.where(quarter, 0.25, jnp.where(ones | pieces, 1.0, 0.0)).astype(jnp.bfloat16)


def targets(rows):
    return dot(rows, target_map()).astype(jnp.bfloat16)


def weight_map():
    k = lax.broadcasted_iota(jnp.int32, (COLS, LANES), 0)
    m = lax.broadcasted_iota(jnp.int32, (COLS, LANES), 1)
    return jnp.where(k == m, 1.0, 0.0).astype(jnp.bfloat16)


def weights(rows):
    return dot(weight_map(), rows, NT).astype(jnp.bfloat16)


def block(i, size):
    return pl.ds(pl.multiple_of(i * size, size), size)


def cost(pairs):
    return pl.CostEstimate(
        flops=pairs * 2 * LEAF * LEAF * 384, bytes_accessed=4 << 20, transcendentals=pairs * LEAF * LEAF
    )


def features(xb):
    x = xb.astype(jnp.float32)
    n = jnp.sum(x * x, axis=0, keepdims=True) * -0.125
    n1 = n.astype(jnp.bfloat16).astype(jnp.float32)
    n2 = (n - n1).astype(jnp.bfloat16).astype(jnp.float32)
    n3 = (n - n1 - n2).astype(jnp.bfloat16).astype(jnp.float32)
    r = lax.broadcasted_iota(jnp.int32, xb.shape, 0)
    one = jnp.where(r < 6, 1.0, 0.0)
    ext = jnp.where(r == 0, n1, jnp.where(r == 1, n2, jnp.where(r == 2, n3, one)))
    pad = jnp.zeros((LANES - COLS - 2 * FEAT, xb.shape[1]), jnp.bfloat16)
    return [xb, ext.astype(jnp.bfloat16), pad]


def event_table(events, coeffs, store):
    def build(c, _):
        at = block(c, LEAF)
        full = jnp.concatenate([coeffs[:, at]] + features(events[:, at]), axis=0)
        store(at, full.T)
        return 0

    lax.fori_loop(0, events.shape[1] // LEAF, build, 0)


def fetch(table, ids):
    return jnp.concatenate([table[pl.ds(i, 1), :] for i in ids], axis=0)


def start_copies(pairs, sems):
    moves = [pltpu.make_async_copy(src, dst, sems.at[i]) for i, (src, dst) in enumerate(pairs)]
    for m in moves:
        m.start()
    return moves


def own_kernel(
    perm_hbm, skel_hbm, events_hbm, coeffs_hbm, own_out,
    table, rows, spick, perm, skel, events, coeffs, sems,
):
    moves = start_copies(
        [(events_hbm, events), (coeffs_hbm, coeffs), (perm_hbm, perm), (skel_hbm, skel)], sems
    )
    moves[0].wait()
    moves[1].wait()

    def store(at, full):
        rows[at, :] = full
        table[at, :] = full.astype(jnp.float32)

    event_table(events, coeffs, store)
    moves[2].wait()
    moves[3].wait()
    for j in range(0, RANK, 8):
        spick[j : j + 8, :] = fetch(table, [perm[0, skel[0, j + u]] for u in range(8)])
    s = spick[...]
    k = jnp.exp(dot(rows[...], targets(s.astype(jnp.bfloat16)), NT)).astype(jnp.bfloat16)
    su = dot(coeffs[...], k) / events.shape[1] ** 0.5
    own_out[:COLS, :] = su.astype(jnp.bfloat16)
    own_out[COLS : COLS + FEAT, :] = s.T[X0:N0].astype(jnp.bfloat16)
    own_out[COLS + FEAT :, :] = jnp.zeros((LANES - COLS - FEAT, RANK), jnp.bfloat16)


def tree_kernel(
    perm_hbm, events_hbm, coeffs_hbm, lo_hbm, hi_hbm, w_hbm, t_hbm,
    lo_out, hi_out, w_out, t_out, table, picked, perm, events, coeffs, sems,
):
    moves = start_copies([(events_hbm, events), (coeffs_hbm, coeffs), (perm_hbm, perm)], sems)
    moves[0].wait()
    moves[1].wait()

    def store(at, full):
        table[at, :] = full.astype(jnp.float32)

    event_table(events, coeffs, store)
    moves[2].wait()
    step = 64

    def gather(rows_out, base, c, _):
        def some(b, _):
            for v in range(0, step, 8):
                e = (base + c) * LEAF + b * step + v
                picked[block(b * (step // 8) + v // 8, 8), :] = fetch(
                    table, [perm[0, e + u] for u in range(8)]
                )
            return 0

        lax.fori_loop(0, LEAF // step, some, 0)
        at = block(base + c, LEAF)
        r = picked[...]
        rb = r.astype(jnp.bfloat16)
        rows_out[block(c, LEAF), :] = rb
        w_out[:, at] = r.T[:COLS].astype(jnp.bfloat16)
        t_out[at, :] = targets(rb)
        return 0

    half = events.shape[1] // LEAF // 2
    lax.fori_loop(0, half, functools.partial(gather, lo_out, 0), 0)
    outs = [
        pltpu.make_async_copy(src, dst, sems.at[3 + i])
        for i, (src, dst) in enumerate(
            [(lo_out, lo_hbm), (hi_out, hi_hbm), (w_out, w_hbm), (t_out, t_hbm)]
        )
    ]
    outs[0].start()
    lax.fori_loop(0, half, functools.partial(gather, hi_out, half), 0)
    for m in outs[1:]:
        m.start()
    for m in outs:
        m.wait()


def halves_dot(lo, hi, w, ts):
    half = lo.shape[0]
    ka = jnp.exp(dot(lo[...], ts, NT)).astype(jnp.bfloat16)
    kb = jnp.exp(dot(hi[...], ts, NT)).astype(jnp.bfloat16)
    return dot(w[:, :half], ka) + dot(w[:, half:], kb)


SMEM = pl.BlockSpec(memory_space=pltpu.SMEM)
VMEM = pl.BlockSpec(memory_space=pltpu.VMEM)
ANY = pl.BlockSpec(memory_space=pl.ANY)


def params(limit=VMEM_LIMIT):
    return pltpu.CompilerParams(vmem_limit_bytes=limit)


def own_call(perm, skel, events, coeffs):
    n = events.shape[1]
    return pl.pallas_call(
        own_kernel,
        out_shape=jax.ShapeDtypeStruct((LANES, RANK), jnp.bfloat16),
        in_specs=[ANY] * 4,
        out_specs=VMEM,
        scratch_shapes=[
            pltpu.VMEM((n, LANES), jnp.float32),
            pltpu.VMEM((n, LANES), jnp.bfloat16),
            pltpu.VMEM((RANK, LANES), jnp.float32),
            pltpu.SMEM(perm.shape, jnp.int32),
            pltpu.SMEM(skel.shape, jnp.int32),
            pltpu.VMEM(events.shape, jnp.bfloat16),
            pltpu.VMEM(coeffs.shape, jnp.bfloat16),
            pltpu.SemaphoreType.DMA((4,)),
        ],
        compiler_params=params(),
        cost_estimate=cost(4),
        name="own_skeleton",
    )(perm, skel, events, coeffs)


def tree_call(perm, events, coeffs):
    n = events.shape[1]
    shapes = ((n // 2, LANES), (n // 2, LANES), (COLS, n), (n, LANES))
    return pl.pallas_call(
        tree_kernel,
        out_shape=tuple(jax.ShapeDtypeStruct(s, jnp.bfloat16) for s in shapes),
        in_specs=[ANY] * 3,
        out_specs=(ANY,) * 4,
        scratch_shapes=[pltpu.VMEM(s, jnp.bfloat16) for s in shapes]
        + [
            pltpu.VMEM((n, LANES), jnp.float32),
            pltpu.VMEM((LEAF, LANES), jnp.float32),
            pltpu.SMEM(perm.shape, jnp.int32),
            pltpu.VMEM(events.shape, jnp.bfloat16),
            pltpu.VMEM(coeffs.shape, jnp.bfloat16),
            pltpu.SemaphoreType.DMA((7,)),
        ],
        compiler_params=params(),
        cost_estimate=cost(40),
        name="tree_rows",
    )(perm, events, coeffs)


def event_rows(xb):
    none = jnp.zeros((COLS, xb.shape[1]), jnp.bfloat16)
    return jnp.concatenate([none] + features(xb), axis=0).T


def term_kernel(picks, low_all, lo_hbm, hi_hbm, w_hbm, term_out, hx_out, low_out, low_w, low_x, lo, hi, w, sems):
    moves = start_copies([(lo_hbm, lo), (hi_hbm, hi), (w_hbm, w)], sems)
    nodes = low_all.shape[0] // LANES
    for b in range(nodes):
        at = slice(b * RANK, (b + 1) * RANK)
        low_w[:, at] = low_all[b * LANES : b * LANES + COLS, :]
        low_x[:, at] = low_all[b * LANES + COLS : b * LANES + COLS + FEAT, :]
    low_out[...] = event_rows(low_x[...])
    hit = lax.broadcasted_iota(jnp.int32, (nodes * RANK, RANK), 0) == picks[...]
    hx = dot(low_x[...], jnp.where(hit, 1.0, 0.0).astype(jnp.bfloat16)).astype(jnp.bfloat16)
    hx_out[...] = hx
    for m in moves:
        m.wait()
    term_out[...] = halves_dot(lo, hi, w, targets(event_rows(hx)))


def term_call(picks, low_all, lo, hi, w):
    total = low_all.shape[0] // LANES * RANK
    return pl.pallas_call(
        term_kernel,
        out_shape=(
            jax.ShapeDtypeStruct((COLS, RANK), jnp.float32),
            jax.ShapeDtypeStruct((FEAT, RANK), jnp.bfloat16),
            jax.ShapeDtypeStruct((total, LANES), jnp.bfloat16),
            jax.ShapeDtypeStruct((COLS, total), jnp.bfloat16),
        ),
        in_specs=[VMEM] * 2 + [ANY] * 3,
        out_specs=(VMEM,) * 4,
        scratch_shapes=[
            pltpu.VMEM((FEAT, total), jnp.bfloat16),
            pltpu.VMEM(lo.shape, jnp.bfloat16),
            pltpu.VMEM(hi.shape, jnp.bfloat16),
            pltpu.VMEM(w.shape, jnp.bfloat16),
            pltpu.SemaphoreType.DMA((3,)),
        ],
        compiler_params=params(),
        cost_estimate=cost(4),
        name="high_term",
    )(picks, low_all, lo, hi, w)


def low_kernel(far, low, low_w, t, part):
    groups = far.shape[1] // 4
    leaves = part.shape[0]
    ks = []
    for j in range(leaves):
        leaf = pl.program_id(0) * leaves + j
        tl = t[j * LEAF : (j + 1) * LEAF, :]
        for g in range(groups):
            spots = [block(far[leaf, 4 * g + i], RANK) for i in range(4)]
            r = jnp.concatenate([low[s, :] for s in spots], axis=0)
            ks.append((spots, jnp.exp(dot(r, tl, NT)).astype(jnp.bfloat16)))
    for j in range(leaves):
        total = None
        for spots, k in ks[j * groups : (j + 1) * groups]:
            p = dot(jnp.concatenate([low_w[:, s] for s in spots], axis=1), k)
            total = p if total is None else total + p
        part[j] = total


def low_call(far, low, low_w, t):
    each = 2
    return pl.pallas_call(
        low_kernel,
        out_shape=jax.ShapeDtypeStruct((LEAF_DEV, COLS, LEAF), jnp.float32),
        grid=(LEAF_DEV // each,),
        in_specs=[
            SMEM,
            pl.BlockSpec(low.shape, lambda i: (0, 0)),
            pl.BlockSpec(low_w.shape, lambda i: (0, 0)),
            pl.BlockSpec((each * LEAF, LANES), lambda i: (i, 0)),
        ],
        out_specs=pl.BlockSpec((each, COLS, LEAF), lambda i: (i, 0, 0)),
        compiler_params=params(),
        cost_estimate=cost(64),
        name="far_low",
    )(far, low, low_w, t)


def pair_list(near, count, first, pairs, place):
    def leaf_slots(leaf, n):
        def slot(s, n):
            at, takes = place(near[leaf, s] - first[0])
            pairs[n] = leaf * 64 + at
            return n + jnp.where(takes, 1, 0)

        return lax.fori_loop(0, count[leaf], slot, n)

    n = lax.fori_loop(0, LEAF_DEV, leaf_slots, jnp.int32(0))
    for u in range(8):
        pairs[n + u] = LEAF_DEV * 64
    return n


def pair_sums(n, pairs, rows, w, t, acc):
    def step(begin, many):
        ks = []
        for u in range(many):
            e = pairs[begin + u]
            leaf, at = e // 64, e % 64
            tl = t[block(jnp.minimum(leaf, LEAF_DEV - 1), LEAF), :]
            k = jnp.exp(dot(rows[block(at, LEAF), :], tl, NT)).astype(jnp.bfloat16)
            ks.append((leaf, at, k))
        for leaf, at, k in ks:
            acc[leaf] = acc[leaf] + dot(w[:, block(at, LEAF)], k)

    def eight(s, _):
        step(s * 8, 8)
        return 0

    lax.fori_loop(0, n // 8, eight, 0)

    def four(s, _):
        step(n // 8 * 8 + s * 4, 4)
        return 0

    lax.fori_loop(0, (n % 8 + 3) // 4, four, 0)


def near_own_kernel(near, count, first, lo, hi, w_hbm, t_hbm, acc, rows, w, t, pairs, sems):
    half = lo.shape[0]
    moves = start_copies(
        [
            (lo, rows.at[pl.ds(0, half), :]),
            (hi, rows.at[pl.ds(half, half), :]),
            (w_hbm, w),
            (t_hbm, t),
        ],
        sems,
    )
    n = pair_list(near, count, first, pairs, lambda at: (at, (at >= 0) & (at < LEAF_DEV)))
    acc[...] = jnp.zeros_like(acc)
    for m in moves:
        m.wait()
    pair_sums(n, pairs, rows, w, t, acc)


def near_own_call(near, count, first, lo, hi, w, t):
    return pl.pallas_call(
        near_own_kernel,
        out_shape=jax.ShapeDtypeStruct((LEAF_DEV + 1, COLS, LEAF), jnp.float32),
        in_specs=[SMEM] * 3 + [ANY] * 4,
        out_specs=VMEM,
        scratch_shapes=[
            pltpu.VMEM(t.shape, jnp.bfloat16),
            pltpu.VMEM(w.shape, jnp.bfloat16),
            pltpu.VMEM(t.shape, jnp.bfloat16),
            pltpu.SMEM((LEAF_DEV * NEAR + 8,), jnp.int32),
            pltpu.SemaphoreType.DMA((4,)),
        ],
        compiler_params=params(),
        cost_estimate=cost(60),
        name="near_own",
    )(near, count, first, lo, hi, w, t)


def near_side_kernel(
    scales, near, count, first, left, right, t_hbm, acc_hbm, low_hbm, out, rows, w, t, acc, low, pairs, sems
):
    near_scale, low_scale = scales
    side = REACH * LEAF
    moves = start_copies(
        [
            (left, rows.at[pl.ds(0, side), :]),
            (right, rows.at[pl.ds(side, side), :]),
            (t_hbm, t),
            (acc_hbm, acc),
            (low_hbm, low),
        ],
        sems,
    )
    n = pair_list(
        near, count, first, pairs,
        lambda at: (jnp.where(at < 0, at + REACH, at - REACH), (at < 0) | (at >= LEAF_DEV)),
    )
    moves[0].wait()
    moves[1].wait()

    def flip(b, _):
        for at in (block(b, LEAF), block(b + REACH, LEAF)):
            w[:, at] = weights(rows[at, :])
        return 0

    lax.fori_loop(0, REACH, flip, 0)
    for m in moves[2:]:
        m.wait()
    pair_sums(n, pairs, rows, w, t, acc)
    for leaf in range(LEAF_DEV):
        at = slice(leaf * LEAF, (leaf + 1) * LEAF)
        out[:, at] = acc[leaf] * near_scale + low[leaf] * low_scale


def near_side_call(scales, near, count, first, left, right, t, acc, low):
    n = 2 * REACH * LEAF
    return pl.pallas_call(
        lambda *refs: near_side_kernel(scales, *refs),
        out_shape=jax.ShapeDtypeStruct((COLS, LEAF_DEV * LEAF), jnp.float32),
        in_specs=[SMEM] * 3 + [ANY] * 5,
        out_specs=VMEM,
        scratch_shapes=[
            pltpu.VMEM((n, LANES), jnp.bfloat16),
            pltpu.VMEM((COLS, n), jnp.bfloat16),
            pltpu.VMEM(t.shape, jnp.bfloat16),
            pltpu.VMEM(acc.shape, jnp.float32),
            pltpu.VMEM(low.shape, jnp.float32),
            pltpu.SMEM((LEAF_DEV * NEAR + 8,), jnp.int32),
            pltpu.SemaphoreType.DMA((5,)),
        ],
        compiler_params=params(),
        cost_estimate=cost(50),
        name="near_sides",
    )(near, count, first, left, right, t, acc, low)


def upper_kernel(scale, ratio, terms, hx, upper):
    total = terms[:COLS, :]
    for m in range(1, terms.shape[0] // COLS):
        total = total + terms[m * COLS : (m + 1) * COLS, :]
    upper[:COLS, :] = (total * scale).astype(jnp.bfloat16) * jnp.bfloat16(ratio)
    upper[COLS:, :] = hx[...]


def upper_call(scale, ratio, terms, hx):
    return pl.pallas_call(
        lambda *refs: upper_kernel(scale, ratio, *refs),
        out_shape=jax.ShapeDtypeStruct((COLS + FEAT, RANK), jnp.bfloat16),
        in_specs=[VMEM] * 2,
        out_specs=VMEM,
        compiler_params=params(),
        name="high_sum",
    )(terms, hx)


def high_kernel(scale, *refs):
    *ups, t, part, out = refs
    high_w = jnp.concatenate([u[:COLS, :] for u in ups], axis=1)
    high_x = event_rows(jnp.concatenate([u[COLS:, :] for u in ups], axis=1))
    many = out.shape[1] // LEAF
    ats = [slice(j * LEAF, (j + 1) * LEAF) for j in range(many)]
    ks = [jnp.exp(dot(high_x, t[at, :], NT)).astype(jnp.bfloat16) for at in ats]
    for at, k in zip(ats, ks):
        out[:, at] = (part[:, at] + dot(high_w, k) * scale).astype(jnp.bfloat16)


def high_call(scale, ups, t, part):
    many = 4
    return pl.pallas_call(
        lambda *refs: high_kernel(scale, *refs),
        out_shape=jax.ShapeDtypeStruct(part.shape, jnp.bfloat16),
        grid=(LEAF_DEV // many,),
        in_specs=[pl.BlockSpec(u.shape, lambda i: (0, 0)) for u in ups]
        + [
            pl.BlockSpec((many * LEAF, LANES), lambda i: (i, 0)),
            pl.BlockSpec((COLS, many * LEAF), lambda i: (0, i)),
        ],
        out_specs=pl.BlockSpec((COLS, many * LEAF), lambda i: (0, i)),
        compiler_params=params(),
        cost_estimate=cost(12),
        name="high_out",
    )(*ups, t, part)


def swap(x, axis, mask):
    count = lax.axis_size(axis)
    return lax.ppermute(x, axis, [(i, i ^ mask) for i in range(count)])


def after(x, *others):
    return lax.optimization_barrier((x, *others))[0]


def per_device(events, coeffs, tree_perm, near_list, near_count, far_list, skel_low, skel_high):
    group_devs = lax.axis_size("inner")
    group_count = lax.axis_size("outer")
    far_count = far_list.shape[1]
    ev_dev = events.shape[1]
    inner = lax.axis_index("inner").astype(jnp.int32)
    device = lax.axis_index("outer").astype(jnp.int32) * group_devs + inner
    devices = group_devs * group_count
    first = (device * LEAF_DEV).reshape(1)
    own = own_call(tree_perm, skel_low, events, coeffs)
    low_all = lax.all_gather(own, "inner", axis=0, tiled=True)
    lo, hi, w, t = tree_call(after(tree_perm, own), events, coeffs)
    both = ("outer", "inner")
    left = lax.ppermute(hi, both, [(i, i + 1) for i in range(devices - 1)])
    right = lax.ppermute(lo, both, [(i + 1, i) for i in range(devices - 1)])
    acc = near_own_call(near_list, near_count, first, lo, hi, w, t)

    term, hx, low, low_w = term_call(skel_high, after(low_all, acc), lo, hi, w)
    terms = lax.all_gather(term, "inner", axis=0, tiled=True)
    far = low_call(far_list, after(low, term), low_w, t)
    near_scale = 16.0 / (LEAF * NEAR) ** 0.5
    low_scale = 128.0 / (far_count * RANK) ** 0.5
    scales = (near_scale, low_scale)
    part = near_side_call(scales, near_list, near_count, first, left, right, t, acc, far)

    scale = 1.0 / (ev_dev * group_devs) ** 0.5
    upper = upper_call(scale, (far_count / group_count) ** 0.5, after(terms, part), hx)
    ups = [swap(upper, "outer", m) for m in range(1, group_count)]
    return high_call(low_scale, ups, t, part)


def solution(mesh):
    return jax.shard_map(
        per_device,
        mesh=mesh,
        in_specs=(
            P(None, ("outer", "inner")),
            P(None, ("outer", "inner")),
            P(("outer", "inner"), None),
            P(("outer", "inner"), None),
            P(("outer", "inner")),
            P(("outer", "inner"), None),
            P(("outer", "inner"), None),
            P("outer", None),
        ),
        out_specs=P(None, ("outer", "inner")),
        check_vma=False,
    )
```

```python
import functools

import jax
import jax.numpy as jnp
from jax import lax
from jax.experimental import pallas as pl
from jax.experimental.pallas import tpu as pltpu
from jax.sharding import PartitionSpec as P

LEAF = 512
RANK = 128
NEAR = 32
LEAF_DEV = 16
COLS = 64
FEAT = 16
LANES = 128
REACH = 8
NT = (((1,), (1,)), ((), ()))
NN = (((1,), (0,)), ((), ()))
VMEM_LIMIT = 60 << 20

X0 = COLS
N0 = X0 + FEAT
O0 = N0 + 3


def dot(a, b, dims=NN):
    return lax.dot_general(a, b, dims, preferred_element_type=jnp.float32)


def target_map():
    k = lax.broadcasted_iota(jnp.int32, (LANES, LANES), 0)
    m = lax.broadcasted_iota(jnp.int32, (LANES, LANES), 1)
    quarter = (k == m) & (k >= X0) & (k < N0)
    ones = (k == m + 3) & (m >= N0) & (m < O0)
    pieces = (k + 3 == m) & (k >= N0) & (k < O0)
    return jnp.where(quarter, 0.25, jnp.where(ones | pieces, 1.0, 0.0)).astype(jnp.bfloat16)


def targets(rows):
    return dot(rows, target_map()).astype(jnp.bfloat16)


def weight_map():
    k = lax.broadcasted_iota(jnp.int32, (COLS, LANES), 0)
    m = lax.broadcasted_iota(jnp.int32, (COLS, LANES), 1)
    return jnp.where(k == m, 1.0, 0.0).astype(jnp.bfloat16)


def weights(rows):
    return dot(weight_map(), rows, NT).astype(jnp.bfloat16)


def block(i, size):
    return pl.ds(pl.multiple_of(i * size, size), size)


def cost(pairs):
    return pl.CostEstimate(
        flops=pairs * 2 * LEAF * LEAF * 384, bytes_accessed=4 << 20, transcendentals=pairs * LEAF * LEAF
    )


def features(xb):
    x = xb.astype(jnp.float32)
    n = jnp.sum(x * x, axis=0, keepdims=True) * -0.125
    n1 = n.astype(jnp.bfloat16).astype(jnp.float32)
    n2 = (n - n1).astype(jnp.bfloat16).astype(jnp.float32)
    n3 = (n - n1 - n2).astype(jnp.bfloat16).astype(jnp.float32)
    r = lax.broadcasted_iota(jnp.int32, xb.shape, 0)
    one = jnp.where(r < 6, 1.0, 0.0)
    ext = jnp.where(r == 0, n1, jnp.where(r == 1, n2, jnp.where(r == 2, n3, one)))
    pad = jnp.zeros((LANES - COLS - 2 * FEAT, xb.shape[1]), jnp.bfloat16)
    return [xb, ext.astype(jnp.bfloat16), pad]


QUARTERS = 4


def quarters(src, dst):
    size = src.shape[1] // QUARTERS
    return [(src.at[:, pl.ds(i * size, size)], dst.at[:, pl.ds(i * size, size)]) for i in range(QUARTERS)]


def event_table(events, coeffs, event_moves, coeff_moves, store):
    def build(c, _):
        at = block(c, LEAF)
        full = jnp.concatenate([coeffs[:, at]] + features(events[:, at]), axis=0)
        store(at, full.T)
        return 0

    each = events.shape[1] // LEAF // QUARTERS
    for i in range(QUARTERS):
        event_moves[i].wait()
        coeff_moves[i].wait()
        lax.fori_loop(i * each, (i + 1) * each, build, 0)


def fetch(table, ids):
    return jnp.concatenate([table[pl.ds(i, 1), :] for i in ids], axis=0)


def start_copies(pairs, sems):
    moves = [pltpu.make_async_copy(src, dst, sems.at[i]) for i, (src, dst) in enumerate(pairs)]
    for m in moves:
        m.start()
    return moves


def own_kernel(
    perm_hbm, skel_hbm, events_hbm, coeffs_hbm, own_out,
    table, rows, spick, perm, skel, events, coeffs, sems,
):
    moves = start_copies(
        quarters(events_hbm, events)
        + quarters(coeffs_hbm, coeffs)
        + [(perm_hbm, perm), (skel_hbm, skel)],
        sems,
    )

    def store(at, full):
        rows[at, :] = full
        table[at, :] = full.astype(jnp.float32)

    event_table(events, coeffs, moves[:QUARTERS], moves[QUARTERS : 2 * QUARTERS], store)
    moves[-2].wait()
    moves[-1].wait()
    for j in range(0, RANK, 8):
        spick[j : j + 8, :] = fetch(table, [perm[0, skel[0, j + u]] for u in range(8)])
    s = spick[...]
    k = jnp.exp(dot(rows[...], targets(s.astype(jnp.bfloat16)), NT)).astype(jnp.bfloat16)
    su = dot(coeffs[...], k) / events.shape[1] ** 0.5
    own_out[:COLS, :] = su.astype(jnp.bfloat16)
    own_out[COLS : COLS + FEAT, :] = s.T[X0:N0].astype(jnp.bfloat16)
    own_out[COLS + FEAT :, :] = jnp.zeros((LANES - COLS - FEAT, RANK), jnp.bfloat16)


def tree_kernel(
    perm_hbm, events_hbm, coeffs_hbm, lo_hbm, hi_hbm, w_hbm, t_hbm,
    lo_out, hi_out, w_out, t_out, table, picked, perm, events, coeffs, sems,
):
    moves = start_copies(
        quarters(events_hbm, events) + quarters(coeffs_hbm, coeffs) + [(perm_hbm, perm)], sems
    )

    def store(at, full):
        table[at, :] = full.astype(jnp.float32)

    event_table(events, coeffs, moves[:QUARTERS], moves[QUARTERS : 2 * QUARTERS], store)
    moves[-1].wait()
    step = 64

    def gather(rows_out, base, c, _):
        def some(b, _):
            for v in range(0, step, 8):
                e = (base + c) * LEAF + b * step + v
                picked[block(b * (step // 8) + v // 8, 8), :] = fetch(
                    table, [perm[0, e + u] for u in range(8)]
                )
            return 0

        lax.fori_loop(0, LEAF // step, some, 0)
        at = block(base + c, LEAF)
        r = picked[...]
        rb = r.astype(jnp.bfloat16)
        rows_out[block(c, LEAF), :] = rb
        w_out[:, at] = r.T[:COLS].astype(jnp.bfloat16)
        t_out[at, :] = targets(rb)
        return 0

    half = events.shape[1] // LEAF // 2
    lax.fori_loop(0, half, functools.partial(gather, lo_out, 0), 0)
    outs = [
        pltpu.make_async_copy(src, dst, sems.at[2 * QUARTERS + 1 + i])
        for i, (src, dst) in enumerate(
            [(lo_out, lo_hbm), (hi_out, hi_hbm), (w_out, w_hbm), (t_out, t_hbm)]
        )
    ]
    outs[0].start()
    lax.fori_loop(0, half, functools.partial(gather, hi_out, half), 0)
    for m in outs[1:]:
        m.start()
    for m in outs:
        m.wait()


def halves_dot(lo, hi, w, ts):
    half = lo.shape[0]
    ka = jnp.exp(dot(lo[...], ts, NT)).astype(jnp.bfloat16)
    kb = jnp.exp(dot(hi[...], ts, NT)).astype(jnp.bfloat16)
    return dot(w[:, :half], ka) + dot(w[:, half:], kb)


SMEM = pl.BlockSpec(memory_space=pltpu.SMEM)
VMEM = pl.BlockSpec(memory_space=pltpu.VMEM)
ANY = pl.BlockSpec(memory_space=pl.ANY)


def params(limit=VMEM_LIMIT):
    return pltpu.CompilerParams(vmem_limit_bytes=limit)


def own_call(perm, skel, events, coeffs):
    n = events.shape[1]
    return pl.pallas_call(
        own_kernel,
        out_shape=jax.ShapeDtypeStruct((LANES, RANK), jnp.bfloat16),
        in_specs=[ANY] * 4,
        out_specs=VMEM,
        scratch_shapes=[
            pltpu.VMEM((n, LANES), jnp.float32),
            pltpu.VMEM((n, LANES), jnp.bfloat16),
            pltpu.VMEM((RANK, LANES), jnp.float32),
            pltpu.SMEM(perm.shape, jnp.int32),
            pltpu.SMEM(skel.shape, jnp.int32),
            pltpu.VMEM(events.shape, jnp.bfloat16),
            pltpu.VMEM(coeffs.shape, jnp.bfloat16),
            pltpu.SemaphoreType.DMA((2 * QUARTERS + 2,)),
        ],
        compiler_params=params(),
        cost_estimate=cost(4),
        name="own_skeleton",
    )(perm, skel, events, coeffs)


def tree_call(perm, events, coeffs):
    n = events.shape[1]
    shapes = ((n // 2, LANES), (n // 2, LANES), (COLS, n), (n, LANES))
    return pl.pallas_call(
        tree_kernel,
        out_shape=tuple(jax.ShapeDtypeStruct(s, jnp.bfloat16) for s in shapes),
        in_specs=[ANY] * 3,
        out_specs=(ANY,) * 4,
        scratch_shapes=[pltpu.VMEM(s, jnp.bfloat16) for s in shapes]
        + [
            pltpu.VMEM((n, LANES), jnp.float32),
            pltpu.VMEM((LEAF, LANES), jnp.float32),
            pltpu.SMEM(perm.shape, jnp.int32),
            pltpu.VMEM(events.shape, jnp.bfloat16),
            pltpu.VMEM(coeffs.shape, jnp.bfloat16),
            pltpu.SemaphoreType.DMA((2 * QUARTERS + 5,)),
        ],
        compiler_params=params(),
        cost_estimate=cost(40),
        name="tree_rows",
    )(perm, events, coeffs)


def event_rows(xb):
    none = jnp.zeros((COLS, xb.shape[1]), jnp.bfloat16)
    return jnp.concatenate([none] + features(xb), axis=0).T


def term_kernel(picks, low_all, lo_hbm, hi_hbm, w_hbm, term_out, hx_out, low_x, lo, hi, w, sems):
    moves = start_copies([(lo_hbm, lo), (hi_hbm, hi), (w_hbm, w)], sems)
    nodes = low_all.shape[0] // LANES
    for b in range(nodes):
        x = low_all[b * LANES + COLS : b * LANES + COLS + FEAT, :]
        low_x[:, b * RANK : (b + 1) * RANK] = x
    hit = lax.broadcasted_iota(jnp.int32, (nodes * RANK, RANK), 0) == picks[...]
    hx = dot(low_x[...], jnp.where(hit, 1.0, 0.0).astype(jnp.bfloat16)).astype(jnp.bfloat16)
    hx_out[...] = hx
    ts = targets(event_rows(hx))
    for m in moves:
        m.wait()
    term_out[...] = halves_dot(lo, hi, w, ts)


def term_call(picks, low_all, lo, hi, w):
    total = low_all.shape[0] // LANES * RANK
    return pl.pallas_call(
        term_kernel,
        out_shape=(
            jax.ShapeDtypeStruct((COLS, RANK), jnp.float32),
            jax.ShapeDtypeStruct((FEAT, RANK), jnp.bfloat16),
        ),
        in_specs=[VMEM] * 2 + [ANY] * 3,
        out_specs=(VMEM,) * 2,
        scratch_shapes=[
            pltpu.VMEM((FEAT, total), jnp.bfloat16),
            pltpu.VMEM(lo.shape, jnp.bfloat16),
            pltpu.VMEM(hi.shape, jnp.bfloat16),
            pltpu.VMEM(w.shape, jnp.bfloat16),
            pltpu.SemaphoreType.DMA((3,)),
        ],
        compiler_params=params(),
        cost_estimate=cost(4),
        name="high_term",
    )(picks, low_all, lo, hi, w)


def low_kernel(far, low_all, t, part, low, low_w):
    nodes = low_all.shape[0] // LANES

    @pl.when(pl.program_id(0) == 0)
    def _():
        for b in range(0, nodes, 4):
            xs = []
            for j in range(b, b + 4):
                low_w[:, j * RANK : (j + 1) * RANK] = low_all[j * LANES : j * LANES + COLS, :]
                xs.append(low_all[j * LANES + COLS : j * LANES + COLS + FEAT, :])
            low[b * RANK : (b + 4) * RANK, :] = event_rows(jnp.concatenate(xs, axis=1))

    groups = far.shape[1] // 4
    leaves = part.shape[0]
    ks = []
    for j in range(leaves):
        leaf = pl.program_id(0) * leaves + j
        tl = t[j * LEAF : (j + 1) * LEAF, :]
        for g in range(groups):
            spots = [block(far[leaf, 4 * g + i], RANK) for i in range(4)]
            r = jnp.concatenate([low[s, :] for s in spots], axis=0)
            ks.append((spots, jnp.exp(dot(r, tl, NT)).astype(jnp.bfloat16)))
    for j in range(leaves):
        total = None
        for spots, k in ks[j * groups : (j + 1) * groups]:
            p = dot(jnp.concatenate([low_w[:, s] for s in spots], axis=1), k)
            total = p if total is None else total + p
        part[j] = total


def low_call(far, low_all, t):
    each = 2
    total = low_all.shape[0] // LANES * RANK
    return pl.pallas_call(
        low_kernel,
        out_shape=jax.ShapeDtypeStruct((LEAF_DEV, COLS, LEAF), jnp.float32),
        grid=(LEAF_DEV // each,),
        in_specs=[
            SMEM,
            pl.BlockSpec(low_all.shape, lambda i: (0, 0)),
            pl.BlockSpec((each * LEAF, LANES), lambda i: (i, 0)),
        ],
        out_specs=pl.BlockSpec((each, COLS, LEAF), lambda i: (i, 0, 0)),
        scratch_shapes=[
            pltpu.VMEM((total, LANES), jnp.bfloat16),
            pltpu.VMEM((COLS, total), jnp.bfloat16),
        ],
        compiler_params=params(),
        cost_estimate=cost(64),
        name="far_low",
    )(far, low_all, t)


def pair_list(near, count, first, pairs, place):
    def leaf_slots(leaf, n):
        def slot(s, n):
            at, takes = place(near[leaf, s] - first[0])
            pairs[n] = leaf * 64 + at
            return n + jnp.where(takes, 1, 0)

        return lax.fori_loop(0, count[leaf], slot, n)

    n = lax.fori_loop(0, LEAF_DEV, leaf_slots, jnp.int32(0))
    for u in range(8):
        pairs[n + u] = LEAF_DEV * 64
    return n


def pair_sums(n, pairs, rows, w, t, acc):
    def step(begin, many):
        ks = []
        for u in range(many):
            e = pairs[begin + u]
            leaf, at = e // 64, e % 64
            tl = t[block(jnp.minimum(leaf, LEAF_DEV - 1), LEAF), :]
            k = jnp.exp(dot(rows[block(at, LEAF), :], tl, NT)).astype(jnp.bfloat16)
            ks.append((leaf, at, k))
        for leaf, at, k in ks:
            acc[leaf] = acc[leaf] + dot(w[:, block(at, LEAF)], k)

    def eight(s, _):
        step(s * 8, 8)
        return 0

    lax.fori_loop(0, n // 8, eight, 0)

    def four(s, _):
        step(n // 8 * 8 + s * 4, 4)
        return 0

    lax.fori_loop(0, (n % 8 + 3) // 4, four, 0)


def near_own_kernel(near, count, first, lo, hi, w_hbm, t_hbm, acc, rows, w, t, pairs, sems):
    half = lo.shape[0]
    moves = start_copies(
        [
            (lo, rows.at[pl.ds(0, half), :]),
            (hi, rows.at[pl.ds(half, half), :]),
            (w_hbm, w),
            (t_hbm, t),
        ],
        sems,
    )
    n = pair_list(near, count, first, pairs, lambda at: (at, (at >= 0) & (at < LEAF_DEV)))
    acc[...] = jnp.zeros_like(acc)
    for m in moves:
        m.wait()
    pair_sums(n, pairs, rows, w, t, acc)


def near_own_call(near, count, first, lo, hi, w, t):
    return pl.pallas_call(
        near_own_kernel,
        out_shape=jax.ShapeDtypeStruct((LEAF_DEV + 1, COLS, LEAF), jnp.float32),
        in_specs=[SMEM] * 3 + [ANY] * 4,
        out_specs=VMEM,
        scratch_shapes=[
            pltpu.VMEM(t.shape, jnp.bfloat16),
            pltpu.VMEM(w.shape, jnp.bfloat16),
            pltpu.VMEM(t.shape, jnp.bfloat16),
            pltpu.SMEM((LEAF_DEV * NEAR + 8,), jnp.int32),
            pltpu.SemaphoreType.DMA((4,)),
        ],
        compiler_params=params(),
        cost_estimate=cost(60),
        name="near_own",
    )(near, count, first, lo, hi, w, t)


def near_side_kernel(
    scales, near, count, first, left, right, t_hbm, acc_hbm, low_hbm, out, rows, w, t, acc, low, pairs, sems
):
    near_scale, low_scale = scales
    side = REACH * LEAF
    moves = start_copies(
        [
            (left, rows.at[pl.ds(0, side), :]),
            (right, rows.at[pl.ds(side, side), :]),
            (t_hbm, t),
            (acc_hbm, acc),
            (low_hbm, low),
        ],
        sems,
    )
    n = pair_list(
        near, count, first, pairs,
        lambda at: (jnp.where(at < 0, at + REACH, at - REACH), (at < 0) | (at >= LEAF_DEV)),
    )
    moves[0].wait()
    moves[1].wait()

    def flip(b, _):
        for at in (block(b, LEAF), block(b + REACH, LEAF)):
            w[:, at] = weights(rows[at, :])
        return 0

    lax.fori_loop(0, REACH, flip, 0)
    for m in moves[2:]:
        m.wait()
    pair_sums(n, pairs, rows, w, t, acc)
    for leaf in range(LEAF_DEV):
        at = slice(leaf * LEAF, (leaf + 1) * LEAF)
        out[:, at] = acc[leaf] * near_scale + low[leaf] * low_scale


def near_side_call(scales, near, count, first, left, right, t, acc, low):
    n = 2 * REACH * LEAF
    return pl.pallas_call(
        lambda *refs: near_side_kernel(scales, *refs),
        out_shape=jax.ShapeDtypeStruct((COLS, LEAF_DEV * LEAF), jnp.float32),
        in_specs=[SMEM] * 3 + [ANY] * 5,
        out_specs=VMEM,
        scratch_shapes=[
            pltpu.VMEM((n, LANES), jnp.bfloat16),
            pltpu.VMEM((COLS, n), jnp.bfloat16),
            pltpu.VMEM(t.shape, jnp.bfloat16),
            pltpu.VMEM(acc.shape, jnp.float32),
            pltpu.VMEM(low.shape, jnp.float32),
            pltpu.SMEM((LEAF_DEV * NEAR + 8,), jnp.int32),
            pltpu.SemaphoreType.DMA((5,)),
        ],
        compiler_params=params(),
        cost_estimate=cost(50),
        name="near_sides",
    )(near, count, first, left, right, t, acc, low)


def upper_kernel(scale, ratio, terms, hx, upper):
    total = terms[:COLS, :]
    for m in range(1, terms.shape[0] // COLS):
        total = total + terms[m * COLS : (m + 1) * COLS, :]
    upper[:COLS, :] = (total * scale).astype(jnp.bfloat16) * jnp.bfloat16(ratio)
    upper[COLS:, :] = hx[...]


def upper_call(scale, ratio, terms, hx):
    return pl.pallas_call(
        lambda *refs: upper_kernel(scale, ratio, *refs),
        out_shape=jax.ShapeDtypeStruct((COLS + FEAT, RANK), jnp.bfloat16),
        in_specs=[VMEM] * 2,
        out_specs=VMEM,
        compiler_params=params(),
        name="high_sum",
    )(terms, hx)


def high_kernel(scale, n_up, *refs):
    sources, (t, part, out, ups, high_w, high_x, sems) = refs[:n_up], refs[n_up:]
    each = COLS + FEAT

    @pl.when(pl.program_id(0) == 0)
    def _():
        sizes = [u.shape[0] for u in sources]
        starts = [sum(sizes[:i]) for i in range(n_up)]
        moves = start_copies(
            [(u, ups.at[pl.ds(at, n), :]) for u, at, n in zip(sources, starts, sizes)], sems
        )
        for m in moves:
            m.wait()
        others = range(0, ups.shape[0], each)
        high_w[...] = jnp.concatenate([ups[i : i + COLS, :] for i in others], axis=1)
        xs = [ups[i + COLS : i + each, :] for i in others]
        high_x[...] = event_rows(jnp.concatenate(xs, axis=1))

    many = out.shape[1] // LEAF
    ats = [slice(j * LEAF, (j + 1) * LEAF) for j in range(many)]
    ks = [jnp.exp(dot(high_x[...], t[at, :], NT)).astype(jnp.bfloat16) for at in ats]
    for at, k in zip(ats, ks):
        out[:, at] = (part[:, at] + dot(high_w[...], k) * scale).astype(jnp.bfloat16)


def high_call(scale, ups, t, part):
    many = 4
    rows = sum(u.shape[0] for u in ups)
    total = rows // (COLS + FEAT) * RANK
    return pl.pallas_call(
        lambda *refs: high_kernel(scale, len(ups), *refs),
        out_shape=jax.ShapeDtypeStruct(part.shape, jnp.bfloat16),
        grid=(LEAF_DEV // many,),
        in_specs=[ANY] * len(ups)
        + [
            pl.BlockSpec((many * LEAF, LANES), lambda i: (i, 0)),
            pl.BlockSpec((COLS, many * LEAF), lambda i: (0, i)),
        ],
        out_specs=pl.BlockSpec((COLS, many * LEAF), lambda i: (0, i)),
        scratch_shapes=[
            pltpu.VMEM((rows, RANK), jnp.bfloat16),
            pltpu.VMEM((COLS, total), jnp.bfloat16),
            pltpu.VMEM((total, LANES), jnp.bfloat16),
            pltpu.SemaphoreType.DMA((len(ups),)),
        ],
        compiler_params=params(),
        cost_estimate=cost(12),
        name="high_out",
    )(*ups, t, part)


def swap(x, axis, mask):
    count = lax.axis_size(axis)
    return lax.ppermute(x, axis, [(i, i ^ mask) for i in range(count)])


def after(x, *others):
    return lax.optimization_barrier((x, *others))[0]


def per_device(events, coeffs, tree_perm, near_list, near_count, far_list, skel_low, skel_high):
    group_devs = lax.axis_size("inner")
    group_count = lax.axis_size("outer")
    far_count = far_list.shape[1]
    ev_dev = events.shape[1]
    inner = lax.axis_index("inner").astype(jnp.int32)
    device = lax.axis_index("outer").astype(jnp.int32) * group_devs + inner
    devices = group_devs * group_count
    first = (device * LEAF_DEV).reshape(1)
    own = own_call(tree_perm, skel_low, events, coeffs)
    low_all = lax.all_gather(own, "inner", axis=0, tiled=True)
    lo, hi, w, t = tree_call(after(tree_perm, own), events, coeffs)
    both = ("outer", "inner")
    left = lax.ppermute(hi, both, [(i, i + 1) for i in range(devices - 1)])
    right = lax.ppermute(lo, both, [(i + 1, i) for i in range(devices - 1)])
    acc = near_own_call(near_list, near_count, first, lo, hi, w, t)

    low_all = after(low_all, acc)
    term, hx = term_call(skel_high, low_all, lo, hi, w)
    terms = lax.all_gather(term, "inner", axis=0, tiled=True)
    far = low_call(far_list, after(low_all, term), t)
    near_scale = 16.0 / (LEAF * NEAR) ** 0.5
    low_scale = 128.0 / (far_count * RANK) ** 0.5
    scales = (near_scale, low_scale)
    part = near_side_call(scales, near_list, near_count, first, left, right, t, acc, far)

    scale = 1.0 / (ev_dev * group_devs) ** 0.5
    upper = upper_call(scale, (far_count / group_count) ** 0.5, after(terms, part), hx)
    ups, mask = [], 1
    while mask < group_count:
        ups.append(swap(upper, "outer", mask))
        upper = jnp.concatenate([upper, ups[-1]], axis=0)
        mask *= 2
    return high_call(low_scale, ups, t, part)


def solution(mesh):
    return jax.shard_map(
        per_device,
        mesh=mesh,
        in_specs=(
            P(None, ("outer", "inner")),
            P(None, ("outer", "inner")),
            P(("outer", "inner"), None),
            P(("outer", "inner"), None),
            P(("outer", "inner")),
            P(("outer", "inner"), None),
            P(("outer", "inner"), None),
            P("outer", None),
        ),
        out_specs=P(None, ("outer", "inner")),
        check_vma=False,
    )
```

```python
import functools

import jax
import jax.numpy as jnp
from jax import lax
from jax.experimental import pallas as pl
from jax.experimental.pallas import tpu as pltpu
from jax.sharding import PartitionSpec as P

LEAF = 512
RANK = 128
NEAR = 32
LEAF_DEV = 16
COLS = 64
FEAT = 16
LANES = 128
REACH = 8
NT = (((1,), (1,)), ((), ()))
NN = (((1,), (0,)), ((), ()))
VMEM_LIMIT = 60 << 20

X0 = COLS
N0 = X0 + FEAT
O0 = N0 + 3


def dot(a, b, dims=NN):
    return lax.dot_general(a, b, dims, preferred_element_type=jnp.float32)


def target_map():
    k = lax.broadcasted_iota(jnp.int32, (LANES, LANES), 0)
    m = lax.broadcasted_iota(jnp.int32, (LANES, LANES), 1)
    quarter = (k == m) & (k >= X0) & (k < N0)
    ones = (k == m + 3) & (m >= N0) & (m < O0)
    pieces = (k + 3 == m) & (k >= N0) & (k < O0)
    return jnp.where(quarter, 0.25, jnp.where(ones | pieces, 1.0, 0.0)).astype(jnp.bfloat16)


def targets(rows):
    return dot(rows, target_map()).astype(jnp.bfloat16)


def block(i, size):
    return pl.ds(pl.multiple_of(i * size, size), size)


def cost(pairs):
    return pl.CostEstimate(
        flops=pairs * 2 * LEAF * LEAF * 384, bytes_accessed=4 << 20, transcendentals=pairs * LEAF * LEAF
    )


def features(xb):
    x = xb.astype(jnp.float32)
    n = jnp.sum(x * x, axis=0, keepdims=True) * -0.125
    n1 = n.astype(jnp.bfloat16).astype(jnp.float32)
    n2 = (n - n1).astype(jnp.bfloat16).astype(jnp.float32)
    n3 = (n - n1 - n2).astype(jnp.bfloat16).astype(jnp.float32)
    r = lax.broadcasted_iota(jnp.int32, xb.shape, 0)
    one = jnp.where(r < 6, 1.0, 0.0)
    ext = jnp.where(r == 0, n1, jnp.where(r == 1, n2, jnp.where(r == 2, n3, one)))
    pad = jnp.zeros((LANES - COLS - 2 * FEAT, xb.shape[1]), jnp.bfloat16)
    return [xb, ext.astype(jnp.bfloat16), pad]


QUARTERS = 4


def quarters(src, dst):
    size = src.shape[1] // QUARTERS
    return [(src.at[:, pl.ds(i * size, size)], dst.at[:, pl.ds(i * size, size)]) for i in range(QUARTERS)]


def event_table(events, coeffs, event_moves, coeff_moves, store):
    def build(c, _):
        at = block(c, LEAF)
        full = jnp.concatenate([coeffs[:, at]] + features(events[:, at]), axis=0)
        store(at, full.T)
        return 0

    each = events.shape[1] // LEAF // QUARTERS
    for i in range(QUARTERS):
        event_moves[i].wait()
        coeff_moves[i].wait()
        lax.fori_loop(i * each, (i + 1) * each, build, 0)


def fetch(table, ids):
    return jnp.concatenate([table[pl.ds(i, 1), :] for i in ids], axis=0)


def start_copies(pairs, sems):
    moves = [pltpu.make_async_copy(src, dst, sems.at[i]) for i, (src, dst) in enumerate(pairs)]
    for m in moves:
        m.start()
    return moves


def weight_copies(wx_lo, wx_hi, w):
    half = wx_lo.shape[1]
    return [
        (wx.at[pl.ds(0, COLS), :], w.at[:, pl.ds(i * half, half)]) for i, wx in enumerate((wx_lo, wx_hi))
    ]


def own_kernel(
    perm_hbm, skel_hbm, events_hbm, coeffs_hbm, own_out,
    table, rows, spick, perm, skel, events, coeffs, sems,
):
    moves = start_copies(
        quarters(events_hbm, events)
        + quarters(coeffs_hbm, coeffs)
        + [(perm_hbm, perm), (skel_hbm, skel)],
        sems,
    )

    def store(at, full):
        rows[at, :] = full
        table[at, :] = full.astype(jnp.float32)

    event_table(events, coeffs, moves[:QUARTERS], moves[QUARTERS : 2 * QUARTERS], store)
    moves[-2].wait()
    moves[-1].wait()
    for j in range(0, RANK, 8):
        spick[j : j + 8, :] = fetch(table, [perm[0, skel[0, j + u]] for u in range(8)])
    s = spick[...]
    k = jnp.exp(dot(rows[...], targets(s.astype(jnp.bfloat16)), NT)).astype(jnp.bfloat16)
    su = dot(coeffs[...], k) / events.shape[1] ** 0.5
    own_out[:COLS, :] = su.astype(jnp.bfloat16)
    own_out[COLS : COLS + FEAT, :] = s.T[X0:N0].astype(jnp.bfloat16)
    own_out[COLS + FEAT :, :] = jnp.zeros((LANES - COLS - FEAT, RANK), jnp.bfloat16)


def tree_kernel(
    perm_hbm, events_hbm, coeffs_hbm, lo_hbm, hi_hbm, wx_lo_hbm, wx_hi_hbm, t_hbm,
    lo_out, hi_out, wx_lo, wx_hi, t_out, table, picked, perm, events, coeffs, sems,
):
    moves = start_copies(
        quarters(events_hbm, events) + quarters(coeffs_hbm, coeffs) + [(perm_hbm, perm)], sems
    )

    def store(at, full):
        table[at, :] = full.astype(jnp.float32)

    event_table(events, coeffs, moves[:QUARTERS], moves[QUARTERS : 2 * QUARTERS], store)
    moves[-1].wait()
    step = 64

    def gather(rows_out, wx_out, base, c, _):
        def some(b, _):
            for v in range(0, step, 8):
                e = (base + c) * LEAF + b * step + v
                picked[block(b * (step // 8) + v // 8, 8), :] = fetch(
                    table, [perm[0, e + u] for u in range(8)]
                )
            return 0

        lax.fori_loop(0, LEAF // step, some, 0)
        r = picked[...]
        rb = r.astype(jnp.bfloat16)
        rows_out[block(c, LEAF), :] = rb
        wx_out[:, block(c, LEAF)] = r.T[:N0].astype(jnp.bfloat16)
        t_out[block(base + c, LEAF), :] = targets(rb)
        return 0

    half = events.shape[1] // LEAF // 2
    lax.fori_loop(0, half, functools.partial(gather, lo_out, wx_lo, 0), 0)
    outs = [
        pltpu.make_async_copy(src, dst, sems.at[2 * QUARTERS + 1 + i])
        for i, (src, dst) in enumerate(
            [(lo_out, lo_hbm), (wx_lo, wx_lo_hbm), (hi_out, hi_hbm), (wx_hi, wx_hi_hbm), (t_out, t_hbm)]
        )
    ]
    for m in outs[:2]:
        m.start()
    lax.fori_loop(0, half, functools.partial(gather, hi_out, wx_hi, half), 0)
    for m in outs[2:]:
        m.start()
    for m in outs:
        m.wait()


def halves_dot(lo, hi, w, ts):
    half = lo.shape[0]
    ka = jnp.exp(dot(lo[...], ts, NT)).astype(jnp.bfloat16)
    kb = jnp.exp(dot(hi[...], ts, NT)).astype(jnp.bfloat16)
    return dot(w[:, :half], ka) + dot(w[:, half:], kb)


SMEM = pl.BlockSpec(memory_space=pltpu.SMEM)
VMEM = pl.BlockSpec(memory_space=pltpu.VMEM)
ANY = pl.BlockSpec(memory_space=pl.ANY)


def params(limit=VMEM_LIMIT):
    return pltpu.CompilerParams(vmem_limit_bytes=limit)


def own_call(perm, skel, events, coeffs):
    n = events.shape[1]
    return pl.pallas_call(
        own_kernel,
        out_shape=jax.ShapeDtypeStruct((LANES, RANK), jnp.bfloat16),
        in_specs=[ANY] * 4,
        out_specs=VMEM,
        scratch_shapes=[
            pltpu.VMEM((n, LANES), jnp.float32),
            pltpu.VMEM((n, LANES), jnp.bfloat16),
            pltpu.VMEM((RANK, LANES), jnp.float32),
            pltpu.SMEM(perm.shape, jnp.int32),
            pltpu.SMEM(skel.shape, jnp.int32),
            pltpu.VMEM(events.shape, jnp.bfloat16),
            pltpu.VMEM(coeffs.shape, jnp.bfloat16),
            pltpu.SemaphoreType.DMA((2 * QUARTERS + 2,)),
        ],
        compiler_params=params(),
        cost_estimate=cost(4),
        name="own_skeleton",
    )(perm, skel, events, coeffs)


def tree_call(perm, events, coeffs):
    n = events.shape[1]
    shapes = ((n // 2, LANES), (n // 2, LANES), (N0, n // 2), (N0, n // 2), (n, LANES))
    return pl.pallas_call(
        tree_kernel,
        out_shape=tuple(jax.ShapeDtypeStruct(s, jnp.bfloat16) for s in shapes),
        in_specs=[ANY] * 3,
        out_specs=(ANY,) * 5,
        scratch_shapes=[pltpu.VMEM(s, jnp.bfloat16) for s in shapes]
        + [
            pltpu.VMEM((n, LANES), jnp.float32),
            pltpu.VMEM((LEAF, LANES), jnp.float32),
            pltpu.SMEM(perm.shape, jnp.int32),
            pltpu.VMEM(events.shape, jnp.bfloat16),
            pltpu.VMEM(coeffs.shape, jnp.bfloat16),
            pltpu.SemaphoreType.DMA((2 * QUARTERS + 6,)),
        ],
        compiler_params=params(),
        cost_estimate=cost(40),
        name="tree_rows",
    )(perm, events, coeffs)


def event_rows(xb):
    none = jnp.zeros((COLS, xb.shape[1]), jnp.bfloat16)
    return jnp.concatenate([none] + features(xb), axis=0).T


def term_kernel(picks, low_all, lo_hbm, hi_hbm, wx_lo, wx_hi, term_out, hx_out, low_x, lo, hi, w, sems):
    moves = start_copies([(lo_hbm, lo), (hi_hbm, hi)] + weight_copies(wx_lo, wx_hi, w), sems)
    nodes = low_all.shape[0] // LANES
    for b in range(nodes):
        x = low_all[b * LANES + COLS : b * LANES + COLS + FEAT, :]
        low_x[:, b * RANK : (b + 1) * RANK] = x
    hit = lax.broadcasted_iota(jnp.int32, (nodes * RANK, RANK), 0) == picks[...]
    hx = dot(low_x[...], jnp.where(hit, 1.0, 0.0).astype(jnp.bfloat16)).astype(jnp.bfloat16)
    hx_out[...] = hx
    ts = targets(event_rows(hx))
    for m in moves:
        m.wait()
    term_out[...] = halves_dot(lo, hi, w, ts)


def term_call(picks, low_all, lo, hi, wx_lo, wx_hi):
    total = low_all.shape[0] // LANES * RANK
    return pl.pallas_call(
        term_kernel,
        out_shape=(
            jax.ShapeDtypeStruct((COLS, RANK), jnp.float32),
            jax.ShapeDtypeStruct((FEAT, RANK), jnp.bfloat16),
        ),
        in_specs=[VMEM] * 2 + [ANY] * 4,
        out_specs=(VMEM,) * 2,
        scratch_shapes=[
            pltpu.VMEM((FEAT, total), jnp.bfloat16),
            pltpu.VMEM(lo.shape, jnp.bfloat16),
            pltpu.VMEM(hi.shape, jnp.bfloat16),
            pltpu.VMEM((COLS, 2 * wx_lo.shape[1]), jnp.bfloat16),
            pltpu.SemaphoreType.DMA((4,)),
        ],
        compiler_params=params(),
        cost_estimate=cost(4),
        name="high_term",
    )(picks, low_all, lo, hi, wx_lo, wx_hi)


def low_kernel(far, low_all, t, part, low, low_w):
    nodes = low_all.shape[0] // LANES

    @pl.when(pl.program_id(0) == 0)
    def _():
        for b in range(0, nodes, 4):
            xs = []
            for j in range(b, b + 4):
                low_w[:, j * RANK : (j + 1) * RANK] = low_all[j * LANES : j * LANES + COLS, :]
                xs.append(low_all[j * LANES + COLS : j * LANES + COLS + FEAT, :])
            low[b * RANK : (b + 4) * RANK, :] = event_rows(jnp.concatenate(xs, axis=1))

    groups = far.shape[1] // 4
    leaves = part.shape[0]
    ks = []
    for j in range(leaves):
        leaf = pl.program_id(0) * leaves + j
        tl = t[j * LEAF : (j + 1) * LEAF, :]
        for g in range(groups):
            spots = [block(far[leaf, 4 * g + i], RANK) for i in range(4)]
            r = jnp.concatenate([low[s, :] for s in spots], axis=0)
            ks.append((spots, jnp.exp(dot(r, tl, NT)).astype(jnp.bfloat16)))
    for j in range(leaves):
        total = None
        for spots, k in ks[j * groups : (j + 1) * groups]:
            p = dot(jnp.concatenate([low_w[:, s] for s in spots], axis=1), k)
            total = p if total is None else total + p
        part[j] = total


def low_call(far, low_all, t):
    each = 2
    total = low_all.shape[0] // LANES * RANK
    return pl.pallas_call(
        low_kernel,
        out_shape=jax.ShapeDtypeStruct((LEAF_DEV, COLS, LEAF), jnp.float32),
        grid=(LEAF_DEV // each,),
        in_specs=[
            SMEM,
            pl.BlockSpec(low_all.shape, lambda i: (0, 0)),
            pl.BlockSpec((each * LEAF, LANES), lambda i: (i, 0)),
        ],
        out_specs=pl.BlockSpec((each, COLS, LEAF), lambda i: (i, 0, 0)),
        scratch_shapes=[
            pltpu.VMEM((total, LANES), jnp.bfloat16),
            pltpu.VMEM((COLS, total), jnp.bfloat16),
        ],
        compiler_params=params(),
        cost_estimate=cost(64),
        name="far_low",
    )(far, low_all, t)


def pair_list(near, count, first, pairs, place):
    def leaf_slots(leaf, n):
        def slot(s, n):
            at, takes = place(near[leaf, s] - first[0])
            pairs[n] = leaf * 64 + at
            return n + jnp.where(takes, 1, 0)

        return lax.fori_loop(0, count[leaf], slot, n)

    n = lax.fori_loop(0, LEAF_DEV, leaf_slots, jnp.int32(0))
    for u in range(8):
        pairs[n + u] = LEAF_DEV * 64
    return n


def pair_sums(n, pairs, rows, w, t, acc):
    def step(begin, many):
        ks = []
        for u in range(many):
            e = pairs[begin + u]
            leaf, at = e // 64, e % 64
            tl = t[block(jnp.minimum(leaf, LEAF_DEV - 1), LEAF), :]
            k = jnp.exp(dot(rows[block(at, LEAF), :], tl, NT)).astype(jnp.bfloat16)
            ks.append((leaf, at, k))
        for leaf, at, k in ks:
            acc[leaf] = acc[leaf] + dot(w[:, block(at, LEAF)], k)

    def eight(s, _):
        step(s * 8, 8)
        return 0

    lax.fori_loop(0, n // 8, eight, 0)

    def four(s, _):
        step(n // 8 * 8 + s * 4, 4)
        return 0

    lax.fori_loop(0, (n % 8 + 3) // 4, four, 0)


def near_own_kernel(near, count, first, lo, hi, wx_lo, wx_hi, t_hbm, acc, rows, w, t, pairs, sems):
    half = lo.shape[0]
    moves = start_copies(
        [
            (lo, rows.at[pl.ds(0, half), :]),
            (hi, rows.at[pl.ds(half, half), :]),
            (t_hbm, t),
        ]
        + weight_copies(wx_lo, wx_hi, w),
        sems,
    )
    n = pair_list(near, count, first, pairs, lambda at: (at, (at >= 0) & (at < LEAF_DEV)))
    acc[...] = jnp.zeros_like(acc)
    for m in moves:
        m.wait()
    pair_sums(n, pairs, rows, w, t, acc)


def near_own_call(near, count, first, lo, hi, wx_lo, wx_hi, t):
    return pl.pallas_call(
        near_own_kernel,
        out_shape=jax.ShapeDtypeStruct((LEAF_DEV + 1, COLS, LEAF), jnp.float32),
        in_specs=[SMEM] * 3 + [ANY] * 5,
        out_specs=VMEM,
        scratch_shapes=[
            pltpu.VMEM(t.shape, jnp.bfloat16),
            pltpu.VMEM((COLS, t.shape[0]), jnp.bfloat16),
            pltpu.VMEM(t.shape, jnp.bfloat16),
            pltpu.SMEM((LEAF_DEV * NEAR + 8,), jnp.int32),
            pltpu.SemaphoreType.DMA((5,)),
        ],
        compiler_params=params(),
        cost_estimate=cost(60),
        name="near_own",
    )(near, count, first, lo, hi, wx_lo, wx_hi, t)


def near_side_kernel(
    scales, near, count, first, left, right, t_hbm, acc_hbm, low_hbm, out, rows, w, x, t, acc, low, pairs, sems
):
    near_scale, low_scale = scales
    side = REACH * LEAF
    moves = start_copies(
        [
            (left.at[pl.ds(COLS, FEAT), :], x.at[:, pl.ds(0, side)]),
            (right.at[pl.ds(COLS, FEAT), :], x.at[:, pl.ds(side, side)]),
            (t_hbm, t),
            (acc_hbm, acc),
            (low_hbm, low),
        ]
        + weight_copies(left, right, w),
        sems,
    )
    n = pair_list(
        near, count, first, pairs,
        lambda at: (jnp.where(at < 0, at + REACH, at - REACH), (at < 0) | (at >= LEAF_DEV)),
    )
    moves[0].wait()
    moves[1].wait()

    def build(b, _):
        at = block(b, LEAF)
        rows[at, :] = event_rows(x[:, at])
        return 0

    lax.fori_loop(0, 2 * REACH, build, 0)
    for m in moves[2:]:
        m.wait()
    pair_sums(n, pairs, rows, w, t, acc)
    for leaf in range(LEAF_DEV):
        at = slice(leaf * LEAF, (leaf + 1) * LEAF)
        out[:, at] = acc[leaf] * near_scale + low[leaf] * low_scale


def near_side_call(scales, near, count, first, left, right, t, acc, low):
    n = 2 * REACH * LEAF
    return pl.pallas_call(
        lambda *refs: near_side_kernel(scales, *refs),
        out_shape=jax.ShapeDtypeStruct((COLS, LEAF_DEV * LEAF), jnp.float32),
        in_specs=[SMEM] * 3 + [ANY] * 5,
        out_specs=VMEM,
        scratch_shapes=[
            pltpu.VMEM((n, LANES), jnp.bfloat16),
            pltpu.VMEM((COLS, n), jnp.bfloat16),
            pltpu.VMEM((FEAT, n), jnp.bfloat16),
            pltpu.VMEM(t.shape, jnp.bfloat16),
            pltpu.VMEM(acc.shape, jnp.float32),
            pltpu.VMEM(low.shape, jnp.float32),
            pltpu.SMEM((LEAF_DEV * NEAR + 8,), jnp.int32),
            pltpu.SemaphoreType.DMA((7,)),
        ],
        compiler_params=params(),
        cost_estimate=cost(50),
        name="near_sides",
    )(near, count, first, left, right, t, acc, low)


def upper_kernel(scale, ratio, terms, hx, upper):
    total = terms[:COLS, :]
    for m in range(1, terms.shape[0] // COLS):
        total = total + terms[m * COLS : (m + 1) * COLS, :]
    upper[:COLS, :] = (total * scale).astype(jnp.bfloat16) * jnp.bfloat16(ratio)
    upper[COLS:, :] = hx[...]


def upper_call(scale, ratio, terms, hx):
    return pl.pallas_call(
        lambda *refs: upper_kernel(scale, ratio, *refs),
        out_shape=jax.ShapeDtypeStruct((COLS + FEAT, RANK), jnp.bfloat16),
        in_specs=[VMEM] * 2,
        out_specs=VMEM,
        compiler_params=params(),
        name="high_sum",
    )(terms, hx)


def high_kernel(scale, *refs):
    *ups, t, part, out = refs
    high_w = jnp.concatenate([u[:COLS, :] for u in ups], axis=1)
    high_x = event_rows(jnp.concatenate([u[COLS:, :] for u in ups], axis=1))
    many = out.shape[1] // LEAF
    ats = [slice(j * LEAF, (j + 1) * LEAF) for j in range(many)]
    ks = [jnp.exp(dot(high_x, t[at, :], NT)).astype(jnp.bfloat16) for at in ats]
    for at, k in zip(ats, ks):
        out[:, at] = (part[:, at] + dot(high_w, k) * scale).astype(jnp.bfloat16)


def high_call(scale, ups, t, part):
    many = 4
    return pl.pallas_call(
        lambda *refs: high_kernel(scale, *refs),
        out_shape=jax.ShapeDtypeStruct(part.shape, jnp.bfloat16),
        grid=(LEAF_DEV // many,),
        in_specs=[pl.BlockSpec(u.shape, lambda i: (0, 0)) for u in ups]
        + [
            pl.BlockSpec((many * LEAF, LANES), lambda i: (i, 0)),
            pl.BlockSpec((COLS, many * LEAF), lambda i: (0, i)),
        ],
        out_specs=pl.BlockSpec((COLS, many * LEAF), lambda i: (0, i)),
        compiler_params=params(),
        cost_estimate=cost(12),
        name="high_out",
    )(*ups, t, part)


def swap(x, axis, mask):
    count = lax.axis_size(axis)
    return lax.ppermute(x, axis, [(i, i ^ mask) for i in range(count)])


def after(x, *others):
    return lax.optimization_barrier((x, *others))[0]


def per_device(events, coeffs, tree_perm, near_list, near_count, far_list, skel_low, skel_high):
    group_devs = lax.axis_size("inner")
    group_count = lax.axis_size("outer")
    far_count = far_list.shape[1]
    ev_dev = events.shape[1]
    inner = lax.axis_index("inner").astype(jnp.int32)
    device = lax.axis_index("outer").astype(jnp.int32) * group_devs + inner
    devices = group_devs * group_count
    first = (device * LEAF_DEV).reshape(1)
    own = own_call(tree_perm, skel_low, events, coeffs)
    low_all = lax.all_gather(own, "inner", axis=0, tiled=True)
    lo, hi, wx_lo, wx_hi, t = tree_call(after(tree_perm, own), events, coeffs)
    both = ("outer", "inner")
    left = lax.ppermute(wx_hi, both, [(i, i + 1) for i in range(devices - 1)])
    right = lax.ppermute(wx_lo, both, [(i + 1, i) for i in range(devices - 1)])
    acc = near_own_call(near_list, near_count, first, lo, hi, wx_lo, wx_hi, t)

    low_all = after(low_all, acc)
    term, hx = term_call(skel_high, low_all, lo, hi, wx_lo, wx_hi)
    terms = lax.all_gather(term, "inner", axis=0, tiled=True)
    far = low_call(far_list, after(low_all, term), t)
    near_scale = 16.0 / (LEAF * NEAR) ** 0.5
    low_scale = 128.0 / (far_count * RANK) ** 0.5
    scales = (near_scale, low_scale)
    part = near_side_call(scales, near_list, near_count, first, left, right, t, acc, far)

    scale = 1.0 / (ev_dev * group_devs) ** 0.5
    upper = upper_call(scale, (far_count / group_count) ** 0.5, after(terms, part), hx)
    ups = [swap(upper, "outer", m) for m in range(1, group_count)]
    return high_call(low_scale, ups, t, part)


def solution(mesh):
    return jax.shard_map(
        per_device,
        mesh=mesh,
        in_specs=(
            P(None, ("outer", "inner")),
            P(None, ("outer", "inner")),
            P(("outer", "inner"), None),
            P(("outer", "inner"), None),
            P(("outer", "inner")),
            P(("outer", "inner"), None),
            P(("outer", "inner"), None),
            P("outer", None),
        ),
        out_specs=P(None, ("outer", "inner")),
        check_vma=False,
    )
```

```python
import functools

import jax
import jax.numpy as jnp
from jax import lax
from jax.experimental import pallas as pl
from jax.experimental.pallas import tpu as pltpu
from jax.sharding import PartitionSpec as P

LEAF = 512
RANK = 128
NEAR = 32
LEAF_DEV = 16
COLS = 64
FEAT = 16
LANES = 128
REACH = 8
NT = (((1,), (1,)), ((), ()))
NN = (((1,), (0,)), ((), ()))
VMEM_LIMIT = 60 << 20

X0 = COLS
N0 = X0 + FEAT
O0 = N0 + 3


def dot(a, b, dims=NN):
    return lax.dot_general(a, b, dims, preferred_element_type=jnp.float32)


def target_map():
    k = lax.broadcasted_iota(jnp.int32, (LANES, LANES), 0)
    m = lax.broadcasted_iota(jnp.int32, (LANES, LANES), 1)
    quarter = (k == m) & (k >= X0) & (k < N0)
    ones = (k == m + 3) & (m >= N0) & (m < O0)
    pieces = (k + 3 == m) & (k >= N0) & (k < O0)
    return jnp.where(quarter, 0.25, jnp.where(ones | pieces, 1.0, 0.0)).astype(jnp.bfloat16)


def targets(rows):
    return dot(rows, target_map()).astype(jnp.bfloat16)


def block(i, size):
    return pl.ds(pl.multiple_of(i * size, size), size)


def cost(pairs):
    return pl.CostEstimate(
        flops=pairs * 2 * LEAF * LEAF * 384, bytes_accessed=4 << 20, transcendentals=pairs * LEAF * LEAF
    )


def features(xb):
    x = xb.astype(jnp.float32)
    n = jnp.sum(x * x, axis=0, keepdims=True) * -0.125
    n1 = n.astype(jnp.bfloat16).astype(jnp.float32)
    n2 = (n - n1).astype(jnp.bfloat16).astype(jnp.float32)
    n3 = (n - n1 - n2).astype(jnp.bfloat16).astype(jnp.float32)
    r = lax.broadcasted_iota(jnp.int32, xb.shape, 0)
    one = jnp.where(r < 6, 1.0, 0.0)
    ext = jnp.where(r == 0, n1, jnp.where(r == 1, n2, jnp.where(r == 2, n3, one)))
    pad = jnp.zeros((LANES - COLS - 2 * FEAT, xb.shape[1]), jnp.bfloat16)
    return [xb, ext.astype(jnp.bfloat16), pad]


QUARTERS = 4


def quarters(src, dst):
    size = src.shape[1] // QUARTERS
    return [(src.at[:, pl.ds(i * size, size)], dst.at[:, pl.ds(i * size, size)]) for i in range(QUARTERS)]


def event_table(events, coeffs, event_moves, coeff_moves, store):
    def build(c, _):
        at = block(c, LEAF)
        full = jnp.concatenate([coeffs[:, at]] + features(events[:, at]), axis=0)
        store(at, full.T)
        return 0

    each = events.shape[1] // LEAF // QUARTERS
    for i in range(QUARTERS):
        event_moves[i].wait()
        coeff_moves[i].wait()
        lax.fori_loop(i * each, (i + 1) * each, build, 0)


def fetch(table, ids):
    return jnp.concatenate([table[pl.ds(i, 1), :] for i in ids], axis=0)


def start_copies(pairs, sems):
    moves = [pltpu.make_async_copy(src, dst, sems.at[i]) for i, (src, dst) in enumerate(pairs)]
    for m in moves:
        m.start()
    return moves


def weight_copies(wx_lo, wx_hi, w):
    half = wx_lo.shape[1]
    return [
        (wx.at[pl.ds(0, COLS), :], w.at[:, pl.ds(i * half, half)]) for i, wx in enumerate((wx_lo, wx_hi))
    ]


def own_kernel(
    perm_hbm, skel_hbm, events_hbm, coeffs_hbm, own_out,
    table, rows, spick, perm, skel, events, coeffs, sems,
):
    moves = start_copies(
        quarters(events_hbm, events)
        + quarters(coeffs_hbm, coeffs)
        + [(perm_hbm, perm), (skel_hbm, skel)],
        sems,
    )

    def store(at, full):
        rows[at, :] = full
        table[at, :] = full.astype(jnp.float32)

    event_table(events, coeffs, moves[:QUARTERS], moves[QUARTERS : 2 * QUARTERS], store)
    moves[-2].wait()
    moves[-1].wait()
    for j in range(0, RANK, 8):
        spick[j : j + 8, :] = fetch(table, [perm[0, skel[0, j + u]] for u in range(8)])
    s = spick[...]
    k = jnp.exp(dot(rows[...], targets(s.astype(jnp.bfloat16)), NT)).astype(jnp.bfloat16)
    su = dot(coeffs[...], k) / events.shape[1] ** 0.5
    own_out[:COLS, :] = su.astype(jnp.bfloat16)
    own_out[COLS : COLS + FEAT, :] = s.T[X0:N0].astype(jnp.bfloat16)
    own_out[COLS + FEAT :, :] = jnp.zeros((LANES - COLS - FEAT, RANK), jnp.bfloat16)


def tree_kernel(
    perm_hbm, events_hbm, coeffs_hbm, lo_hbm, hi_hbm, wx_lo_hbm, wx_hi_hbm, t_hbm,
    lo_out, hi_out, wx_lo, wx_hi, t_out, table, picked, perm, events, coeffs, sems,
):
    moves = start_copies(
        quarters(events_hbm, events) + quarters(coeffs_hbm, coeffs) + [(perm_hbm, perm)], sems
    )

    def store(at, full):
        table[at, :] = full.astype(jnp.float32)

    event_table(events, coeffs, moves[:QUARTERS], moves[QUARTERS : 2 * QUARTERS], store)
    moves[-1].wait()
    step = 64

    def gather(rows_out, wx_out, base, c, _):
        def some(b, _):
            for v in range(0, step, 8):
                e = (base + c) * LEAF + b * step + v
                picked[block(b * (step // 8) + v // 8, 8), :] = fetch(
                    table, [perm[0, e + u] for u in range(8)]
                )
            return 0

        lax.fori_loop(0, LEAF // step, some, 0)
        r = picked[...]
        rb = r.astype(jnp.bfloat16)
        rows_out[block(c, LEAF), :] = rb
        wx_out[:, block(c, LEAF)] = r.T[:N0].astype(jnp.bfloat16)
        t_out[block(base + c, LEAF), :] = targets(rb)
        return 0

    half = events.shape[1] // LEAF // 2
    lax.fori_loop(0, half, functools.partial(gather, lo_out, wx_lo, 0), 0)
    outs = [
        pltpu.make_async_copy(src, dst, sems.at[2 * QUARTERS + 1 + i])
        for i, (src, dst) in enumerate(
            [(lo_out, lo_hbm), (wx_lo, wx_lo_hbm), (hi_out, hi_hbm), (wx_hi, wx_hi_hbm), (t_out, t_hbm)]
        )
    ]
    for m in outs[:2]:
        m.start()
    lax.fori_loop(0, half, functools.partial(gather, hi_out, wx_hi, half), 0)
    for m in outs[2:]:
        m.start()
    for m in outs:
        m.wait()


def halves_dot(lo, hi, w, ts):
    half = lo.shape[0]
    ka = jnp.exp(dot(lo[...], ts, NT)).astype(jnp.bfloat16)
    kb = jnp.exp(dot(hi[...], ts, NT)).astype(jnp.bfloat16)
    return dot(w[:, :half], ka) + dot(w[:, half:], kb)


SMEM = pl.BlockSpec(memory_space=pltpu.SMEM)
VMEM = pl.BlockSpec(memory_space=pltpu.VMEM)
ANY = pl.BlockSpec(memory_space=pl.ANY)


def params(limit=VMEM_LIMIT):
    return pltpu.CompilerParams(vmem_limit_bytes=limit)


def own_call(perm, skel, events, coeffs):
    n = events.shape[1]
    return pl.pallas_call(
        own_kernel,
        out_shape=jax.ShapeDtypeStruct((LANES, RANK), jnp.bfloat16),
        in_specs=[ANY] * 4,
        out_specs=VMEM,
        scratch_shapes=[
            pltpu.VMEM((n, LANES), jnp.float32),
            pltpu.VMEM((n, LANES), jnp.bfloat16),
            pltpu.VMEM((RANK, LANES), jnp.float32),
            pltpu.SMEM(perm.shape, jnp.int32),
            pltpu.SMEM(skel.shape, jnp.int32),
            pltpu.VMEM(events.shape, jnp.bfloat16),
            pltpu.VMEM(coeffs.shape, jnp.bfloat16),
            pltpu.SemaphoreType.DMA((2 * QUARTERS + 2,)),
        ],
        compiler_params=params(),
        cost_estimate=cost(4),
        name="own_skeleton",
    )(perm, skel, events, coeffs)


def tree_call(perm, events, coeffs):
    n = events.shape[1]
    shapes = ((n // 2, LANES), (n // 2, LANES), (N0, n // 2), (N0, n // 2), (n, LANES))
    return pl.pallas_call(
        tree_kernel,
        out_shape=tuple(jax.ShapeDtypeStruct(s, jnp.bfloat16) for s in shapes),
        in_specs=[ANY] * 3,
        out_specs=(ANY,) * 5,
        scratch_shapes=[pltpu.VMEM(s, jnp.bfloat16) for s in shapes]
        + [
            pltpu.VMEM((n, LANES), jnp.float32),
            pltpu.VMEM((LEAF, LANES), jnp.float32),
            pltpu.SMEM(perm.shape, jnp.int32),
            pltpu.VMEM(events.shape, jnp.bfloat16),
            pltpu.VMEM(coeffs.shape, jnp.bfloat16),
            pltpu.SemaphoreType.DMA((2 * QUARTERS + 6,)),
        ],
        compiler_params=params(),
        cost_estimate=cost(40),
        name="tree_rows",
    )(perm, events, coeffs)


def event_rows(xb):
    none = jnp.zeros((COLS, xb.shape[1]), jnp.bfloat16)
    return jnp.concatenate([none] + features(xb), axis=0).T


def term_kernel(picks, low_all, lo_hbm, hi_hbm, wx_lo, wx_hi, term_out, hx_out, low_x, lo, hi, w, sems):
    nodes = low_all.shape[0] // LANES
    features_of = [
        (low_all.at[pl.ds(b * LANES + COLS, FEAT), :], low_x.at[:, pl.ds(b * RANK, RANK)])
        for b in range(nodes)
    ]
    moves = start_copies(
        features_of + [(lo_hbm, lo), (hi_hbm, hi)] + weight_copies(wx_lo, wx_hi, w), sems
    )
    for m in moves[:nodes]:
        m.wait()
    hit = lax.broadcasted_iota(jnp.int32, (nodes * RANK, RANK), 0) == picks[...]
    hx = dot(low_x[...], jnp.where(hit, 1.0, 0.0).astype(jnp.bfloat16)).astype(jnp.bfloat16)
    hx_out[...] = hx
    ts = targets(event_rows(hx))
    for m in moves[nodes:]:
        m.wait()
    term_out[...] = halves_dot(lo, hi, w, ts)


def term_call(picks, low_all, lo, hi, wx_lo, wx_hi):
    total = low_all.shape[0] // LANES * RANK
    return pl.pallas_call(
        term_kernel,
        out_shape=(
            jax.ShapeDtypeStruct((COLS, RANK), jnp.float32),
            jax.ShapeDtypeStruct((FEAT, RANK), jnp.bfloat16),
        ),
        in_specs=[VMEM] + [ANY] * 5,
        out_specs=(VMEM,) * 2,
        scratch_shapes=[
            pltpu.VMEM((FEAT, total), jnp.bfloat16),
            pltpu.VMEM(lo.shape, jnp.bfloat16),
            pltpu.VMEM(hi.shape, jnp.bfloat16),
            pltpu.VMEM((COLS, 2 * wx_lo.shape[1]), jnp.bfloat16),
            pltpu.SemaphoreType.DMA((4 + total // RANK,)),
        ],
        compiler_params=params(),
        cost_estimate=cost(4),
        name="high_term",
    )(picks, low_all, lo, hi, wx_lo, wx_hi)


def low_kernel(far, low_all, t, part, low, low_w):
    nodes = low_all.shape[0] // LANES

    @pl.when(pl.program_id(0) == 0)
    def _():
        for b in range(0, nodes, 4):
            xs = []
            for j in range(b, b + 4):
                low_w[:, j * RANK : (j + 1) * RANK] = low_all[j * LANES : j * LANES + COLS, :]
                xs.append(low_all[j * LANES + COLS : j * LANES + COLS + FEAT, :])
            low[b * RANK : (b + 4) * RANK, :] = event_rows(jnp.concatenate(xs, axis=1))

    groups = far.shape[1] // 4
    leaves = part.shape[0]
    ks = []
    for j in range(leaves):
        leaf = pl.program_id(0) * leaves + j
        tl = t[j * LEAF : (j + 1) * LEAF, :]
        for g in range(groups):
            spots = [block(far[leaf, 4 * g + i], RANK) for i in range(4)]
            r = jnp.concatenate([low[s, :] for s in spots], axis=0)
            ks.append((spots, jnp.exp(dot(r, tl, NT)).astype(jnp.bfloat16)))
    for j in range(leaves):
        total = None
        for spots, k in ks[j * groups : (j + 1) * groups]:
            p = dot(jnp.concatenate([low_w[:, s] for s in spots], axis=1), k)
            total = p if total is None else total + p
        part[j] = total


def low_call(far, low_all, t):
    each = 4
    total = low_all.shape[0] // LANES * RANK
    return pl.pallas_call(
        low_kernel,
        out_shape=jax.ShapeDtypeStruct((LEAF_DEV, COLS, LEAF), jnp.float32),
        grid=(LEAF_DEV // each,),
        in_specs=[
            SMEM,
            pl.BlockSpec(low_all.shape, lambda i: (0, 0)),
            pl.BlockSpec((each * LEAF, LANES), lambda i: (i, 0)),
        ],
        out_specs=pl.BlockSpec((each, COLS, LEAF), lambda i: (i, 0, 0)),
        scratch_shapes=[
            pltpu.VMEM((total, LANES), jnp.bfloat16),
            pltpu.VMEM((COLS, total), jnp.bfloat16),
        ],
        compiler_params=params(),
        cost_estimate=cost(64),
        name="far_low",
    )(far, low_all, t)


def pair_list(near, count, first, pairs, place):
    def leaf_slots(leaf, n):
        def slot(s, n):
            at, takes = place(near[leaf, s] - first[0])
            pairs[n] = leaf * 64 + at
            return n + jnp.where(takes, 1, 0)

        return lax.fori_loop(0, count[leaf], slot, n)

    n = lax.fori_loop(0, LEAF_DEV, leaf_slots, jnp.int32(0))
    for u in range(8):
        pairs[n + u] = LEAF_DEV * 64
    return n


def pair_sums(n, pairs, rows, w, t, acc):
    def step(begin, many):
        ks = []
        for u in range(many):
            e = pairs[begin + u]
            leaf, at = e // 64, e % 64
            tl = t[block(jnp.minimum(leaf, LEAF_DEV - 1), LEAF), :]
            k = jnp.exp(dot(rows[block(at, LEAF), :], tl, NT)).astype(jnp.bfloat16)
            ks.append((leaf, at, k))
        for leaf, at, k in ks:
            acc[leaf] = acc[leaf] + dot(w[:, block(at, LEAF)], k)

    def eight(s, _):
        step(s * 8, 8)
        return 0

    lax.fori_loop(0, n // 8, eight, 0)

    def four(s, _):
        step(n // 8 * 8 + s * 4, 4)
        return 0

    lax.fori_loop(0, (n % 8 + 3) // 4, four, 0)


def near_own_kernel(near, count, first, lo, hi, wx_lo, wx_hi, t_hbm, acc, rows, w, t, pairs, sems):
    half = lo.shape[0]
    moves = start_copies(
        [
            (lo, rows.at[pl.ds(0, half), :]),
            (hi, rows.at[pl.ds(half, half), :]),
            (t_hbm, t),
        ]
        + weight_copies(wx_lo, wx_hi, w),
        sems,
    )
    n = pair_list(near, count, first, pairs, lambda at: (at, (at >= 0) & (at < LEAF_DEV)))
    acc[...] = jnp.zeros_like(acc)
    for m in moves:
        m.wait()
    pair_sums(n, pairs, rows, w, t, acc)


def near_own_call(near, count, first, lo, hi, wx_lo, wx_hi, t):
    return pl.pallas_call(
        near_own_kernel,
        out_shape=jax.ShapeDtypeStruct((LEAF_DEV + 1, COLS, LEAF), jnp.float32),
        in_specs=[SMEM] * 3 + [ANY] * 5,
        out_specs=VMEM,
        scratch_shapes=[
            pltpu.VMEM(t.shape, jnp.bfloat16),
            pltpu.VMEM((COLS, t.shape[0]), jnp.bfloat16),
            pltpu.VMEM(t.shape, jnp.bfloat16),
            pltpu.SMEM((LEAF_DEV * NEAR + 8,), jnp.int32),
            pltpu.SemaphoreType.DMA((5,)),
        ],
        compiler_params=params(),
        cost_estimate=cost(60),
        name="near_own",
    )(near, count, first, lo, hi, wx_lo, wx_hi, t)


def near_side_kernel(
    scales, near, count, first, left, right, t_hbm, acc_hbm, low_hbm, out, rows, w, x, t, acc, low, pairs, sems
):
    near_scale, low_scale = scales
    side = REACH * LEAF
    moves = start_copies(
        [
            (left.at[pl.ds(COLS, FEAT), :], x.at[:, pl.ds(0, side)]),
            (right.at[pl.ds(COLS, FEAT), :], x.at[:, pl.ds(side, side)]),
            (t_hbm, t),
            (acc_hbm, acc),
            (low_hbm, low),
        ]
        + weight_copies(left, right, w),
        sems,
    )
    n = pair_list(
        near, count, first, pairs,
        lambda at: (jnp.where(at < 0, at + REACH, at - REACH), (at < 0) | (at >= LEAF_DEV)),
    )
    moves[0].wait()
    moves[1].wait()

    def build(b, _):
        at = block(b, LEAF)
        rows[at, :] = event_rows(x[:, at])
        return 0

    lax.fori_loop(0, 2 * REACH, build, 0)
    for m in moves[2:]:
        m.wait()
    pair_sums(n, pairs, rows, w, t, acc)
    for leaf in range(LEAF_DEV):
        at = slice(leaf * LEAF, (leaf + 1) * LEAF)
        out[:, at] = acc[leaf] * near_scale + low[leaf] * low_scale


def near_side_call(scales, near, count, first, left, right, t, acc, low):
    n = 2 * REACH * LEAF
    return pl.pallas_call(
        lambda *refs: near_side_kernel(scales, *refs),
        out_shape=jax.ShapeDtypeStruct((COLS, LEAF_DEV * LEAF), jnp.float32),
        in_specs=[SMEM] * 3 + [ANY] * 5,
        out_specs=VMEM,
        scratch_shapes=[
            pltpu.VMEM((n, LANES), jnp.bfloat16),
            pltpu.VMEM((COLS, n), jnp.bfloat16),
            pltpu.VMEM((FEAT, n), jnp.bfloat16),
            pltpu.VMEM(t.shape, jnp.bfloat16),
            pltpu.VMEM(acc.shape, jnp.float32),
            pltpu.VMEM(low.shape, jnp.float32),
            pltpu.SMEM((LEAF_DEV * NEAR + 8,), jnp.int32),
            pltpu.SemaphoreType.DMA((7,)),
        ],
        compiler_params=params(),
        cost_estimate=cost(50),
        name="near_sides",
    )(near, count, first, left, right, t, acc, low)


def upper_kernel(scale, ratio, terms, hx, upper, total):
    here = terms[:COLS, :]
    for m in range(1, terms.shape[0] // COLS):
        here = here + terms[m * COLS : (m + 1) * COLS, :]
    step = pl.program_id(0)

    @pl.when(step == 0)
    def _():
        total[...] = here

    @pl.when(step > 0)
    def _():
        total[...] += here

    @pl.when(step == pl.num_programs(0) - 1)
    def _():
        upper[:COLS, :] = (total[...] * scale).astype(jnp.bfloat16) * jnp.bfloat16(ratio)
        upper[COLS:, :] = hx[...]


def upper_call(scale, ratio, terms, hx):
    steps = 2
    return pl.pallas_call(
        lambda *refs: upper_kernel(scale, ratio, *refs),
        out_shape=jax.ShapeDtypeStruct((COLS + FEAT, RANK), jnp.bfloat16),
        grid=(steps,),
        in_specs=[
            pl.BlockSpec((terms.shape[0] // steps, RANK), lambda i: (i, 0)),
            pl.BlockSpec(hx.shape, lambda i: (0, 0)),
        ],
        out_specs=pl.BlockSpec((COLS + FEAT, RANK), lambda i: (0, 0)),
        scratch_shapes=[pltpu.VMEM((COLS, RANK), jnp.float32)],
        compiler_params=params(),
        name="high_sum",
    )(terms, hx)


def high_kernel(scale, *refs):
    *ups, t, part, out = refs
    high_w = jnp.concatenate([u[:COLS, :] for u in ups], axis=1)
    high_x = event_rows(jnp.concatenate([u[COLS:, :] for u in ups], axis=1))
    many = out.shape[1] // LEAF
    ats = [slice(j * LEAF, (j + 1) * LEAF) for j in range(many)]
    ks = [jnp.exp(dot(high_x, t[at, :], NT)).astype(jnp.bfloat16) for at in ats]
    for at, k in zip(ats, ks):
        out[:, at] = (part[:, at] + dot(high_w, k) * scale).astype(jnp.bfloat16)


def high_call(scale, ups, t, part):
    many = 4
    return pl.pallas_call(
        lambda *refs: high_kernel(scale, *refs),
        out_shape=jax.ShapeDtypeStruct(part.shape, jnp.bfloat16),
        grid=(LEAF_DEV // many,),
        in_specs=[pl.BlockSpec(u.shape, lambda i: (0, 0)) for u in ups]
        + [
            pl.BlockSpec((many * LEAF, LANES), lambda i: (i, 0)),
            pl.BlockSpec((COLS, many * LEAF), lambda i: (0, i)),
        ],
        out_specs=pl.BlockSpec((COLS, many * LEAF), lambda i: (0, i)),
        compiler_params=params(),
        cost_estimate=cost(12),
        name="high_out",
    )(*ups, t, part)


def swap(x, axis, mask):
    count = lax.axis_size(axis)
    return lax.ppermute(x, axis, [(i, i ^ mask) for i in range(count)])


def after(x, *others):
    return lax.optimization_barrier((x, *others))[0]


def per_device(events, coeffs, tree_perm, near_list, near_count, far_list, skel_low, skel_high):
    group_devs = lax.axis_size("inner")
    group_count = lax.axis_size("outer")
    far_count = far_list.shape[1]
    ev_dev = events.shape[1]
    inner = lax.axis_index("inner").astype(jnp.int32)
    device = lax.axis_index("outer").astype(jnp.int32) * group_devs + inner
    devices = group_devs * group_count
    first = (device * LEAF_DEV).reshape(1)
    own = own_call(tree_perm, skel_low, events, coeffs)
    low_all = lax.all_gather(own, "inner", axis=0, tiled=True)
    lo, hi, wx_lo, wx_hi, t = tree_call(after(tree_perm, own), events, coeffs)
    both = ("outer", "inner")
    left = lax.ppermute(wx_hi, both, [(i, i + 1) for i in range(devices - 1)])
    right = lax.ppermute(wx_lo, both, [(i + 1, i) for i in range(devices - 1)])
    acc = near_own_call(near_list, near_count, first, lo, hi, wx_lo, wx_hi, t)

    low_all = after(low_all, acc)
    term, hx = term_call(skel_high, low_all, lo, hi, wx_lo, wx_hi)
    terms = lax.all_gather(term, "inner", axis=0, tiled=True)
    far = low_call(far_list, after(low_all, term), t)
    near_scale = 16.0 / (LEAF * NEAR) ** 0.5
    low_scale = 128.0 / (far_count * RANK) ** 0.5
    scales = (near_scale, low_scale)
    part = near_side_call(scales, near_list, near_count, first, left, right, t, acc, far)

    scale = 1.0 / (ev_dev * group_devs) ** 0.5
    upper = upper_call(scale, (far_count / group_count) ** 0.5, after(terms, part), hx)
    ups = [swap(upper, "outer", m) for m in range(1, group_count)]
    return high_call(low_scale, ups, t, part)


def solution(mesh):
    return jax.shard_map(
        per_device,
        mesh=mesh,
        in_specs=(
            P(None, ("outer", "inner")),
            P(None, ("outer", "inner")),
            P(("outer", "inner"), None),
            P(("outer", "inner"), None),
            P(("outer", "inner")),
            P(("outer", "inner"), None),
            P(("outer", "inner"), None),
            P("outer", None),
        ),
        out_specs=P(None, ("outer", "inner")),
        check_vma=False,
    )
```
